32 devices in a mesh: fsdp: 2 (over y), ctx: 8 (over z, core), tp: 2 (over x).
Axes of the slice: x: 2, y: 2, z: 4, core: 2. Of those that a mesh axis runs over, the one named last changes fastest.
Arguments:
- tokens: bfloat16 [2, 2048, 1280], P(None, ('fsdp', 'ctx')), may hold values from -6 to 6
- lengths: int32 [2, 2, 3], P('fsdp'), may hold values from 128 to 512, as said below
- attn_gain: bfloat16 [1280], P(('fsdp', 'ctx')), may hold values from 0.5 to 1.5
- w_query: bfloat16 [1280, 1280], P(('fsdp', 'ctx'), 'tp'), may hold values from -0.15625 to 0.15625
- w_key: bfloat16 [1280, 320], P(('fsdp', 'ctx')), may hold values from -0.15625 to 0.15625
- w_value: bfloat16 [1280, 320], P(('fsdp', 'ctx')), may hold values from -0.15625 to 0.15625
- w_out: bfloat16 [1280, 1280], P('tp', ('fsdp', 'ctx')), may hold values from -2.5 to 2.5
- ffn_gain: bfloat16 [1280], P(('fsdp', 'ctx')), may hold values from 0.5 to 1.5
- w_gate: bfloat16 [1280, 3584], P(('fsdp', 'ctx'), 'tp'), may hold values from -0.15625 to 0.15625
- w_up: bfloat16 [1280, 3584], P(('fsdp', 'ctx'), 'tp'), may hold values from -0.15625 to 0.15625
- w_down: bfloat16 [3584, 1280], P('tp', ('fsdp', 'ctx')), may hold values from -0.1875 to 0.1875
- cotangent: bfloat16 [2, 2048, 1280], P(None, ('fsdp', 'ctx')), may hold values from -6 to 6
Outputs:
- output: bfloat16 [2, 2048, 1280], P(None, ('fsdp', 'ctx'))
- input_grad: float32 [2, 2048, 1280], P(None, ('fsdp', 'ctx'))
- grad_attn_gain: float32 [1280], P(('fsdp', 'ctx'))
- grad_query: float32 [1280, 1280], P(('fsdp', 'ctx'), 'tp')
- grad_key: float32 [1280, 320], P(('fsdp', 'ctx', 'tp'))
- grad_value: float32 [1280, 320], P(('fsdp', 'ctx', 'tp'))
- grad_out: float32 [1280, 1280], P('tp', ('fsdp', 'ctx'))
- grad_ffn_gain: float32 [1280], P(('fsdp', 'ctx'))
- grad_gate: float32 [1280, 3584], P(('fsdp', 'ctx'), 'tp')
- grad_up: float32 [1280, 3584], P(('fsdp', 'ctx'), 'tp')
- grad_down: float32 [3584, 1280], P('tp', ('fsdp', 'ctx'))
The draws below stay inside these ranges and needn't reach their ends.
Inputs may be any that keep to these rules, and one draw needn't show every extreme that they name: Each row holds 3 document lengths; exactly one of them is 512, the others lie between 128 and 256; the rows of the micro-batch after the last document are padding.
All inputs are finite; a program needn't handle non-finite values.
Results may differ from the reference program's by a relative error of at most 0.019.
Values may be sent and summed in bfloat16 or wider, within the bound.
A program may use at most 192 MiB of HBM per device.

```python
import math
import jax
import jax.numpy as jnp
from jax import lax

D = 1280
H = 20
KV = 5
HD = 64
FF = 3584
MICRO = 2
DOCS = 3
MB = 1024
MAXLEN = 512
MINLEN = 128
ROWS = 2048
N_FSDP = 2


def draw_lengths(key, part):
    first_key, second_key = jax.random.split(key)
    others = jax.random.randint(first_key, (N_FSDP, MICRO, DOCS), MINLEN, MAXLEN // 2 + 1)
    longest_at = jax.random.randint(second_key, (N_FSDP, MICRO, 1), 0, DOCS)
    columns = jnp.arange(DOCS, dtype=jnp.int32)[None, None, :]
    return jnp.where(columns == longest_at, MAXLEN, others).astype(jnp.int32)


def block_levels(key, shape, shards, least, high):
    factor_of = 1.0
    for dim, parts in shards:
        heights = jax.random.uniform(jax.random.fold_in(jax.random.fold_in(key, 6), dim), (parts,), jnp.float32, least / len(shards), high / len(shards))
        factor_of = factor_of * jnp.repeat(jnp.exp(heights), shape[dim] // parts).reshape((-1,) + (1,) * (len(shape) - 1 - dim))
    return factor_of


def normal_values(key, shape, scale, reach, cuts=(), held_as=jnp.bfloat16):
    values = scale * jax.random.normal(key, shape, jnp.float32)
    if cuts:
        values = values * block_levels(key, shape, cuts, -0.22, 0.18)
    return jnp.clip(values, -reach, reach).astype(held_as)


def setup_inputs(seed: int = 0) -> dict:
    keys = jax.random.split(jax.random.key(seed), 13)
    return {
        "tokens": normal_values(keys[0], (MICRO, ROWS, D), 1.0, 6.0, ((1, 16),)),
        "lengths": draw_lengths(jax.random.fold_in(keys[12], 71), 0),
        "attn_gain": jnp.clip(1.0 + 0.1 * jax.random.normal(keys[2], (D,), jnp.float32), 0.5, 1.5).astype(jnp.bfloat16),
        "w_query": normal_values(keys[3], (D, H * HD), D ** -0.5, 0.15625, ((0, 16), (1, 2))),
        "w_key": normal_values(keys[4], (D, KV * HD), D ** -0.5, 0.15625, ((0, 16),)),
        "w_value": normal_values(keys[5], (D, KV * HD), D ** -0.5, 0.15625, ((0, 16),)),
        "w_out": normal_values(keys[6], (H * HD, D), (D // 256) ** -0.5, 2.5, ((0, 2), (1, 16))),
        "ffn_gain": jnp.clip(1.0 + 0.1 * jax.random.normal(keys[7], (D,), jnp.float32), 0.5, 1.5).astype(jnp.bfloat16),
        "w_gate": normal_values(keys[8], (D, FF), D ** -0.5, 0.15625, ((0, 16), (1, 2))),
        "w_up": normal_values(keys[9], (D, FF), D ** -0.5, 0.15625, ((0, 16), (1, 2))),
        "w_down": normal_values(keys[10], (FF, D), (FF // 4) ** -0.5, 0.1875, ((0, 2), (1, 16))),
        "cotangent": normal_values(keys[11], (MICRO, ROWS, D), 1.0, 6.0, ((1, 16),)),
    }


EPSILON = 1e-05
THETA = 10000.0
MASKED = -1e+30
HIGHEST = lax.Precision.HIGHEST

@jax.custom_vjp
def low(v):
    return lax.optimization_barrier(v.astype(jnp.bfloat16)).astype(jnp.float32)

@jax.custom_vjp
def low_back(v):
    return v

def low_keep(v):
    return (low(v), None)

def low_pass(kept, grad):
    return (grad,)

def back_keep(v):
    return (v, None)

def back_low(kept, grad):
    return (low(grad),)
low.defvjp(low_keep, low_pass)
low_back.defvjp(back_keep, back_low)

def layout(lengths_row, total_rows):
    ending = jnp.cumsum(lengths_row).astype(jnp.int32)
    opening = (ending - lengths_row).astype(jnp.int32)
    doc_count = lengths_row.shape[0]
    places = jnp.arange(total_rows, dtype=jnp.int32)
    segment = lax.optimization_barrier(jnp.sum((places[:, None] >= ending[None, :]).astype(jnp.int32), axis=1)).astype(jnp.int32)
    firsts = jnp.concatenate([opening, ending[-1:]]).astype(jnp.int32)
    labels = jnp.arange(doc_count + 1, dtype=jnp.int32)
    begins = lax.optimization_barrier(jnp.sum(jnp.where(segment[:, None] == labels[None, :], firsts[None, :], 0), axis=1)).astype(jnp.int32)
    return (segment, (places - begins).astype(jnp.int32), segment < doc_count)

def rotary(position):
    halves = HD // 2
    inverse = jnp.exp(jnp.arange(halves, dtype=jnp.float32) * (-2.0 * math.log(THETA) / HD))
    angles = position.astype(jnp.float32)[:, None] * inverse[None, :]
    cos_table = jnp.cos(angles)
    sin_table = jnp.sin(angles)
    return (jnp.concatenate([cos_table, cos_table], axis=1), jnp.concatenate([sin_table, sin_table], axis=1))

def turn(tensor, cos_table, sin_table):
    halves = tensor.shape[-1] // 2
    rotated = jnp.concatenate([-tensor[..., halves:], tensor[..., :halves]], axis=-1)
    return tensor * cos_table[:, None, :] + rotated * sin_table[:, None, :]

def normalize(values, gain_vec):
    factor = lax.rsqrt(lax.optimization_barrier(jnp.mean(values * values, axis=-1, keepdims=True)) + EPSILON)
    return values * factor * gain_vec

def attend(queries, keys_rot, values_in, segment):
    row_count = queries.shape[0]
    query_block = min(512, row_count)
    block_count = row_count // query_block
    scaling = 1.0 / math.sqrt(HD)
    places = jnp.arange(row_count, dtype=jnp.int32)
    keys_wide = jnp.repeat(keys_rot, H // KV, axis=1)
    values_wide = jnp.repeat(values_in, H // KV, axis=1)

    def one_block(block_data):
        query_rows, segment_rows, places_rows = block_data
        logits = low_back(jnp.einsum('qhd,khd->hqk', query_rows, keys_wide, precision=HIGHEST) * scaling)
        allowed = (segment_rows[:, None] == segment[None, :]) & (places[None, :] <= places_rows[:, None])
        logits = jnp.where(allowed[None], logits, MASKED)
        top_score = lax.optimization_barrier(jnp.max(logits, axis=-1, keepdims=True))
        expo = jnp.exp(logits - top_score)
        probs = low(expo / lax.optimization_barrier(jnp.sum(expo, axis=-1, keepdims=True)))
        return jnp.einsum('hqk,khd->qhd', probs, values_wide, precision=HIGHEST)
    blocked = (queries.reshape(block_count, query_block, H, HD), segment.reshape(block_count, query_block), places.reshape(block_count, query_block))
    result = lax.map(jax.checkpoint(one_block), blocked)
    return result.reshape(row_count, H * HD)

def forward(inputs, params, segment, cos_table, sin_table):
    attn_gain, w_query, w_key, w_value, w_out, ffn_gain, w_gate, w_up, w_down = params
    length = inputs.shape[0]
    normed = low(normalize(inputs, attn_gain))
    queries = low_back(jnp.dot(normed, w_query, precision=HIGHEST)).reshape(length, H, HD)
    keys_rot = low_back(jnp.dot(normed, w_key, precision=HIGHEST)).reshape(length, KV, HD)
    valued = low(low_back(jnp.dot(normed, w_value, precision=HIGHEST))).reshape(length, KV, HD)
    queries = low(turn(queries, cos_table, sin_table))
    keys_rot = low(turn(keys_rot, cos_table, sin_table))
    attended = low(low_back(attend(queries, keys_rot, valued, segment)))
    hidden = inputs + low_back(jnp.dot(attended, w_out, precision=HIGHEST))
    normed_two = low(normalize(hidden, ffn_gain))
    gate_pre = low_back(jnp.dot(normed_two, w_gate, precision=HIGHEST))
    upward = low_back(jnp.dot(normed_two, w_up, precision=HIGHEST))
    active = low(jax.nn.silu(gate_pre) * upward)
    return hidden + low_back(jnp.dot(active, w_down, precision=HIGHEST))

def reference(tokens, lengths, attn_gain, w_query, w_key, w_value, w_out, ffn_gain, w_gate, w_up, w_down, cotangent):
    weights = tuple((weight.astype(jnp.float32) for weight in (attn_gain, w_query, w_key, w_value, w_out, ffn_gain, w_gate, w_up, w_down)))
    item_count = N_FSDP * MICRO

    def split_rows(array):
        return array.reshape(MICRO, N_FSDP, MB, D).transpose(1, 0, 2, 3).reshape(item_count, MB, D)

    def join_rows(array):
        return array.reshape(N_FSDP, MICRO, MB, D).transpose(1, 0, 2, 3).reshape(MICRO, N_FSDP * MB, D)
    stacked = (split_rows(tokens), lengths.reshape(item_count, DOCS), split_rows(cotangent))
    initial = tuple((jnp.zeros(weight.shape, jnp.float32) for weight in weights))

    def stepper(carry, item_data):
        inputs, lengths_row, cot_rows = item_data
        segment, position, live = layout(lengths_row, MB)
        cos_table, sin_table = rotary(position)

        def run_layer(inputs_in, *params):
            return forward(inputs_in, params, segment, cos_table, sin_table)
        result, pullback = jax.vjp(run_layer, inputs.astype(jnp.float32), *weights)
        grads = pullback(cot_rows.astype(jnp.float32) * live[:, None].astype(jnp.float32))
        summed = tuple((prior + fresh for prior, fresh in zip(carry, grads[1:])))
        return (summed, (result.astype(jnp.bfloat16), grads[0]))
    totals, (results, input_grads) = lax.scan(stepper, initial, stacked)
    return (join_rows(results), join_rows(input_grads), totals[0], totals[1], totals[2], totals[3], totals[4], totals[5], totals[6], totals[7], totals[8])
```

```python
import functools
import math

import jax
import jax.numpy as jnp
from jax import lax
from jax.experimental import pallas as pl
from jax.experimental.pallas import tpu as pltpu
from jax.sharding import PartitionSpec as P

H = 20
KV = 5
HD = 64


EPSILON = 1e-05
THETA = 10000.0
MASKED = -1e30


def layout(lengths_row, total_rows):
    ending = jnp.cumsum(lengths_row)
    opening = ending - lengths_row
    doc_count = lengths_row.shape[0]
    places = jnp.arange(total_rows, dtype=jnp.int32)
    segment = jnp.sum((places[:, None] >= ending[None, :]).astype(jnp.int32), axis=1)
    firsts = jnp.concatenate([opening, ending[-1:]])
    labels = jnp.arange(doc_count + 1, dtype=jnp.int32)
    begins = jnp.sum(jnp.where(segment[:, None] == labels[None, :], firsts[None, :], 0), axis=1)
    return (segment, places - begins, segment < doc_count)


def rotary(position, head_size):
    halves = head_size // 2
    inverse = jnp.exp(jnp.arange(halves, dtype=jnp.float32) * (-2.0 * math.log(THETA) / head_size))
    angles = position.astype(jnp.float32)[:, None] * inverse[None, :]
    cos_table = jnp.cos(angles)
    sin_table = jnp.sin(angles)
    return (
        jnp.concatenate([cos_table, cos_table], axis=1),
        jnp.concatenate([sin_table, sin_table], axis=1),
    )


def turn(tensor, cos_table, sin_table):
    halves = tensor.shape[-1] // 2
    rotated = jnp.concatenate([-tensor[..., halves:], tensor[..., :halves]], axis=-1)
    return tensor * cos_table[:, None, :] + rotated * sin_table[:, None, :]


def turn_back(tensor, cos_table, sin_table):
    halves = tensor.shape[-1] // 2
    shifted = tensor * sin_table[:, None, :]
    rotated = jnp.concatenate([shifted[..., halves:], -shifted[..., :halves]], axis=-1)
    return tensor * cos_table[:, None, :] + rotated


def norm_back(values, factor, gain_vec, grad_in):
    scaled = gain_vec * grad_in
    return factor * scaled - values * factor**3 * jnp.mean(scaled * values, axis=-1, keepdims=True)


def collect(attn_gain, w_query, w_key, w_value, w_out, ffn_gain, w_gate, w_up, w_down):
    return (
        lax.all_gather(attn_gain, ("fsdp", "ctx"), axis=0, tiled=True),
        lax.all_gather(w_query, ("fsdp", "ctx"), axis=0, tiled=True),
        lax.all_gather(w_key, ("fsdp", "ctx"), axis=0, tiled=True),
        lax.all_gather(w_value, ("fsdp", "ctx"), axis=0, tiled=True),
        lax.all_gather(w_out, ("fsdp", "ctx"), axis=1, tiled=True),
        lax.all_gather(ffn_gain, ("fsdp", "ctx"), axis=0, tiled=True),
        lax.all_gather(w_gate, ("fsdp", "ctx"), axis=0, tiled=True),
        lax.all_gather(w_up, ("fsdp", "ctx"), axis=0, tiled=True),
        lax.all_gather(w_down, ("fsdp", "ctx"), axis=1, tiled=True),
    )


def collect_again(attn_gain, w_query, w_key, w_value, w_out, ffn_gain, w_gate, w_up, w_down):
    return (
        lax.all_gather(attn_gain, ("fsdp", "ctx"), axis=0, tiled=True),
        lax.all_gather(w_query, ("fsdp", "ctx"), axis=0, tiled=True),
        lax.all_gather(w_key, ("fsdp", "ctx"), axis=0, tiled=True),
        lax.all_gather(w_value, ("fsdp", "ctx"), axis=0, tiled=True),
        lax.all_gather(w_out, ("fsdp", "ctx"), axis=1, tiled=True),
        lax.all_gather(ffn_gain, ("fsdp", "ctx"), axis=0, tiled=True),
        lax.all_gather(w_gate, ("fsdp", "ctx"), axis=0, tiled=True),
        lax.all_gather(w_up, ("fsdp", "ctx"), axis=0, tiled=True),
        lax.all_gather(w_down, ("fsdp", "ctx"), axis=1, tiled=True),
    )


def reduce_grads(main_part, pair_part):
    shares = (
        lax.psum_scatter(main_part[0], ("fsdp", "ctx"), scatter_dimension=0, tiled=True),
        lax.psum_scatter(main_part[1], ("fsdp", "ctx"), scatter_dimension=0, tiled=True),
        lax.psum_scatter(main_part[2], ("fsdp", "ctx"), scatter_dimension=1, tiled=True),
        lax.psum_scatter(main_part[3], ("fsdp", "ctx"), scatter_dimension=0, tiled=True),
        lax.psum_scatter(main_part[4], ("fsdp", "ctx"), scatter_dimension=0, tiled=True),
        lax.psum_scatter(main_part[5], ("fsdp", "ctx"), scatter_dimension=0, tiled=True),
        lax.psum_scatter(main_part[6], ("fsdp", "ctx"), scatter_dimension=1, tiled=True),
    )
    pairs = (
        lax.psum_scatter(pair_part[0], ("fsdp", "ctx", "tp"), scatter_dimension=0, tiled=True),
        lax.psum_scatter(pair_part[1], ("fsdp", "ctx", "tp"), scatter_dimension=0, tiled=True),
    )
    return (shares, pairs)


def block_allowed(segment_rows, places_rows, segment_all, block_at, key_block):
    segment_keys = lax.dynamic_slice_in_dim(segment_all, block_at * key_block, key_block)
    place_keys = block_at * key_block + jnp.arange(key_block, dtype=jnp.int32)
    return (segment_rows[:, None] == segment_keys[None, :]) & (
        place_keys[None, :] <= places_rows[:, None]
    )


def sweep(visit, initial, block_count, useful):

    def advance(block_at, state):
        return lax.cond(
            useful(block_at),
            lambda current: visit(block_at, current),
            lambda current: current,
            state,
        )

    return lax.fori_loop(0, block_count, advance, initial)


def shards(
    tokens,
    lengths,
    attn_gain,
    w_query,
    w_key,
    w_value,
    w_out,
    ffn_gain,
    w_gate,
    w_up,
    w_down,
    cotangent,
):
    f32 = jnp.float32
    b16 = jnp.bfloat16
    micro_count = tokens.shape[0]
    tok_rows = tokens.shape[1]
    model_width = tokens.shape[2]
    ctx_count = lax.axis_size("ctx")
    tp_count = lax.axis_size("tp")
    ctx_at = lax.axis_index("ctx")
    tp_at = lax.axis_index("tp")
    total_rows = tok_rows * ctx_count
    half_rows = tok_rows // tp_count
    local_heads = w_query.shape[1] // HD
    kv_width = KV * HD
    scaling = 1.0 / math.sqrt(HD)
    key_block = min(512, total_rows)
    block_count = total_rows // key_block
    heads_global = tp_at * local_heads + jnp.arange(local_heads, dtype=jnp.int32)
    select = heads_global[:, None] // (H // KV) == jnp.arange(KV, dtype=jnp.int32)[None, :]
    select_low = select.astype(b16)
    select_high = select.astype(f32)
    row_offset = tp_at * half_rows
    start_row = ctx_at * tok_rows
    places_mine = start_row + jnp.arange(tok_rows, dtype=jnp.int32)
    outputs_list = []
    input_list = []
    main_total = None
    pair_total = None
    for micro_at in range(micro_count):
        gathered = collect(
            attn_gain, w_query, w_key, w_value, w_out, ffn_gain, w_gate, w_up, w_down
        )
        (
            gain_first,
            query_full,
            key_full,
            value_full,
            out_full,
            gain_second,
            gate_full,
            up_full,
            down_full,
        ) = gathered
        inputs = tokens[micro_at].astype(f32)
        segment_all, position_all, live_all = layout(lengths[0, micro_at], total_rows)
        segment_mine = lax.dynamic_slice_in_dim(segment_all, start_row, tok_rows)
        position_mine = lax.dynamic_slice_in_dim(position_all, start_row, tok_rows)
        live_mine = lax.dynamic_slice_in_dim(live_all, start_row, tok_rows)
        cos_table, sin_table = rotary(position_mine, HD)
        rms_first = lax.rsqrt(jnp.mean(inputs * inputs, axis=-1, keepdims=True) + EPSILON)
        normed_first = (inputs * rms_first * gain_first.astype(f32)).astype(b16)
        queries = jnp.dot(normed_first, query_full, preferred_element_type=f32).reshape(
            tok_rows, local_heads, HD
        )
        queries = turn(queries, cos_table, sin_table).astype(b16)
        key_lin = jnp.dot(normed_first, key_full, preferred_element_type=f32).reshape(
            tok_rows, KV, HD
        )
        key_rot = turn(key_lin, cos_table, sin_table).astype(b16).reshape(tok_rows, kv_width)
        value_rot = jnp.dot(normed_first, value_full, preferred_element_type=f32).astype(b16)
        keys_all, values_all = (
            lax.all_gather(key_rot, "ctx", axis=0, tiled=True),
            lax.all_gather(value_rot, "ctx", axis=0, tiled=True),
        )
        keys_local = jnp.einsum(
            "tjd,hj->thd",
            keys_all.reshape(total_rows, KV, HD),
            select_low,
            preferred_element_type=f32,
        ).astype(b16)
        values_local = jnp.einsum(
            "tjd,hj->thd",
            values_all.reshape(total_rows, KV, HD),
            select_low,
            preferred_element_type=f32,
        ).astype(b16)

        def useful(block_at):
            return jnp.any(
                block_allowed(segment_mine, places_mine, segment_all, block_at, key_block)
            )

        def logits_of(block_at):
            key_rows = lax.dynamic_slice_in_dim(keys_local, block_at * key_block, key_block)
            raw_scores = (
                jnp.einsum("qhd,khd->hqk", queries, key_rows, preferred_element_type=f32) * scaling
            )
            allowed = block_allowed(segment_mine, places_mine, segment_all, block_at, key_block)
            return jnp.where(allowed[None], raw_scores, MASKED)

        def statistic(block_at, state):
            top_score, mass_sum = state
            logits = logits_of(block_at)
            new_top = jnp.maximum(top_score, jnp.max(logits, axis=-1))
            mass_sum = mass_sum * jnp.exp(top_score - new_top) + jnp.sum(
                jnp.exp(logits - new_top[..., None]), axis=-1
            )
            return (new_top, mass_sum)

        start_state = (
            jnp.full((local_heads, tok_rows), MASKED, f32),
            jnp.zeros((local_heads, tok_rows), f32),
        )
        top_score, mass_sum = sweep(statistic, start_state, block_count, useful)

        def probable(block_at):
            return jnp.exp(logits_of(block_at) - top_score[..., None]) / mass_sum[..., None]

        def accumulate(block_at, running):
            probs_low = probable(block_at).astype(b16)
            value_rows = lax.dynamic_slice_in_dim(values_local, block_at * key_block, key_block)
            return running + jnp.einsum(
                "hqk,khd->qhd", probs_low, value_rows, preferred_element_type=f32
            )

        attended = sweep(
            accumulate, jnp.zeros((tok_rows, local_heads, HD), f32), block_count, useful
        )
        attended_low = attended.reshape(tok_rows, local_heads * HD).astype(b16)
        branch = lax.psum(
            jnp.dot(attended_low, out_full, preferred_element_type=f32).astype(jnp.bfloat16), "tp"
        ).astype(jnp.float32)
        hidden = inputs + branch
        rms_second = lax.rsqrt(jnp.mean(hidden * hidden, axis=-1, keepdims=True) + EPSILON)
        normed_second = (hidden * rms_second * gain_second.astype(f32)).astype(b16)
        gate_pre = jnp.dot(normed_second, gate_full, preferred_element_type=f32)
        upward = jnp.dot(normed_second, up_full, preferred_element_type=f32)
        sigmoid_gate = jax.nn.sigmoid(gate_pre)
        silu_gate = jax.nn.silu(gate_pre)
        active = (silu_gate * upward).astype(b16)
        mixed = lax.psum(
            jnp.dot(active, down_full, preferred_element_type=f32).astype(jnp.bfloat16), "tp"
        ).astype(jnp.float32)
        outputs_list.append((hidden + mixed).astype(b16))
        gathered = collect_again(
            attn_gain, w_query, w_key, w_value, w_out, ffn_gain, w_gate, w_up, w_down
        )
        (
            gain_first,
            query_full,
            key_full,
            value_full,
            out_full,
            gain_second,
            gate_full,
            up_full,
            down_full,
        ) = gathered
        grad_rows = cotangent[micro_at].astype(f32) * live_mine[:, None].astype(f32)
        grad_low = grad_rows.astype(b16)
        grad_down = jnp.einsum("tf,td->fd", active, grad_low, preferred_element_type=f32)
        grad_active = jnp.einsum("td,fd->tf", grad_low, down_full, preferred_element_type=f32)
        grad_gate_pre = (
            grad_active * upward * sigmoid_gate * (1.0 + gate_pre * (1.0 - sigmoid_gate))
        ).astype(b16)
        grad_upward = (grad_active * silu_gate).astype(b16)
        grad_gate = jnp.einsum(
            "te,tf->ef", normed_second, grad_gate_pre, preferred_element_type=f32
        )
        grad_up = jnp.einsum("te,tf->ef", normed_second, grad_upward, preferred_element_type=f32)
        grad_normed_second = jnp.einsum(
            "tf,ef->te", grad_gate_pre, gate_full, preferred_element_type=f32
        ) + jnp.einsum("tf,ef->te", grad_upward, up_full, preferred_element_type=f32)
        grad_normed_second = lax.psum(grad_normed_second.astype(jnp.bfloat16), "tp").astype(
            jnp.float32
        )
        grad_gain_second = jnp.sum(grad_normed_second * hidden * rms_second, axis=0)
        grad_hidden = grad_rows + norm_back(
            hidden, rms_second, gain_second.astype(f32), grad_normed_second
        )
        grad_branch = grad_hidden.astype(b16)
        grad_out = jnp.einsum("te,td->ed", attended_low, grad_branch, preferred_element_type=f32)
        grad_att = (
            jnp.einsum("td,ed->te", grad_branch, out_full, preferred_element_type=f32)
            .astype(b16)
            .reshape(tok_rows, local_heads, HD)
        )
        delta_rows = jnp.sum(grad_att.astype(f32) * attended, axis=-1).T

        def backward_visit(block_at, state):
            grad_queries, grad_keys, grad_values = state
            first_row = block_at * key_block
            key_rows = lax.dynamic_slice_in_dim(keys_local, first_row, key_block)
            value_rows = lax.dynamic_slice_in_dim(values_local, first_row, key_block)
            probs = probable(block_at)
            probs_low = probs.astype(b16)
            grad_probs = jnp.einsum(
                "qhd,khd->hqk", grad_att, value_rows, preferred_element_type=f32
            )
            grad_logits = (probs * (grad_probs - delta_rows[..., None])).astype(b16)
            grad_queries = (
                grad_queries
                + jnp.einsum("hqk,khd->qhd", grad_logits, key_rows, preferred_element_type=f32)
                * scaling
            )
            key_part = (
                jnp.einsum("hqk,qhd->khd", grad_logits, queries, preferred_element_type=f32)
                * scaling
            )
            value_part = jnp.einsum("hqk,qhd->khd", probs_low, grad_att, preferred_element_type=f32)
            grad_keys = lax.dynamic_update_slice_in_dim(grad_keys, key_part, first_row, 0)
            grad_values = lax.dynamic_update_slice_in_dim(grad_values, value_part, first_row, 0)
            return (grad_queries, grad_keys, grad_values)

        back_state = (
            jnp.zeros((tok_rows, local_heads, HD), f32),
            jnp.zeros((total_rows, local_heads, HD), f32),
            jnp.zeros((total_rows, local_heads, HD), f32),
        )
        grad_queries, grad_keys, grad_values = sweep(
            backward_visit, back_state, block_count, useful
        )
        key_heads = jnp.einsum(
            "thd,hj->tjd", grad_keys, select_high, precision=lax.Precision.HIGHEST
        ).reshape(total_rows, kv_width)
        value_heads = jnp.einsum(
            "thd,hj->tjd", grad_values, select_high, precision=lax.Precision.HIGHEST
        ).reshape(total_rows, kv_width)
        key_sum, value_sum = (
            lax.psum_scatter(
                key_heads.astype(jnp.bfloat16), ("ctx", "tp"), scatter_dimension=0, tiled=True
            ).astype(jnp.float32),
            lax.psum_scatter(
                value_heads.astype(jnp.bfloat16), ("ctx", "tp"), scatter_dimension=0, tiled=True
            ).astype(jnp.float32),
        )
        cos_half = lax.dynamic_slice_in_dim(cos_table, row_offset, half_rows)
        sin_half = lax.dynamic_slice_in_dim(sin_table, row_offset, half_rows)
        grad_key_lin = (
            turn_back(key_sum.reshape(half_rows, KV, HD), cos_half, sin_half)
            .astype(b16)
            .reshape(half_rows, kv_width)
        )
        grad_value_lin = value_sum.astype(b16)
        normed_half = lax.dynamic_slice_in_dim(normed_first, row_offset, half_rows)
        grad_key = jnp.einsum("te,tk->ek", normed_half, grad_key_lin, preferred_element_type=f32)
        grad_value = jnp.einsum(
            "te,tk->ek", normed_half, grad_value_lin, preferred_element_type=f32
        )
        grad_normed_pair = jnp.einsum(
            "tk,ek->te", grad_key_lin, key_full, preferred_element_type=f32
        ) + jnp.einsum("tk,ek->te", grad_value_lin, value_full, preferred_element_type=f32)
        grad_query_lin = (
            turn_back(grad_queries, cos_table, sin_table)
            .astype(b16)
            .reshape(tok_rows, local_heads * HD)
        )
        grad_query = jnp.einsum(
            "te,tq->eq", normed_first, grad_query_lin, preferred_element_type=f32
        )
        grad_normed_first = jnp.einsum(
            "tq,eq->te", grad_query_lin, query_full, preferred_element_type=f32
        )
        grad_normed_first = grad_normed_first + lax.dynamic_update_slice_in_dim(
            jnp.zeros((tok_rows, model_width), f32), grad_normed_pair, row_offset, 0
        )
        grad_normed_first = lax.psum(grad_normed_first.astype(jnp.bfloat16), "tp").astype(
            jnp.float32
        )
        grad_gain_first = jnp.sum(grad_normed_first * inputs * rms_first, axis=0)
        input_list.append(
            grad_hidden + norm_back(inputs, rms_first, gain_first.astype(f32), grad_normed_first)
        )
        main_part = (
            grad_gain_first,
            grad_query,
            grad_out,
            grad_gain_second,
            grad_gate,
            grad_up,
            grad_down,
        )
        pair_part = (grad_key, grad_value)
        main_part, pair_part = reduce_grads(main_part, pair_part)
        if main_total is None:
            main_total = main_part
            pair_total = pair_part
        else:
            main_total = jax.tree.map(jnp.add, main_total, main_part)
            pair_total = jax.tree.map(jnp.add, pair_total, pair_part)
    return (
        jnp.stack(outputs_list),
        jnp.stack(input_list),
        main_total[0],
        main_total[1],
        pair_total[0],
        pair_total[1],
        main_total[2],
        main_total[3],
        main_total[4],
        main_total[5],
        main_total[6],
    )


F32 = jnp.float32
B16 = jnp.bfloat16
HD = 64
EPSILON = 1e-05
THETA = 10000.0
MASKED = -1e30
SCALE = 1.0 / math.sqrt(HD)
VMEM = pltpu.VMEM

def nn(a, b): return lax.dot_general(a, b, (((1,), (0,)), ((), ())), preferred_element_type=F32)
def nt(a, b): return lax.dot_general(a, b, (((1,), (1,)), ((), ())), preferred_element_type=F32)
def tn(a, b): return lax.dot_general(a, b, (((0,), (0,)), ((), ())), preferred_element_type=F32)

def lanes(shape): return lax.broadcasted_iota(jnp.int32, shape, len(shape) - 1)

def rope(t, cos, sin):
    low = lanes(t.shape) % 64 < 32
    rot = jnp.where(low, -pltpu.roll(t, 96, 1), pltpu.roll(t, 32, 1))
    return t * cos + rot * sin

def rope_back(u, cos, sin):
    low = lanes(u.shape) % 64 < 32
    us = u * sin
    return u * cos + jnp.where(low, pltpu.roll(us, 96, 1), -pltpu.roll(us, 32, 1))

def rms(v): return lax.rsqrt(jnp.mean(v * v, axis=-1, keepdims=True) + EPSILON)

def norm_back(v, r, gain, d):
    s = gain * d
    return r * s - v * (r * r * r) * jnp.mean(s * v, axis=-1, keepdims=True)

def project(x_ref, gain_ref, a_ref, cos_ref, sin_ref, n1_ref, q_ref, kv_ref):
    x = x_ref[...].astype(F32)
    n1 = (x * rms(x) * gain_ref[...]).astype(B16)
    n1_ref[...] = n1
    lin = nn(n1, a_ref[...])
    qw = q_ref.shape[1]
    cos, sin = cos_ref[...], sin_ref[...]
    for i in range(lin.shape[1] // 128):
        tile = lin[:, 128 * i:128 * (i + 1)]
        j = i - qw // 128
        if j <= 0:
            tile = rope(tile, cos, sin)
        elif j == 1:
            tile = jnp.where(lanes(tile.shape) < 64, rope(tile, cos, sin), tile)
        if j < 0: q_ref[:, 128 * i:128 * (i + 1)] = tile.astype(B16)
        else: kv_ref[:, 128 * j:128 * (j + 1)] = tile.astype(B16)

def doubled(tile, which):
    t = tile.astype(F32)
    r = pltpu.roll(t, 64, 1)
    low = lanes(t.shape) < 64
    return (jnp.where(low, t, r) if which == 0 else jnp.where(low, r, t)).astype(B16)

def window_start(t, nblk): return jnp.maximum(t - nblk + 1, 0)

def window(kvall_ref, w0, nblk, m, rows, tile):
    return jnp.concatenate([kvall_ref[w0 + b, m * rows:(m + 1) * rows, 128 * tile:128 * (tile + 1)] for b in range(nblk)], axis=0)

def heads_kv(kvall_ref, w0, nblk, m, rows):
    k01 = window(kvall_ref, w0, nblk, m, rows, 0)
    k2v2 = window(kvall_ref, w0, nblk, m, rows, 1)
    v01 = window(kvall_ref, w0, nblk, m, rows, 2)
    ks = [doubled(k01, 0), doubled(k01, 1), doubled(k2v2, 0)]
    vs = [doubled(v01, 0), doubled(v01, 1), doubled(k2v2, 1)]
    return ks, vs

def pick(group, p, tp):
    a, b = p // 2, (p + 1) // 2
    return group[a] if a == b else jnp.where(tp == 0, group[a], group[b])

def stacked(head):
    low = lanes(head.shape) < 64
    zero = jnp.zeros_like(head)
    return jnp.concatenate([jnp.where(low, head, zero), jnp.where(low, zero, head)], axis=0)

def allowed_of(begin, row0, key0, rows, keys):
    i = row0 + lax.broadcasted_iota(jnp.int32, (rows, keys), 0)
    j = key0 + lax.broadcasted_iota(jnp.int32, (rows, keys), 1)
    return (j <= i) & (j >= begin)

def attention(micros, rows, nblk, q_ref, kvall_ref, begin_ref, wo_ref, ao_ref, pr_ref, part_ref):
    t = lax.axis_index("ctx"); tp = lax.axis_index("tp")
    w0 = window_start(t, nblk)
    keys = nblk * rows
    pairs = q_ref.shape[1] // 128
    for m in range(micros):
        sl = slice(m * rows, (m + 1) * rows)
        ks, vs = heads_kv(kvall_ref, w0, nblk, m, rows)
        ok = allowed_of(begin_ref[sl, :1], t * rows, w0 * rows, rows, keys)
        for p in range(pairs):
            kb = stacked(pick(ks, p, tp)); vb = stacked(pick(vs, p, tp))
            s = nt(q_ref[sl, 128 * p:128 * (p + 1)], kb) * SCALE
            halves = []
            for h in range(2):
                sh = jnp.where(ok, s[:, h * keys:(h + 1) * keys], MASKED)
                e = jnp.exp(sh - jnp.max(sh, axis=-1, keepdims=True))
                halves.append((e / jnp.sum(e, axis=-1, keepdims=True)).astype(B16))
            pr = jnp.concatenate(halves, axis=1)
            pr_ref[m * pairs + p] = pr
            ao_ref[sl, 128 * p:128 * (p + 1)] = nn(pr, vb).astype(B16)
    part_ref[...] = nt(ao_ref[...], wo_ref[...]).astype(B16)

def feed(x_ref, p1_ref, r1_ref, gain_ref, wg_ref, wu_ref, wd_ref, hid_ref, n2_ref, gate_ref, up_ref, act_ref, part_ref):
    hid = x_ref[...].astype(F32) + (p1_ref[...].astype(F32) + r1_ref[...].astype(F32))
    hid_ref[...] = hid
    n2 = (hid * rms(hid) * gain_ref[...]).astype(B16)
    n2_ref[...] = n2
    gate = nn(n2, wg_ref[...]); up = nn(n2, wu_ref[...])
    gate_ref[...] = gate; up_ref[...] = up
    act = (gate * jax.nn.sigmoid(gate) * up).astype(B16)
    act_ref[...] = act
    part_ref[...] = nt(act, wd_ref[...]).astype(B16)

def feed_back(ct_ref, live_ref, gate_ref, up_ref, act_ref, n2_ref, wg_ref, wu_ref, wd_ref, g_ref, dpart_ref, gg_ref, gu_ref, gd_ref):
    g = (ct_ref[...].astype(F32) * live_ref[:, :1]).astype(B16)
    g_ref[...] = g
    da = nn(g, wd_ref[...])
    gate = gate_ref[...]; up = up_ref[...]
    sg = jax.nn.sigmoid(gate)
    dgate = (da * up * sg * (1.0 + gate * (1.0 - sg))).astype(B16)
    dup = (da * (gate * sg)).astype(B16)
    dpart_ref[...] = (nt(dgate, wg_ref[...]) + nt(dup, wu_ref[...])).astype(B16)
    gd_ref[...] = tn(g, act_ref[...]).astype(B16)
    gg_ref[...] = tn(n2_ref[...], dgate).astype(B16)
    gu_ref[...] = tn(n2_ref[...], dup).astype(B16)

def attention_back(micros, rows, nblk, g_ref, p_ref, r_ref, hid_ref, gain_ref, q_ref, kvall_ref, wo_ref, ao_ref, pr_ref,
                   dh_ref, go_ref, gain_out_ref, dq_ref, dkv_ref, do_ref):
    t = lax.axis_index("ctx"); tp = lax.axis_index("tp")
    w0 = window_start(t, nblk)
    keys = nblk * rows
    pairs = q_ref.shape[1] // 128
    dn2 = p_ref[...].astype(F32) + r_ref[...].astype(F32)
    hid = hid_ref[...]
    r2 = rms(hid)
    gain_out_ref[...] = jnp.broadcast_to(jnp.sum(dn2 * hid * r2, axis=0, keepdims=True), gain_out_ref.shape)
    dh = g_ref[...].astype(F32) + norm_back(hid, r2, gain_ref[...], dn2)
    dh_ref[...] = dh
    db = dh.astype(B16)
    go_ref[...] = tn(db, ao_ref[...]).astype(B16)
    do_ref[...] = nn(db, wo_ref[...]).astype(B16)
    dkv_ref[...] = jnp.zeros_like(dkv_ref)
    for m in range(micros):
        sl = slice(m * rows, (m + 1) * rows)
        ks, vs = heads_kv(kvall_ref, w0, nblk, m, rows)
        dks = [jnp.zeros((keys, 128), F32) for _ in range(3)]
        dvs = [jnp.zeros((keys, 128), F32) for _ in range(3)]
        for p in range(pairs):
            kb = stacked(pick(ks, p, tp)); vb = stacked(pick(vs, p, tp))
            qt = q_ref[sl, 128 * p:128 * (p + 1)]
            dot_ = do_ref[sl, 128 * p:128 * (p + 1)]
            pr = pr_ref[m * pairs + p]
            dp = nt(dot_, vb)
            halves = []
            for h in range(2):
                ph = pr[:, h * keys:(h + 1) * keys].astype(F32)
                dph = dp[:, h * keys:(h + 1) * keys]
                delta = jnp.sum(ph * dph, axis=-1, keepdims=True)
                halves.append((ph * (dph - delta)).astype(B16))
            ds = jnp.concatenate(halves, axis=1)
            dq_ref[sl, 128 * p:128 * (p + 1)] = nn(ds, kb) * SCALE
            dkb = tn(ds, qt) * SCALE
            dvb = tn(pr, dot_)
            low = lanes((keys, 128)) < 64
            dk = jnp.where(low, dkb[:keys], dkb[keys:])
            dv = jnp.where(low, dvb[:keys], dvb[keys:])
            a, b = p // 2, (p + 1) // 2
            if a == b:
                dks[a] = dks[a] + dk; dvs[a] = dvs[a] + dv
            else:
                first = (tp == 0).astype(F32); second = 1.0 - first
                dks[a] = dks[a] + dk * first; dvs[a] = dvs[a] + dv * first
                dks[b] = dks[b] + dk * second; dvs[b] = dvs[b] + dv * second
        low = lanes((keys, 128)) < 64
        def full(v): return v + pltpu.roll(v, 64, 1)
        dk0, dk1, dk2 = [full(v) for v in dks]
        dv0, dv1, dv2 = [full(v) for v in dvs]
        tiles = [jnp.where(low, dk0, dk1), jnp.where(low, dk2, dv2), jnp.where(low, dv0, dv1)]
        for b in range(nblk):
            for i in range(3):
                dkv_ref[w0 + b, m * rows:(m + 1) * rows, 128 * i:128 * (i + 1)] = tiles[i][b * rows:(b + 1) * rows].astype(B16)

def project_back(dq_ref, dkv_ref, cos_ref, sin_ref, n1_ref, a_ref, ga_ref, part_ref, dl_ref):
    cos, sin = cos_ref[...], sin_ref[...]
    qt = dq_ref.shape[1] // 128
    for i in range(dl_ref.shape[1] // 128):
        j = i - qt
        tile = dq_ref[:, 128 * i:128 * (i + 1)] if j < 0 else dkv_ref[:, 128 * j:128 * (j + 1)].astype(F32)
        if j <= 0: tile = rope_back(tile, cos, sin)
        elif j == 1: tile = jnp.where(lanes(tile.shape) < 64, rope_back(tile, cos, sin), tile)
        dl_ref[:, 128 * i:128 * (i + 1)] = tile.astype(B16)
    dl = dl_ref[...]
    part_ref[...] = nt(dl, a_ref[...]).astype(B16)
    ga_ref[...] = tn(n1_ref[...], dl).astype(B16)

def input_back(x_ref, p_ref, r_ref, dh_ref, gain_ref, dx_ref, gain_out_ref):
    x = x_ref[...].astype(F32)
    r1 = rms(x)
    dn1 = p_ref[...].astype(F32) + r_ref[...].astype(F32)
    gain_out_ref[...] = jnp.broadcast_to(jnp.sum(dn1 * x * r1, axis=0, keepdims=True), gain_out_ref.shape)
    dx_ref[...] = dh_ref[...] + norm_back(x, r1, gain_ref[...], dn1)

MESHT = pl.DeviceIdType.MESH

def ag_body(nf, nz, chunks, n_mat, *refs):
    shards = refs[:n_mat]; outs = refs[n_mat:2*n_mat]
    send_sem, recv_sem, loc_sem = refs[2*n_mat:]
    y = lax.axis_index("fsdp") if nf > 1 else 0
    t = lax.axis_index("ctx")
    z = t // 2; c = lax.rem(t, 2)
    nc = 2 * nz
    barrier = pltpu.get_barrier_semaphore()
    def sig(**dev):
        pl.semaphore_signal(barrier, inc=1, device_id=dev, device_id_type=MESHT)
    @pl.when(z > 0)
    def _(): sig(ctx=t - 2)
    @pl.when(z < nz - 1)
    def _(): sig(ctx=t + 2)
    sig(ctx=t + 1 - 2 * c)
    for p in range(1, nf): sig(fsdp=lax.rem(y + p, nf))
    @pl.when((z > 0) & (z < nz - 1))
    def _(): pl.semaphore_wait(barrier, 2 + nf)
    @pl.when((z == 0) | (z == nz - 1))
    def _(): pl.semaphore_wait(barrier, 1 + nf)

    def shard(yy, zz, cc): return yy * nc + zz * 2 + cc
    def at(k, s):
        m, c0, cn = chunks[k]
        return outs[m].at[s, :, pl.ds(c0, cn)]
    def send(k, s, slot, dev, src=None):
        pltpu.make_async_remote_copy(src_ref=at(k, s) if src is None else src, dst_ref=at(k, s),
            send_sem=send_sem.at[k, slot], recv_sem=recv_sem.at[k, s], device_id=dev, device_id_type=MESHT).start()
    def rcopy(k, s, slot):
        return pltpu.make_async_remote_copy(src_ref=at(k, s), dst_ref=at(k, s),
            send_sem=send_sem.at[k, slot], recv_sem=recv_sem.at[k, s], device_id=dict(ctx=t + 1 - 2 * c), device_id_type=MESHT)
    nslots = [0]
    def new(n=1):
        v = nslots[0]; nslots[0] += n; return v
    S_ownL, S_ownR, S_ownC = new(), new(), new()
    S_ownY = new(nf - 1)
    S_z = {}
    for d in range(1, nz):
        for side in (0, 1):
            S_z[(side, d)] = (new(), new(), new(nf - 1))
    S_yc = {(p, zz): new() for p in range(1, nf) for zz in range(nz)}
    me = shard(y, z, c)
    sib = dict(ctx=t + 1 - 2 * c)
    def ydev(p): return dict(fsdp=lax.rem(y + p, nf))
    K = len(chunks)
    own_local = []
    for k in range(K):
        m, c0, cn = chunks[k]
        src = shards[m].at[:, pl.ds(c0, cn)]
        for p in range(1, nf): send(k, me, S_ownY + p - 1, ydev(p), src)
        @pl.when(z > 0)
        def _(): send(k, me, S_ownL, dict(ctx=t - 2), src)
        @pl.when(z < nz - 1)
        def _(): send(k, me, S_ownR, dict(ctx=t + 2), src)
        send(k, me, S_ownC, sib, src)
    for m in range(n_mat):
        pltpu.make_async_copy(shards[m], outs[m].at[me], loc_sem.at[m]).start()
    for k in range(K):
        for d in range(1, nz):
            for side in (0, 1):
                ok = (z >= d) if side == 0 else (z + d <= nz - 1)
                more = (z < nz - 1) if side == 0 else (z > 0)
                zz = z - d if side == 0 else z + d
                s = shard(y, zz, c)
                sf, sc, sy = S_z[(side, d)]
                @pl.when(ok)
                def _():
                    rcopy(k, s, 0).wait_recv()
                    @pl.when(more)
                    def _(): send(k, s, sf, dict(ctx=t + 2 if side == 0 else t - 2))
                    for p in range(1, nf): send(k, s, sy + p - 1, ydev(p))
                    send(k, s, sc, sib)
        for p in range(1, nf):
            yy = lax.rem(y + nf - p, nf)
            for zz in range(nz):
                s = shard(yy, zz, c)
                rcopy(k, s, 0).wait_recv()
                send(k, s, S_yc[(p, zz)], sib)
    for k in range(K):
        for yy in range(nf):
            for zz in range(nz):
                rcopy(k, shard(yy, zz, 1 - c), 0).wait_recv()
        for p in range(1, nf): rcopy(k, me, S_ownY + p - 1).wait_send()
        @pl.when(z > 0)
        def _(): rcopy(k, me, S_ownL).wait_send()
        @pl.when(z < nz - 1)
        def _(): rcopy(k, me, S_ownR).wait_send()
        rcopy(k, me, S_ownC).wait_send()
        for d in range(1, nz):
            for side in (0, 1):
                ok = (z >= d) if side == 0 else (z + d <= nz - 1)
                more = (z < nz - 1) if side == 0 else (z > 0)
                sf, sc, sy = S_z[(side, d)]
                @pl.when(ok)
                def _():
                    @pl.when(more)
                    def _(): rcopy(k, me, sf).wait_send()
                    for p in range(1, nf): rcopy(k, me, sy + p - 1).wait_send()
                    rcopy(k, me, sc).wait_send()
        for p in range(1, nf):
            for zz in range(nz):
                rcopy(k, me, S_yc[(p, zz)]).wait_send()
    for m in range(n_mat):
        pltpu.make_async_copy(shards[m], outs[m].at[me], loc_sem.at[m]).wait()

def n_slots(nf, nz):
    return 3 + (nf - 1) + 2 * (nz - 1) * (2 + nf - 1) + (nf - 1) * nz

def all_gather_weights(nf, nz, shards, chunks, cid=0, space=pl.ANY, name="weights_gather"):
    ns = nf * nz * 2
    n = len(shards)
    return pl.pallas_call(
        functools.partial(ag_body, nf, nz, chunks, n),
        out_shape=[jax.ShapeDtypeStruct((ns,) + s.shape, s.dtype) for s in shards],
        in_specs=[pl.BlockSpec(memory_space=pltpu.VMEM)] * n,
        out_specs=[pl.BlockSpec(memory_space=space)] * n,
        scratch_shapes=[pltpu.SemaphoreType.DMA((len(chunks), n_slots(nf, nz))), pltpu.SemaphoreType.DMA((len(chunks), ns)), pltpu.SemaphoreType.DMA((n,))],
        compiler_params=pltpu.CompilerParams(collective_id=cid, has_side_effects=True, vmem_limit_bytes=60 << 20),
        name=name,
    )(*shards)

MESHT = pl.DeviceIdType.MESH

def rs_body(nf, nz, chunks, n_mat, *refs):
    nb = nf * nz
    ins = refs[:n_mat]; outs = refs[n_mat:2*n_mat]
    own = refs[2*n_mat:3*n_mat]; crecv = refs[3*n_mat:4*n_mat]; zrecv = refs[4*n_mat:5*n_mat]
    rest = refs[5*n_mat:]
    if nf > 1:
        yrecv = rest[:n_mat]; rest = rest[n_mat:]
    lsem, cs, cr, ys, yr, zs, zr = rest
    y = lax.axis_index("fsdp") if nf > 1 else 0
    t = lax.axis_index("ctx")
    z = t // 2; c = lax.rem(t, 2)
    sib = dict(ctx=t + 1 - 2 * c)
    barrier = pltpu.get_barrier_semaphore()
    pl.semaphore_signal(barrier, inc=1, device_id=sib, device_id_type=MESHT)
    for p in range(1, nf):
        pl.semaphore_signal(barrier, inc=1, device_id=dict(fsdp=lax.rem(y + p, nf)), device_id_type=MESHT)
    def zdev(p): return lax.rem(z + p, nz)
    for p in range(1, nz):
        pl.semaphore_signal(barrier, inc=1, device_id=dict(ctx=zdev(p) * 2 + c), device_id_type=MESHT)
    pl.semaphore_wait(barrier, nf + nz - 1)
    def remote(src, dst, ss, rs, dev):
        return pltpu.make_async_remote_copy(src_ref=src, dst_ref=dst, send_sem=ss, recv_sem=rs, device_id=dev, device_id_type=MESHT)
    def ccopy(k):
        m, c0, cn = chunks[k]
        return remote(ins[m].at[:, 1 - c, :, pl.ds(c0, cn)], crecv[m].at[:, :, pl.ds(c0, cn)], cs.at[k], cr.at[k], sib)
    def lcopy(k):
        m, c0, cn = chunks[k]
        return pltpu.make_async_copy(ins[m].at[:, c, :, pl.ds(c0, cn)], own[m].at[:, :, pl.ds(c0, cn)], lsem.at[k])
    def ycopy(k, p):
        m, c0, cn = chunks[k]
        yy = lax.rem(y + p, nf)
        return remote(own[m].at[pl.ds(yy * nz, nz), :, pl.ds(c0, cn)], yrecv[m].at[p - 1, :, :, pl.ds(c0, cn)], ys.at[k, p - 1], yr.at[k, p - 1], dict(fsdp=yy))
    def zcopy(k, p):
        m, c0, cn = chunks[k]
        return remote(own[m].at[y * nz + zdev(p), :, pl.ds(c0, cn)], zrecv[m].at[p - 1, :, pl.ds(c0, cn)], zs.at[k, p - 1], zr.at[k, p - 1], dict(ctx=zdev(p) * 2 + c))
    K = len(chunks)
    for k in range(K):
        ccopy(k).start()
        lcopy(k).start()
    def stage_core(k):
        m, c0, cn = chunks[k]
        lcopy(k).wait()
        ccopy(k).wait_recv()
        def add(b, _):
            own[m][b, :, pl.ds(c0, cn)] = own[m][b, :, pl.ds(c0, cn)] + crecv[m][b, :, pl.ds(c0, cn)]
            return _
        lax.fori_loop(0, nb, add, 0)
        for p in range(1, nf): ycopy(k, p).start()
    def stage_y(k):
        m, c0, cn = chunks[k]
        for p in range(1, nf): ycopy(k, p).wait_recv()
        if nf > 1:
            def add(b, _):
                acc = own[m][y * nz + b, :, pl.ds(c0, cn)].astype(jnp.float32)
                for p in range(1, nf):
                    acc = acc + yrecv[m][p - 1, b, :, pl.ds(c0, cn)].astype(jnp.float32)
                own[m][y * nz + b, :, pl.ds(c0, cn)] = acc.astype(jnp.bfloat16)
                return _
            lax.fori_loop(0, nz, add, 0)
        for p in range(1, nz): zcopy(k, p).start()
    def stage_z(k):
        m, c0, cn = chunks[k]
        for p in range(1, nz): zcopy(k, p).wait_recv()
        acc = own[m][y * nz + z, :, pl.ds(c0, cn)].astype(jnp.float32)
        for p in range(1, nz):
            acc = acc + zrecv[m][p - 1, :, pl.ds(c0, cn)].astype(jnp.float32)
        outs[m][:, pl.ds(c0, cn)] = acc.astype(outs[m].dtype)
    for s in range(K + 2):
        if s < K: stage_core(s)
        if 0 <= s - 1 < K: stage_y(s - 1)
        if 0 <= s - 2 < K: stage_z(s - 2)
    for k in range(K):
        ccopy(k).wait_send()
        for p in range(1, nf): ycopy(k, p).wait_send()
        for p in range(1, nz): zcopy(k, p).wait_send()

def reduce_scatter_blocks(nf, nz, mats, chunks, cid, out_dtype=jnp.float32, name="grads_scatter"):
    n = len(mats); nb = nf * nz; K = len(chunks)
    b16 = jnp.bfloat16
    sh = [(m.shape[2], m.shape[3]) for m in mats]
    scratch = [pltpu.VMEM((nb,) + s, b16) for s in sh] + [pltpu.VMEM((nb,) + s, b16) for s in sh] + [pltpu.VMEM((nz - 1,) + s, b16) for s in sh]
    if nf > 1: scratch += [pltpu.VMEM((nf - 1, nz) + s, b16) for s in sh]
    D = pltpu.SemaphoreType.DMA
    scratch += [D((K,)), D((K,)), D((K,)), D((K, max(1, nf - 1))), D((K, max(1, nf - 1))), D((K, nz - 1)), D((K, nz - 1))]
    return pl.pallas_call(
        functools.partial(rs_body, nf, nz, chunks, n),
        out_shape=[jax.ShapeDtypeStruct(s, out_dtype) for s in sh],
        in_specs=[pl.BlockSpec(memory_space=pl.ANY)] * n,
        out_specs=[pl.BlockSpec(memory_space=pltpu.VMEM)] * n,
        scratch_shapes=scratch,
        compiler_params=pltpu.CompilerParams(collective_id=cid, has_side_effects=True, vmem_limit_bytes=62 << 20),
        name=name,
    )(*mats)

def swap_body(src_ref, dst_ref, ssem, rsem):
    other = dict(tp=1 - lax.axis_index("tp"))
    barrier = pltpu.get_barrier_semaphore()
    pl.semaphore_signal(barrier, inc=1, device_id=other, device_id_type=MESHT)
    pl.semaphore_wait(barrier, 1)
    cp = pltpu.make_async_remote_copy(src_ref=src_ref, dst_ref=dst_ref, send_sem=ssem, recv_sem=rsem, device_id=other, device_id_type=MESHT)
    cp.start()
    cp.wait()

def swap(v, cid):
    return pl.pallas_call(
        swap_body, out_shape=jax.ShapeDtypeStruct(v.shape, v.dtype),
        in_specs=[pl.BlockSpec(memory_space=VMEM)], out_specs=pl.BlockSpec(memory_space=VMEM),
        scratch_shapes=[pltpu.SemaphoreType.DMA, pltpu.SemaphoreType.DMA],
        compiler_params=pltpu.CompilerParams(collective_id=cid, has_side_effects=True),
        name="tp_swap_%d" % v.shape[0],
    )(v)

def run(body, outs, args, scratch=(), name=None):
    return pl.pallas_call(
        body, out_shape=[jax.ShapeDtypeStruct(s, d) for s, d in outs],
        in_specs=[pl.BlockSpec(memory_space=VMEM)] * len(args),
        out_specs=[pl.BlockSpec(memory_space=VMEM)] * len(outs),
        scratch_shapes=list(scratch), name=name,
        compiler_params=pltpu.CompilerParams(vmem_limit_bytes=60 << 20),
    )(*args)

def chunked(widths, width):
    out = []
    for m, w in enumerate(widths):
        n = max(1, round(w / width))
        c0 = 0
        for i in range(n):
            cn = (w // 128 // n + (1 if i < (w // 128) % n else 0)) * 128
            out.append((m, c0, cn))
            c0 += cn
    return out

def fast(tokens, lengths, attn_gain, w_query, w_key, w_value, w_out, ffn_gain, w_gate, w_up, w_down, cotangent):
    micros, rows, width = tokens.shape
    nf, nctx = lax.axis_size("fsdp"), lax.axis_size("ctx")
    nz = nctx // 2
    tp, t = lax.axis_index("tp"), lax.axis_index("ctx")
    total = rows * nctx
    nblk = total // 2 // rows + 1
    shard = w_query.shape[0]
    qw, ff = w_query.shape[1], w_gate.shape[1]
    M = micros * rows
    def kv3(w):
        w = lax.dynamic_slice_in_dim(w, tp * 2 * HD, 3 * HD, axis=1)
        return w[:, :2 * HD], w[:, 2 * HD:]
    k01, k2 = kv3(w_key); v01, v2 = kv3(w_value)
    sa = jnp.concatenate([w_query, k01, k2, v2, v01], axis=1)
    gains = jnp.concatenate([jnp.broadcast_to(attn_gain[:, None], (shard, 64)), jnp.broadcast_to(ffn_gain[:, None], (shard, 64))], axis=1)
    so = jnp.concatenate([w_out.T, gains], axis=1)
    mats = [sa, so, w_gate, w_up, w_down.T]
    widths = [m.shape[1] for m in mats]
    full = all_gather_weights(nf, nz, mats, chunked(widths, 2000), cid=0)
    A, O, G, U, Dn = [m.reshape(width, m.shape[2]) for m in full]
    gain1 = O[:, qw].astype(F32)[None]
    gain2 = O[:, qw + 64].astype(F32)[None]
    O = O[:, :qw]
    ends = jnp.cumsum(lengths[0], axis=1)
    place = t * rows + jnp.arange(rows, dtype=jnp.int32)
    begin = jnp.sum(jnp.where(place[None, :, None] >= ends[:, None, :], lengths[0][:, None, :], 0), axis=2).reshape(M, 1)
    live = (jnp.tile(place, micros) < jnp.repeat(ends[:, -1], rows)).astype(F32)[:, None]
    inverse = jnp.exp(jnp.arange(HD // 2, dtype=F32) * (-2.0 * math.log(THETA) / HD))
    angle = (jnp.tile(place, micros)[:, None] - begin).astype(F32) * jnp.tile(inverse, 4)[None, :]
    cos, sin = jnp.cos(angle), jnp.sin(angle)
    begin = jnp.broadcast_to(begin, (M, 128))
    live = jnp.broadcast_to(live, (M, 128))
    x = tokens.reshape(M, width)
    n1, q, kv = run(project, [((M, width), B16), ((M, qw), B16), ((M, 384), B16)], [x, gain1, A, cos, sin], name="project")
    kvall, = all_gather_weights(1, nz, [kv], [(0, 0, 384)], cid=1, name="kv_gather")
    pairs = qw // 128
    keys = nblk * rows
    ao, pr, part = run(functools.partial(attention, micros, rows, nblk),
        [((M, qw), B16), ((micros * pairs, rows, 2 * keys), B16), ((M, width), B16)], [q, kvall, begin, O], name="attention")
    peer = swap(part, 2)
    hid, n2, gate, up, act, part2 = run(feed, [((M, width), F32), ((M, width), B16), ((M, ff), F32), ((M, ff), F32), ((M, ff), B16), ((M, width), B16)],
        [x, part, peer, gain2, G, U, Dn], name="feed")
    peer2 = swap(part2, 2)
    output = (hid + (part2.astype(F32) + peer2.astype(F32))).astype(B16)
    g, dpart, gg, gu, gd = run(feed_back, [((M, width), B16), ((M, width), B16), ((width, ff), B16), ((width, ff), B16), ((width, ff), B16)],
        [cotangent.reshape(M, width), live, gate, up, act, n2, G, U, Dn], name="feed_back")
    dpeer = swap(dpart, 2)
    dh, go, gain2_part, dq, dkv = run(functools.partial(attention_back, micros, rows, nblk),
        [((M, width), F32), ((width, qw), B16), ((8, width), F32), ((M, qw), F32), ((nctx, M, 384), B16)],
        [g, dpart, dpeer, hid, gain2, q, kvall, O, ao, pr], scratch=[VMEM((M, qw), B16)], name="attention_back")
    dkv_own, = reduce_scatter_blocks(1, nz, [dkv.reshape(nz, 2, M, 384)], [(0, 0, 384)], cid=3, out_dtype=F32, name="kv_scatter")
    ga, npart = run(project_back, [((width, qw + 384), B16), ((M, width), B16)], [dq, dkv_own, cos, sin, n1, A], scratch=[VMEM((M, qw + 384), B16)], name="project_back")
    npeer = swap(npart, 2)
    dx, gain1_part = run(input_back, [((M, width), F32), ((8, width), F32)], [x, npart, npeer, dh, gain1], name="input_back")
    gains_part = jnp.concatenate([jnp.broadcast_to(gain1_part[0].astype(B16)[:, None], (width, 64)), jnp.broadcast_to(gain2_part[0].astype(B16)[:, None], (width, 64))], axis=1)
    go = jnp.concatenate([go, gains_part], axis=1)
    grads = [m.reshape(nf * nz, 2, shard, m.shape[1]) for m in (gd, gg, gu, go, ga)]
    rd, rg, ru, ro, ra = reduce_scatter_blocks(nf, nz, grads, chunked([m.shape[3] for m in grads], 1024), cid=4)
    half = shard // 2
    kvg = ra[:, qw:].reshape(2, half, 384)
    mine = lax.dynamic_index_in_dim(kvg, tp, 0, keepdims=False)
    theirs = swap(lax.dynamic_index_in_dim(kvg, 1 - tp, 0, keepdims=False), 5)
    low, high = jnp.where(tp == 0, mine, theirs), jnp.where(tp == 0, theirs, mine)
    def spread(lo, hi): return jnp.pad(lo, ((0, 0), (0, 128))) + jnp.pad(hi, ((0, 0), (128, 0)))
    def ks(v): return v[:, :192]
    def vs(v): return jnp.concatenate([v[:, 256:384], v[:, 192:256]], axis=1)
    grad_key = spread(ks(low), ks(high))
    grad_value = spread(vs(low), vs(high))
    return (output.reshape(micros, rows, width), dx.reshape(micros, rows, width), ro[:, qw], ra[:, :qw], grad_key, grad_value,
            ro[:, :qw].T, ro[:, qw + 64], rg, ru, rd.T)


def solution(mesh):
    placed = (
        P(None, ("fsdp", "ctx"), None),
        P("fsdp", None, None),
        P(("fsdp", "ctx")),
        P(("fsdp", "ctx"), "tp"),
        P(("fsdp", "ctx"), None),
        P(("fsdp", "ctx"), None),
        P("tp", ("fsdp", "ctx")),
        P(("fsdp", "ctx")),
        P(("fsdp", "ctx"), "tp"),
        P(("fsdp", "ctx"), "tp"),
        P("tp", ("fsdp", "ctx")),
        P(None, ("fsdp", "ctx"), None),
    )
    def chosen(*args):
        fits = args[3].shape[0] % 16 == 0 and mesh.shape["tp"] == 2 and mesh.shape["ctx"] % 2 == 0
        return (fast if fits else shards)(*args)

    return jax.shard_map(
        chosen,
        mesh=mesh,
        in_specs=placed,
        out_specs=(
            P(None, ("fsdp", "ctx"), None),
            P(None, ("fsdp", "ctx"), None),
            P(("fsdp", "ctx")),
            P(("fsdp", "ctx"), "tp"),
            P(("fsdp", "ctx", "tp"), None),
            P(("fsdp", "ctx", "tp"), None),
            P("tp", ("fsdp", "ctx")),
            P(("fsdp", "ctx")),
            P(("fsdp", "ctx"), "tp"),
            P(("fsdp", "ctx"), "tp"),
            P("tp", ("fsdp", "ctx")),
        ),
        check_vma=False,
    )
```

```python
import functools
import math

import jax
import jax.numpy as jnp
from jax import lax
from jax.experimental import pallas as pl
from jax.experimental.pallas import tpu as pltpu
from jax.sharding import PartitionSpec as P

H = 20
KV = 5
HD = 64


EPSILON = 1e-05
THETA = 10000.0
MASKED = -1e30


def layout(lengths_row, total_rows):
    ending = jnp.cumsum(lengths_row)
    opening = ending - lengths_row
    doc_count = lengths_row.shape[0]
    places = jnp.arange(total_rows, dtype=jnp.int32)
    segment = jnp.sum((places[:, None] >= ending[None, :]).astype(jnp.int32), axis=1)
    firsts = jnp.concatenate([opening, ending[-1:]])
    labels = jnp.arange(doc_count + 1, dtype=jnp.int32)
    begins = jnp.sum(jnp.where(segment[:, None] == labels[None, :], firsts[None, :], 0), axis=1)
    return (segment, places - begins, segment < doc_count)


def rotary(position, head_size):
    halves = head_size // 2
    inverse = jnp.exp(jnp.arange(halves, dtype=jnp.float32) * (-2.0 * math.log(THETA) / head_size))
    angles = position.astype(jnp.float32)[:, None] * inverse[None, :]
    cos_table = jnp.cos(angles)
    sin_table = jnp.sin(angles)
    return (
        jnp.concatenate([cos_table, cos_table], axis=1),
        jnp.concatenate([sin_table, sin_table], axis=1),
    )


def turn(tensor, cos_table, sin_table):
    halves = tensor.shape[-1] // 2
    rotated = jnp.concatenate([-tensor[..., halves:], tensor[..., :halves]], axis=-1)
    return tensor * cos_table[:, None, :] + rotated * sin_table[:, None, :]


def turn_back(tensor, cos_table, sin_table):
    halves = tensor.shape[-1] // 2
    shifted = tensor * sin_table[:, None, :]
    rotated = jnp.concatenate([shifted[..., halves:], -shifted[..., :halves]], axis=-1)
    return tensor * cos_table[:, None, :] + rotated


def norm_back(values, factor, gain_vec, grad_in):
    scaled = gain_vec * grad_in
    return factor * scaled - values * factor**3 * jnp.mean(scaled * values, axis=-1, keepdims=True)


def collect(attn_gain, w_query, w_key, w_value, w_out, ffn_gain, w_gate, w_up, w_down):
    return (
        lax.all_gather(attn_gain, ("fsdp", "ctx"), axis=0, tiled=True),
        lax.all_gather(w_query, ("fsdp", "ctx"), axis=0, tiled=True),
        lax.all_gather(w_key, ("fsdp", "ctx"), axis=0, tiled=True),
        lax.all_gather(w_value, ("fsdp", "ctx"), axis=0, tiled=True),
        lax.all_gather(w_out, ("fsdp", "ctx"), axis=1, tiled=True),
        lax.all_gather(ffn_gain, ("fsdp", "ctx"), axis=0, tiled=True),
        lax.all_gather(w_gate, ("fsdp", "ctx"), axis=0, tiled=True),
        lax.all_gather(w_up, ("fsdp", "ctx"), axis=0, tiled=True),
        lax.all_gather(w_down, ("fsdp", "ctx"), axis=1, tiled=True),
    )


def collect_again(attn_gain, w_query, w_key, w_value, w_out, ffn_gain, w_gate, w_up, w_down):
    return (
        lax.all_gather(attn_gain, ("fsdp", "ctx"), axis=0, tiled=True),
        lax.all_gather(w_query, ("fsdp", "ctx"), axis=0, tiled=True),
        lax.all_gather(w_key, ("fsdp", "ctx"), axis=0, tiled=True),
        lax.all_gather(w_value, ("fsdp", "ctx"), axis=0, tiled=True),
        lax.all_gather(w_out, ("fsdp", "ctx"), axis=1, tiled=True),
        lax.all_gather(ffn_gain, ("fsdp", "ctx"), axis=0, tiled=True),
        lax.all_gather(w_gate, ("fsdp", "ctx"), axis=0, tiled=True),
        lax.all_gather(w_up, ("fsdp", "ctx"), axis=0, tiled=True),
        lax.all_gather(w_down, ("fsdp", "ctx"), axis=1, tiled=True),
    )


def reduce_grads(main_part, pair_part):
    shares = (
        lax.psum_scatter(main_part[0], ("fsdp", "ctx"), scatter_dimension=0, tiled=True),
        lax.psum_scatter(main_part[1], ("fsdp", "ctx"), scatter_dimension=0, tiled=True),
        lax.psum_scatter(main_part[2], ("fsdp", "ctx"), scatter_dimension=1, tiled=True),
        lax.psum_scatter(main_part[3], ("fsdp", "ctx"), scatter_dimension=0, tiled=True),
        lax.psum_scatter(main_part[4], ("fsdp", "ctx"), scatter_dimension=0, tiled=True),
        lax.psum_scatter(main_part[5], ("fsdp", "ctx"), scatter_dimension=0, tiled=True),
        lax.psum_scatter(main_part[6], ("fsdp", "ctx"), scatter_dimension=1, tiled=True),
    )
    pairs = (
        lax.psum_scatter(pair_part[0], ("fsdp", "ctx", "tp"), scatter_dimension=0, tiled=True),
        lax.psum_scatter(pair_part[1], ("fsdp", "ctx", "tp"), scatter_dimension=0, tiled=True),
    )
    return (shares, pairs)


def block_allowed(segment_rows, places_rows, segment_all, block_at, key_block):
    segment_keys = lax.dynamic_slice_in_dim(segment_all, block_at * key_block, key_block)
    place_keys = block_at * key_block + jnp.arange(key_block, dtype=jnp.int32)
    return (segment_rows[:, None] == segment_keys[None, :]) & (
        place_keys[None, :] <= places_rows[:, None]
    )


def sweep(visit, initial, block_count, useful):

    def advance(block_at, state):
        return lax.cond(
            useful(block_at),
            lambda current: visit(block_at, current),
            lambda current: current,
            state,
        )

    return lax.fori_loop(0, block_count, advance, initial)


def shards(
    tokens,
    lengths,
    attn_gain,
    w_query,
    w_key,
    w_value,
    w_out,
    ffn_gain,
    w_gate,
    w_up,
    w_down,
    cotangent,
):
    f32 = jnp.float32
    b16 = jnp.bfloat16
    micro_count = tokens.shape[0]
    tok_rows = tokens.shape[1]
    model_width = tokens.shape[2]
    ctx_count = lax.axis_size("ctx")
    tp_count = lax.axis_size("tp")
    ctx_at = lax.axis_index("ctx")
    tp_at = lax.axis_index("tp")
    total_rows = tok_rows * ctx_count
    half_rows = tok_rows // tp_count
    local_heads = w_query.shape[1] // HD
    kv_width = KV * HD
    scaling = 1.0 / math.sqrt(HD)
    key_block = min(512, total_rows)
    block_count = total_rows // key_block
    heads_global = tp_at * local_heads + jnp.arange(local_heads, dtype=jnp.int32)
    select = heads_global[:, None] // (H // KV) == jnp.arange(KV, dtype=jnp.int32)[None, :]
    select_low = select.astype(b16)
    select_high = select.astype(f32)
    row_offset = tp_at * half_rows
    start_row = ctx_at * tok_rows
    places_mine = start_row + jnp.arange(tok_rows, dtype=jnp.int32)
    outputs_list = []
    input_list = []
    main_total = None
    pair_total = None
    for micro_at in range(micro_count):
        gathered = collect(
            attn_gain, w_query, w_key, w_value, w_out, ffn_gain, w_gate, w_up, w_down
        )
        (
            gain_first,
            query_full,
            key_full,
            value_full,
            out_full,
            gain_second,
            gate_full,
            up_full,
            down_full,
        ) = gathered
        inputs = tokens[micro_at].astype(f32)
        segment_all, position_all, live_all = layout(lengths[0, micro_at], total_rows)
        segment_mine = lax.dynamic_slice_in_dim(segment_all, start_row, tok_rows)
        position_mine = lax.dynamic_slice_in_dim(position_all, start_row, tok_rows)
        live_mine = lax.dynamic_slice_in_dim(live_all, start_row, tok_rows)
        cos_table, sin_table = rotary(position_mine, HD)
        rms_first = lax.rsqrt(jnp.mean(inputs * inputs, axis=-1, keepdims=True) + EPSILON)
        normed_first = (inputs * rms_first * gain_first.astype(f32)).astype(b16)
        queries = jnp.dot(normed_first, query_full, preferred_element_type=f32).reshape(
            tok_rows, local_heads, HD
        )
        queries = turn(queries, cos_table, sin_table).astype(b16)
        key_lin = jnp.dot(normed_first, key_full, preferred_element_type=f32).reshape(
            tok_rows, KV, HD
        )
        key_rot = turn(key_lin, cos_table, sin_table).astype(b16).reshape(tok_rows, kv_width)
        value_rot = jnp.dot(normed_first, value_full, preferred_element_type=f32).astype(b16)
        keys_all, values_all = (
            lax.all_gather(key_rot, "ctx", axis=0, tiled=True),
            lax.all_gather(value_rot, "ctx", axis=0, tiled=True),
        )
        keys_local = jnp.einsum(
            "tjd,hj->thd",
            keys_all.reshape(total_rows, KV, HD),
            select_low,
            preferred_element_type=f32,
        ).astype(b16)
        values_local = jnp.einsum(
            "tjd,hj->thd",
            values_all.reshape(total_rows, KV, HD),
            select_low,
            preferred_element_type=f32,
        ).astype(b16)

        def useful(block_at):
            return jnp.any(
                block_allowed(segment_mine, places_mine, segment_all, block_at, key_block)
            )

        def logits_of(block_at):
            key_rows = lax.dynamic_slice_in_dim(keys_local, block_at * key_block, key_block)
            raw_scores = (
                jnp.einsum("qhd,khd->hqk", queries, key_rows, preferred_element_type=f32) * scaling
            )
            allowed = block_allowed(segment_mine, places_mine, segment_all, block_at, key_block)
            return jnp.where(allowed[None], raw_scores, MASKED)

        def statistic(block_at, state):
            top_score, mass_sum = state
            logits = logits_of(block_at)
            new_top = jnp.maximum(top_score, jnp.max(logits, axis=-1))
            mass_sum = mass_sum * jnp.exp(top_score - new_top) + jnp.sum(
                jnp.exp(logits - new_top[..., None]), axis=-1
            )
            return (new_top, mass_sum)

        start_state = (
            jnp.full((local_heads, tok_rows), MASKED, f32),
            jnp.zeros((local_heads, tok_rows), f32),
        )
        top_score, mass_sum = sweep(statistic, start_state, block_count, useful)

        def probable(block_at):
            return jnp.exp(logits_of(block_at) - top_score[..., None]) / mass_sum[..., None]

        def accumulate(block_at, running):
            probs_low = probable(block_at).astype(b16)
            value_rows = lax.dynamic_slice_in_dim(values_local, block_at * key_block, key_block)
            return running + jnp.einsum(
                "hqk,khd->qhd", probs_low, value_rows, preferred_element_type=f32
            )

        attended = sweep(
            accumulate, jnp.zeros((tok_rows, local_heads, HD), f32), block_count, useful
        )
        attended_low = attended.reshape(tok_rows, local_heads * HD).astype(b16)
        branch = lax.psum(
            jnp.dot(attended_low, out_full, preferred_element_type=f32).astype(jnp.bfloat16), "tp"
        ).astype(jnp.float32)
        hidden = inputs + branch
        rms_second = lax.rsqrt(jnp.mean(hidden * hidden, axis=-1, keepdims=True) + EPSILON)
        normed_second = (hidden * rms_second * gain_second.astype(f32)).astype(b16)
        gate_pre = jnp.dot(normed_second, gate_full, preferred_element_type=f32)
        upward = jnp.dot(normed_second, up_full, preferred_element_type=f32)
        sigmoid_gate = jax.nn.sigmoid(gate_pre)
        silu_gate = jax.nn.silu(gate_pre)
        active = (silu_gate * upward).astype(b16)
        mixed = lax.psum(
            jnp.dot(active, down_full, preferred_element_type=f32).astype(jnp.bfloat16), "tp"
        ).astype(jnp.float32)
        outputs_list.append((hidden + mixed).astype(b16))
        gathered = collect_again(
            attn_gain, w_query, w_key, w_value, w_out, ffn_gain, w_gate, w_up, w_down
        )
        (
            gain_first,
            query_full,
            key_full,
            value_full,
            out_full,
            gain_second,
            gate_full,
            up_full,
            down_full,
        ) = gathered
        grad_rows = cotangent[micro_at].astype(f32) * live_mine[:, None].astype(f32)
        grad_low = grad_rows.astype(b16)
        grad_down = jnp.einsum("tf,td->fd", active, grad_low, preferred_element_type=f32)
        grad_active = jnp.einsum("td,fd->tf", grad_low, down_full, preferred_element_type=f32)
        grad_gate_pre = (
            grad_active * upward * sigmoid_gate * (1.0 + gate_pre * (1.0 - sigmoid_gate))
        ).astype(b16)
        grad_upward = (grad_active * silu_gate).astype(b16)
        grad_gate = jnp.einsum(
            "te,tf->ef", normed_second, grad_gate_pre, preferred_element_type=f32
        )
        grad_up = jnp.einsum("te,tf->ef", normed_second, grad_upward, preferred_element_type=f32)
        grad_normed_second = jnp.einsum(
            "tf,ef->te", grad_gate_pre, gate_full, preferred_element_type=f32
        ) + jnp.einsum("tf,ef->te", grad_upward, up_full, preferred_element_type=f32)
        grad_normed_second = lax.psum(grad_normed_second.astype(jnp.bfloat16), "tp").astype(
            jnp.float32
        )
        grad_gain_second = jnp.sum(grad_normed_second * hidden * rms_second, axis=0)
        grad_hidden = grad_rows + norm_back(
            hidden, rms_second, gain_second.astype(f32), grad_normed_second
        )
        grad_branch = grad_hidden.astype(b16)
        grad_out = jnp.einsum("te,td->ed", attended_low, grad_branch, preferred_element_type=f32)
        grad_att = (
            jnp.einsum("td,ed->te", grad_branch, out_full, preferred_element_type=f32)
            .astype(b16)
            .reshape(tok_rows, local_heads, HD)
        )
        delta_rows = jnp.sum(grad_att.astype(f32) * attended, axis=-1).T

        def backward_visit(block_at, state):
            grad_queries, grad_keys, grad_values = state
            first_row = block_at * key_block
            key_rows = lax.dynamic_slice_in_dim(keys_local, first_row, key_block)
            value_rows = lax.dynamic_slice_in_dim(values_local, first_row, key_block)
            probs = probable(block_at)
            probs_low = probs.astype(b16)
            grad_probs = jnp.einsum(
                "qhd,khd->hqk", grad_att, value_rows, preferred_element_type=f32
            )
            grad_logits = (probs * (grad_probs - delta_rows[..., None])).astype(b16)
            grad_queries = (
                grad_queries
                + jnp.einsum("hqk,khd->qhd", grad_logits, key_rows, preferred_element_type=f32)
                * scaling
            )
            key_part = (
                jnp.einsum("hqk,qhd->khd", grad_logits, queries, preferred_element_type=f32)
                * scaling
            )
            value_part = jnp.einsum("hqk,qhd->khd", probs_low, grad_att, preferred_element_type=f32)
            grad_keys = lax.dynamic_update_slice_in_dim(grad_keys, key_part, first_row, 0)
            grad_values = lax.dynamic_update_slice_in_dim(grad_values, value_part, first_row, 0)
            return (grad_queries, grad_keys, grad_values)

        back_state = (
            jnp.zeros((tok_rows, local_heads, HD), f32),
            jnp.zeros((total_rows, local_heads, HD), f32),
            jnp.zeros((total_rows, local_heads, HD), f32),
        )
        grad_queries, grad_keys, grad_values = sweep(
            backward_visit, back_state, block_count, useful
        )
        key_heads = jnp.einsum(
            "thd,hj->tjd", grad_keys, select_high, precision=lax.Precision.HIGHEST
        ).reshape(total_rows, kv_width)
        value_heads = jnp.einsum(
            "thd,hj->tjd", grad_values, select_high, precision=lax.Precision.HIGHEST
        ).reshape(total_rows, kv_width)
        key_sum, value_sum = (
            lax.psum_scatter(
                key_heads.astype(jnp.bfloat16), ("ctx", "tp"), scatter_dimension=0, tiled=True
            ).astype(jnp.float32),
            lax.psum_scatter(
                value_heads.astype(jnp.bfloat16), ("ctx", "tp"), scatter_dimension=0, tiled=True
            ).astype(jnp.float32),
        )
        cos_half = lax.dynamic_slice_in_dim(cos_table, row_offset, half_rows)
        sin_half = lax.dynamic_slice_in_dim(sin_table, row_offset, half_rows)
        grad_key_lin = (
            turn_back(key_sum.reshape(half_rows, KV, HD), cos_half, sin_half)
            .astype(b16)
            .reshape(half_rows, kv_width)
        )
        grad_value_lin = value_sum.astype(b16)
        normed_half = lax.dynamic_slice_in_dim(normed_first, row_offset, half_rows)
        grad_key = jnp.einsum("te,tk->ek", normed_half, grad_key_lin, preferred_element_type=f32)
        grad_value = jnp.einsum(
            "te,tk->ek", normed_half, grad_value_lin, preferred_element_type=f32
        )
        grad_normed_pair = jnp.einsum(
            "tk,ek->te", grad_key_lin, key_full, preferred_element_type=f32
        ) + jnp.einsum("tk,ek->te", grad_value_lin, value_full, preferred_element_type=f32)
        grad_query_lin = (
            turn_back(grad_queries, cos_table, sin_table)
            .astype(b16)
            .reshape(tok_rows, local_heads * HD)
        )
        grad_query = jnp.einsum(
            "te,tq->eq", normed_first, grad_query_lin, preferred_element_type=f32
        )
        grad_normed_first = jnp.einsum(
            "tq,eq->te", grad_query_lin, query_full, preferred_element_type=f32
        )
        grad_normed_first = grad_normed_first + lax.dynamic_update_slice_in_dim(
            jnp.zeros((tok_rows, model_width), f32), grad_normed_pair, row_offset, 0
        )
        grad_normed_first = lax.psum(grad_normed_first.astype(jnp.bfloat16), "tp").astype(
            jnp.float32
        )
        grad_gain_first = jnp.sum(grad_normed_first * inputs * rms_first, axis=0)
        input_list.append(
            grad_hidden + norm_back(inputs, rms_first, gain_first.astype(f32), grad_normed_first)
        )
        main_part = (
            grad_gain_first,
            grad_query,
            grad_out,
            grad_gain_second,
            grad_gate,
            grad_up,
            grad_down,
        )
        pair_part = (grad_key, grad_value)
        main_part, pair_part = reduce_grads(main_part, pair_part)
        if main_total is None:
            main_total = main_part
            pair_total = pair_part
        else:
            main_total = jax.tree.map(jnp.add, main_total, main_part)
            pair_total = jax.tree.map(jnp.add, pair_total, pair_part)
    return (
        jnp.stack(outputs_list),
        jnp.stack(input_list),
        main_total[0],
        main_total[1],
        pair_total[0],
        pair_total[1],
        main_total[2],
        main_total[3],
        main_total[4],
        main_total[5],
        main_total[6],
    )


F32 = jnp.float32
B16 = jnp.bfloat16
HD = 64
EPSILON = 1e-05
THETA = 10000.0
MASKED = -1e30
SCALE = 1.0 / math.sqrt(HD)
VMEM = pltpu.VMEM

def nn(a, b): return lax.dot_general(a, b, (((1,), (0,)), ((), ())), preferred_element_type=F32)
def nt(a, b): return lax.dot_general(a, b, (((1,), (1,)), ((), ())), preferred_element_type=F32)
def tn(a, b): return lax.dot_general(a, b, (((0,), (0,)), ((), ())), preferred_element_type=F32)

def lanes(shape): return lax.broadcasted_iota(jnp.int32, shape, len(shape) - 1)

def rope(t, cos, sin):
    low = lanes(t.shape) % 64 < 32
    rot = jnp.where(low, -pltpu.roll(t, 96, 1), pltpu.roll(t, 32, 1))
    return t * cos + rot * sin

def rope_back(u, cos, sin):
    low = lanes(u.shape) % 64 < 32
    us = u * sin
    return u * cos + jnp.where(low, pltpu.roll(us, 96, 1), -pltpu.roll(us, 32, 1))

def rms(v): return lax.rsqrt(jnp.mean(v * v, axis=-1, keepdims=True) + EPSILON)

def norm_back(v, r, gain, d):
    s = gain * d
    return r * s - v * (r * r * r) * jnp.mean(s * v, axis=-1, keepdims=True)

def doubled(tile, which):
    t = tile.astype(F32)
    r = pltpu.roll(t, 64, 1)
    low = lanes(t.shape) < 64
    return (jnp.where(low, t, r) if which == 0 else jnp.where(low, r, t)).astype(B16)

def window_start(t, nblk): return jnp.maximum(t - nblk + 1, 0)

def window(kvall_ref, w0, nblk, m, rows, tile):
    return jnp.concatenate([kvall_ref[w0 + b, m * rows:(m + 1) * rows, 128 * tile:128 * (tile + 1)] for b in range(nblk)], axis=0)

def heads_kv(kvall_ref, w0, nblk, m, rows):
    k01 = window(kvall_ref, w0, nblk, m, rows, 0)
    k2v2 = window(kvall_ref, w0, nblk, m, rows, 1)
    v01 = window(kvall_ref, w0, nblk, m, rows, 2)
    ks = [doubled(k01, 0), doubled(k01, 1), doubled(k2v2, 0)]
    vs = [doubled(v01, 0), doubled(v01, 1), doubled(k2v2, 1)]
    return ks, vs

def pick(group, p, tp):
    a, b = p // 2, (p + 1) // 2
    return group[a] if a == b else jnp.where(tp == 0, group[a], group[b])

def stacked(head):
    low = lanes(head.shape) < 64
    zero = jnp.zeros_like(head)
    return jnp.concatenate([jnp.where(low, head, zero), jnp.where(low, zero, head)], axis=0)

def allowed_of(begin, row0, key0, rows, keys):
    i = row0 + lax.broadcasted_iota(jnp.int32, (rows, keys), 0)
    j = key0 + lax.broadcasted_iota(jnp.int32, (rows, keys), 1)
    return (j <= i) & (j >= begin)

MESHT = pl.DeviceIdType.MESH

def n_slots(nf, nz):
    return 3 + (nf - 1) + 2 * (nz - 1) * (2 + nf - 1) + (nf - 1) * nz

def swap_body(src_ref, dst_ref, ssem, rsem):
    other = dict(tp=1 - lax.axis_index("tp"))
    barrier = pltpu.get_barrier_semaphore()
    pl.semaphore_signal(barrier, inc=1, device_id=other, device_id_type=MESHT)
    pl.semaphore_wait(barrier, 1)
    cp = pltpu.make_async_remote_copy(src_ref=src_ref, dst_ref=dst_ref, send_sem=ssem, recv_sem=rsem, device_id=other, device_id_type=MESHT)
    cp.start()
    cp.wait()

def swap(v, cid):
    return pl.pallas_call(
        swap_body, out_shape=jax.ShapeDtypeStruct(v.shape, v.dtype),
        in_specs=[pl.BlockSpec(memory_space=VMEM)], out_specs=pl.BlockSpec(memory_space=VMEM),
        scratch_shapes=[pltpu.SemaphoreType.DMA, pltpu.SemaphoreType.DMA],
        compiler_params=pltpu.CompilerParams(collective_id=cid, has_side_effects=True),
        name="tp_swap_%d" % v.shape[0],
    )(v)

def greet(t, z, c, nz, y, nf, all_z):
    barrier = pltpu.get_barrier_semaphore()
    def sig(**dev):
        pl.semaphore_signal(barrier, inc=1, device_id=dev, device_id_type=MESHT)
    sig(ctx=t + 1 - 2 * c)
    sig(tp=1 - lax.axis_index("tp"))
    for p in range(1, nf): sig(fsdp=lax.rem(y + p, nf))
    if all_z:
        for p in range(1, nz): sig(ctx=lax.rem(z + p, nz) * 2 + c)
        pl.semaphore_wait(barrier, nf + nz)
        return
    @pl.when(z > 0)
    def _(): sig(ctx=t - 2)
    @pl.when(z < nz - 1)
    def _(): sig(ctx=t + 2)
    @pl.when((z > 0) & (z < nz - 1))
    def _(): pl.semaphore_wait(barrier, 3 + nf)
    @pl.when((z == 0) | (z == nz - 1))
    def _(): pl.semaphore_wait(barrier, 2 + nf)

class Gather:
    def __init__(self, nf, nz, at, own_src, send_sem, recv_sem):
        self.nf, self.nz, self.at, self.own_src, self.ss, self.rs = nf, nz, at, own_src, send_sem, recv_sem
        self.y = lax.axis_index("fsdp") if nf > 1 else 0
        self.t = lax.axis_index("ctx")
        self.z, self.c = self.t // 2, lax.rem(self.t, 2)
        self.sib = dict(ctx=self.t + 1 - 2 * self.c)
        self.me = self.shard(self.y, self.z, self.c)
        count = [0]
        def new(n=1):
            count[0] += n
            return count[0] - n
        self.ownL, self.ownR, self.ownC, self.ownY = new(), new(), new(), new(nf - 1)
        self.zs = {(side, d): (new(), new(), new(nf - 1)) for d in range(1, nz) for side in (0, 1)}
        self.yc = {(p, zz): new() for p in range(1, nf) for zz in range(nz)}

    def shard(self, yy, zz, cc): return yy * self.nz * 2 + zz * 2 + cc
    def ydev(self, p): return dict(fsdp=lax.rem(self.y + p, self.nf))
    def copy(self, k, s, slot, dev, src=None):
        return pltpu.make_async_remote_copy(src_ref=self.at(k, s) if src is None else src, dst_ref=self.at(k, s),
            send_sem=self.ss.at[k, slot], recv_sem=self.rs.at[k, s], device_id=dev, device_id_type=MESHT)
    def send(self, *a): self.copy(*a).start()
    def got(self, k, s): self.copy(k, s, 0, self.sib).wait_recv()
    def sent(self, k, slot): self.copy(k, self.me, slot, self.sib).wait_send()
    def when_z(self, side, d):
        z, nz = self.z, self.nz
        return ((z >= d), (z < nz - 1), z - d, self.t + 2) if side == 0 else ((z + d <= nz - 1), (z > 0), z + d, self.t - 2)

    def own(self, k):
        src = self.own_src(k)
        for p in range(1, self.nf): self.send(k, self.me, self.ownY + p - 1, self.ydev(p), src)
        @pl.when(self.z > 0)
        def _(): self.send(k, self.me, self.ownL, dict(ctx=self.t - 2), src)
        @pl.when(self.z < self.nz - 1)
        def _(): self.send(k, self.me, self.ownR, dict(ctx=self.t + 2), src)
        self.send(k, self.me, self.ownC, self.sib, src)

    def zstep(self, k, d, side):
        ok, more, zz, far = self.when_z(side, d)
        s = self.shard(self.y, zz, self.c)
        sf, sc, sy = self.zs[(side, d)]
        @pl.when(ok)
        def _():
            self.got(k, s)
            if d < self.nz - 1:
                @pl.when(more)
                def _(): self.send(k, s, sf, dict(ctx=far))
            for p in range(1, self.nf): self.send(k, s, sy + p - 1, self.ydev(p))
            self.send(k, s, sc, self.sib)

    def ystep(self, k, p, zz):
        s = self.shard(lax.rem(self.y + self.nf - p, self.nf), zz, self.c)
        self.got(k, s)
        self.send(k, s, self.yc[(p, zz)], self.sib)

    def Z(self, k): return [functools.partial(self.zstep, k, d, side) for d in range(1, self.nz) for side in (0, 1)]
    def Zd(self, k, d): return [functools.partial(self.zstep, k, d, side) for side in (0, 1)]
    def Y(self, k): return [functools.partial(self.ystep, k, p, zz) for p in range(1, self.nf) for zz in range(self.nz)]

    def arrived(self, k):
        for yy in range(self.nf):
            for zz in range(self.nz):
                self.got(k, self.shard(yy, zz, 1 - self.c))

    def drain(self, k):
        for p in range(1, self.nf): self.sent(k, self.ownY + p - 1)
        @pl.when(self.z > 0)
        def _(): self.sent(k, self.ownL)
        @pl.when(self.z < self.nz - 1)
        def _(): self.sent(k, self.ownR)
        self.sent(k, self.ownC)
        for d in range(1, self.nz):
            for side in (0, 1):
                ok, more, _zz, _far = self.when_z(side, d)
                sf, sc, sy = self.zs[(side, d)]
                @pl.when(ok)
                def _():
                    if d < self.nz - 1:
                        @pl.when(more)
                        def _(): self.sent(k, sf)
                    for p in range(1, self.nf): self.sent(k, sy + p - 1)
                    self.sent(k, sc)
        for v in self.yc.values(): self.sent(k, v)

def emit(*lists):
    for steps in lists:
        for step in steps: step()

def front(nf, nz, micros, rows, nblk, chunks, shard,
          x_ref, cos_ref, sin_ref, begin_ref, sa, so, sg, su, sd,
          A, O, G, U, D, kvall_ref, n1_ref, q_ref, ao_ref, pr_ref, part_ref, peer_ref, gains_ref,
          xr_ref, wss, wrs, lsem, kss, krs, pss, prs):
    t = lax.axis_index("ctx"); tp = lax.axis_index("tp")
    y = lax.axis_index("fsdp") if nf > 1 else 0
    z, c = t // 2, lax.rem(t, 2)
    greet(t, z, c, nz, y, nf, False)
    shards, outs = [sa, so, sg, su, sd], [A, O, G, U, D]
    def at(k, s):
        m, c0, cn = chunks[k]
        return outs[m].at[pl.ds(pl.multiple_of(s * shard, 16), shard), pl.ds(c0, cn)]
    def own_src(k):
        m, c0, cn = chunks[k]
        return shards[m].at[:, pl.ds(c0, cn)]
    W = Gather(nf, nz, at, own_src, wss, wrs)
    V = Gather(1, nz, lambda k, s: kvall_ref.at[s], lambda k: kvall_ref.at[t], kss, krs)
    K = len(chunks)
    def local(m):
        return pltpu.make_async_copy(shards[m], outs[m].at[pl.ds(pl.multiple_of(W.me * shard, 16), shard), :], lsem.at[m])
    other = dict(tp=1 - tp)
    def swap_part(m):
        sl = pl.ds(m * rows, rows)
        return pltpu.make_async_remote_copy(src_ref=part_ref.at[sl, :], dst_ref=peer_ref.at[sl, :], send_sem=pss.at[m], recv_sem=prs.at[m], device_id=other, device_id_type=MESHT)
    for k in range(3): W.own(k)
    for m in range(5): local(m).start()
    x = x_ref[...].astype(F32)
    xr_ref[...] = x * rms(x)
    emit(W.Z(0))
    W.own(3)
    emit(W.Z(1), W.Y(0), W.Z(2), W.Y(1))
    local(0).wait()
    W.arrived(0); W.arrived(1)
    qw = q_ref.shape[1]
    sel = (lax.broadcasted_iota(jnp.int32, (8, 128), 1) == jnp.where(lax.broadcasted_iota(jnp.int32, (8, 128), 0) < 4, 0, 64)).astype(B16)
    gains = nt(sel, A[:, qw + 384:qw + 512])
    gains_ref[...] = gains
    n1_ref[...] = (xr_ref[...] * gains[0:1, :]).astype(B16)
    cos, sin = cos_ref[...], sin_ref[...]
    lin = nn(n1_ref[...], A[:, qw:qw + 384])
    low = lanes((lin.shape[0], 128)) < 64
    mid = lin[:, 128:256]
    kvall_ref[t, :, 0:128] = rope(lin[:, :128], cos, sin).astype(B16)
    kvall_ref[t, :, 128:256] = jnp.where(low, rope(mid, cos, sin), mid).astype(B16)
    kvall_ref[t, :, 256:384] = lin[:, 256:384].astype(B16)
    z3, y2 = W.Z(3), W.Y(2)
    emit(z3[:1])
    V.own(0)
    emit(z3[1:2])
    lin = nn(n1_ref[...], A[:, :qw])
    for i in range(qw // 128):
        q_ref[:, 128 * i:128 * (i + 1)] = rope(lin[:, 128 * i:128 * (i + 1)], cos, sin).astype(B16)
    W.own(4)
    emit(z3[2:], V.Zd(0, 1), y2)
    W.own(5)
    z4 = W.Z(4)
    emit(z4[:4])
    for d in range(2, nz): emit(V.Zd(0, d), z4[2 * d:2 * d + 2])
    emit(W.Y(3))
    V.arrived(0)
    local(1).wait()
    W.arrived(2)
    W.own(6)
    pump = W.Z(5) + W.Y(4) + [functools.partial(W.own, 7)] + W.Z(6)
    w0 = window_start(t, nblk)
    keys = nblk * rows
    pairs = qw // 128
    done = 0
    for m in range(micros):
        sl = slice(m * rows, (m + 1) * rows)
        ks, vs = heads_kv(kvall_ref, w0, nblk, m, rows)
        ok = allowed_of(begin_ref[sl, :1], t * rows, w0 * rows, rows, keys)
        for p in range(pairs):
            kb = stacked(pick(ks, p, tp)); vb = stacked(pick(vs, p, tp))
            s = nt(q_ref[sl, 128 * p:128 * (p + 1)], kb) * SCALE
            halves = []
            for h in range(2):
                sh = jnp.where(ok, s[:, h * keys:(h + 1) * keys], MASKED)
                e = jnp.exp(sh - jnp.max(sh, axis=-1, keepdims=True))
                halves.append((e / jnp.sum(e, axis=-1, keepdims=True)).astype(B16))
            pr = jnp.concatenate(halves, axis=1)
            pr_ref[m * pairs + p] = pr
            ao_ref[sl, 128 * p:128 * (p + 1)] = nn(pr, vb).astype(B16)
            upto = len(pump) * (m * pairs + p + 1) // (micros * pairs)
            emit(pump[done:upto])
            done = upto
        part_ref[sl, :] = nt(ao_ref[sl, :], O[...]).astype(B16)
        swap_part(m).start()
    emit(pump[done:])
    W.own(8)
    emit(W.Y(5), W.Z(7), W.Y(6), W.Z(8), W.Y(7), W.Y(8))
    for k in range(3, K): W.arrived(k)
    for m in range(2, 5): local(m).wait()
    for m in range(micros): swap_part(m).wait()
    for k in range(K): W.drain(k)
    V.drain(0)

def middle(x_ref, p1_ref, r1_ref, gains_ref, G_hbm, U_hbm, D_hbm, ct_ref, live_ref,
           hid_ref, part_ref, g_ref, dpart_ref, gg_hbm, gu_hbm, gd_hbm,
           G, U, D, gate_ref, up_ref, act_ref, n2_ref, gg, gu, gd, sem):
    loads = [pltpu.make_async_copy(a, b, sem.at[i]) for i, (a, b) in enumerate(((G_hbm, G), (U_hbm, U), (D_hbm, D)))]
    for cp in loads: cp.start()
    hid = x_ref[...].astype(F32) + (p1_ref[...].astype(F32) + r1_ref[...].astype(F32))
    hid_ref[...] = hid
    n2_ref[...] = (hid * rms(hid) * gains_ref[4:5, :]).astype(B16)
    g_ref[...] = (ct_ref[...].astype(F32) * live_ref[:, :1]).astype(B16)
    loads[0].wait()
    gate_ref[...] = nn(n2_ref[...], G[...])
    loads[1].wait()
    up_ref[...] = nn(n2_ref[...], U[...])
    gate = gate_ref[...]
    act_ref[...] = (gate * jax.nn.sigmoid(gate) * up_ref[...]).astype(B16)
    stores = [pltpu.make_async_copy(b, a, sem.at[3 + i]) for i, (a, b) in enumerate(((gg_hbm, gg), (gu_hbm, gu), (gd_hbm, gd)))]
    gd[...] = tn(g_ref[...], act_ref[...]).astype(B16)
    stores[2].start()
    loads[2].wait()
    part_ref[...] = nt(act_ref[...], D[...]).astype(B16)
    da = nn(g_ref[...], D[...])
    gate = gate_ref[...]; up = up_ref[...]
    sg = jax.nn.sigmoid(gate)
    dgate = (da * up * sg * (1.0 + gate * (1.0 - sg))).astype(B16)
    dup = (da * (gate * sg)).astype(B16)
    gg[...] = tn(n2_ref[...], dgate).astype(B16)
    stores[0].start()
    gu[...] = tn(n2_ref[...], dup).astype(B16)
    stores[1].start()
    dpart_ref[...] = (nt(dgate, G[...]) + nt(dup, U[...])).astype(B16)
    for cp in stores: cp.wait()

def back(nf, nz, micros, rows, nblk, chunks, shard,
         gd, gg, gu, g_ref, dpart_ref, part2_ref, hid_ref, gains_ref, q_ref, kvall_ref, O, A, ao_ref, pr_ref, n1_ref, cos_ref, sin_ref, x_ref,
         rd, rg, ru, ro, ra, dx_ref, out_ref,
         own_d, own_g, own_u, c_d, c_g, c_u, c_o, c_a, y_d, y_g, y_u, y_o, y_a, z_d, z_g, z_u, z_o, z_a,
         go_ref, ga_ref, dh_ref, do_ref, dq_ref, dkv_ref, kc_ref, kz_ref, dl_ref, dpeer_ref, peer2_ref, npart_ref, npeer_ref,
         lsem, cs, cr, ys, yr, zs, zr, kcs, kcr, kzs, kzr, ss, sr):
    t = lax.axis_index("ctx"); tp = lax.axis_index("tp")
    y = lax.axis_index("fsdp") if nf > 1 else 0
    z, c = t // 2, lax.rem(t, 2)
    nb = nf * nz
    greet(t, z, c, nz, y, nf, True)
    ins, outs = [gd, gg, gu, go_ref, ga_ref], [rd, rg, ru, ro, ra]
    crecv, yrecv, zrecv = [c_d, c_g, c_u, c_o, c_a], [y_d, y_g, y_u, y_o, y_a], [z_d, z_g, z_u, z_o, z_a]
    acc = [own_d, own_g, own_u, c_o, c_a]
    sib, other = dict(ctx=t + 1 - 2 * c), dict(tp=1 - tp)
    def zdev(p): return lax.rem(z + p, nz)
    def remote(src, dst, s, r, dev):
        return pltpu.make_async_remote_copy(src_ref=src, dst_ref=dst, send_sem=s, recv_sem=r, device_id=dev, device_id_type=MESHT)
    def ccopy(k):
        m, c0, cn = chunks[k]
        return remote(ins[m].at[:, 1 - c, :, pl.ds(c0, cn)], crecv[m].at[:, :, pl.ds(c0, cn)], cs.at[k], cr.at[k], sib)
    def lcopy(k):
        m, c0, cn = chunks[k]
        return pltpu.make_async_copy(ins[m].at[:, c, :, pl.ds(c0, cn)], acc[m].at[:, :, pl.ds(c0, cn)], lsem.at[k])
    def ycopy(k, p):
        m, c0, cn = chunks[k]
        yy = lax.rem(y + p, nf)
        return remote(acc[m].at[pl.ds(yy * nz, nz), :, pl.ds(c0, cn)], yrecv[m].at[p - 1, :, :, pl.ds(c0, cn)], ys.at[k, p - 1], yr.at[k, p - 1], dict(fsdp=yy))
    def zcopy(k, p):
        m, c0, cn = chunks[k]
        return remote(acc[m].at[y * nz + zdev(p), :, pl.ds(c0, cn)], zrecv[m].at[p - 1, :, pl.ds(c0, cn)], zs.at[k, p - 1], zr.at[k, p - 1], dict(ctx=zdev(p) * 2 + c))
    def stage_core(k):
        m, c0, cn = chunks[k]
        cols = pl.ds(c0, cn)
        if m < 3: lcopy(k).wait()
        ccopy(k).wait_recv()
        def add(b, _):
            first = acc[m][b, :, cols] if m < 3 else ins[m][b, c, :, cols]
            acc[m][b, :, cols] = first + crecv[m][b, :, cols]
            return _
        lax.fori_loop(0, nb, add, 0)
        for p in range(1, nf): ycopy(k, p).start()
    def stage_y(k):
        m, c0, cn = chunks[k]
        cols = pl.ds(c0, cn)
        for p in range(1, nf): ycopy(k, p).wait_recv()
        def add(b, _):
            total = acc[m][y * nz + b, :, cols].astype(F32)
            for p in range(1, nf): total = total + yrecv[m][p - 1, b, :, cols].astype(F32)
            acc[m][y * nz + b, :, cols] = total.astype(B16)
            return _
        lax.fori_loop(0, nz, add, 0)
        for p in range(1, nz): zcopy(k, p).start()
    def stage_z(k):
        m, c0, cn = chunks[k]
        cols = pl.ds(c0, cn)
        for p in range(1, nz): zcopy(k, p).wait_recv()
        total = acc[m][y * nz + z, :, cols].astype(F32)
        for p in range(1, nz): total = total + zrecv[m][p - 1, :, cols].astype(F32)
        outs[m][:, cols] = total
    dswap = remote(dpart_ref, dpeer_ref, ss.at[0], sr.at[0], other)
    oswap = remote(part2_ref, peer2_ref, ss.at[1], sr.at[1], other)
    nswap = remote(npart_ref, npeer_ref, ss.at[2], sr.at[2], other)
    K = len(chunks)
    dswap.start()
    for k in range(6):
        ccopy(k).start(); lcopy(k).start()
    dkv_ref[...] = jnp.zeros_like(dkv_ref)
    stage_core(0); stage_core(1); stage_core(2)
    dswap.wait_recv()
    oswap.start()
    dn2 = dpart_ref[...].astype(F32) + dpeer_ref[...].astype(F32)
    hid = hid_ref[...]
    r2 = rms(hid)
    gain2 = jnp.sum(dn2 * hid * r2, axis=0, keepdims=True)
    dh = g_ref[...].astype(F32) + norm_back(hid, r2, gains_ref[4:5, :], dn2)
    dh_ref[...] = dh
    db = dh.astype(B16)
    do_ref[...] = nn(db, O[...]).astype(B16)
    stage_y(0)
    go = tn(db, ao_ref[...]).astype(B16)
    for s in range(2 * nb): go_ref[s // 2, s % 2] = go[s * shard:(s + 1) * shard]
    stage_core(3)
    ccopy(6).start()
    w0 = window_start(t, nblk)
    keys = nblk * rows
    pairs = q_ref.shape[1] // 128
    low = lanes((keys, 128)) < 64
    pump = [functools.partial(stage_y, 1), functools.partial(stage_z, 0), functools.partial(stage_core, 4)]
    for m in range(micros):
        sl = slice(m * rows, (m + 1) * rows)
        ks, vs = heads_kv(kvall_ref, w0, nblk, m, rows)
        dks = [jnp.zeros((keys, 128), F32) for _ in range(3)]
        dvs = [jnp.zeros((keys, 128), F32) for _ in range(3)]
        for p in range(pairs):
            kb = stacked(pick(ks, p, tp)); vb = stacked(pick(vs, p, tp))
            qt = q_ref[sl, 128 * p:128 * (p + 1)]
            dot_ = do_ref[sl, 128 * p:128 * (p + 1)]
            pr = pr_ref[m * pairs + p]
            dp = nt(dot_, vb)
            halves = []
            for h in range(2):
                ph = pr[:, h * keys:(h + 1) * keys].astype(F32)
                dph = dp[:, h * keys:(h + 1) * keys]
                delta = jnp.sum(ph * dph, axis=-1, keepdims=True)
                halves.append((ph * (dph - delta)).astype(B16))
            ds = jnp.concatenate(halves, axis=1)
            dq_ref[sl, 128 * p:128 * (p + 1)] = nn(ds, kb) * SCALE
            dkb = tn(ds, qt) * SCALE
            dvb = tn(pr, dot_)
            dk = jnp.where(low, dkb[:keys], dkb[keys:])
            dv = jnp.where(low, dvb[:keys], dvb[keys:])
            a, b = p // 2, (p + 1) // 2
            if a == b:
                dks[a] = dks[a] + dk; dvs[a] = dvs[a] + dv
            else:
                first = (tp == 0).astype(F32); second = 1.0 - first
                dks[a] = dks[a] + dk * first; dvs[a] = dvs[a] + dv * first
                dks[b] = dks[b] + dk * second; dvs[b] = dvs[b] + dv * second
        def full(v): return v + pltpu.roll(v, 64, 1)
        dk0, dk1, dk2 = [full(v) for v in dks]
        dv0, dv1, dv2 = [full(v) for v in dvs]
        tiles = [jnp.where(low, dk0, dk1), jnp.where(low, dk2, dv2), jnp.where(low, dv0, dv1)]
        for b in range(nblk):
            at = w0 + b
            for i in range(3):
                dkv_ref[at // 2, lax.rem(at, 2), m * rows:(m + 1) * rows, 128 * i:128 * (i + 1)] = tiles[i][b * rows:(b + 1) * rows].astype(B16)
        if m == 0: emit(pump[:2])
    kvc = remote(dkv_ref.at[:, 1 - c], kc_ref, kcs.at[0], kcr.at[0], sib)
    def kvz(p): return remote(kc_ref.at[zdev(p)], kz_ref.at[p - 1], kzs.at[p - 1], kzr.at[p - 1], dict(ctx=zdev(p) * 2 + c))
    kvc.start()
    emit(pump[2:])
    kvc.wait_recv()
    def add_kv(b, _):
        kc_ref[b] = kc_ref[b] + dkv_ref[b, c]
        return _
    lax.fori_loop(0, nz, add_kv, 0)
    for p in range(1, nz): kvz(p).start()
    stage_y(2); stage_z(1); stage_core(5)
    oswap.wait_recv()
    out_ref[...] = (hid_ref[...] + (part2_ref[...].astype(F32) + peer2_ref[...].astype(F32))).astype(B16)
    stage_y(3); stage_z(2)
    for p in range(1, nz): kvz(p).wait_recv()
    dkv = kc_ref[z].astype(F32)
    for p in range(1, nz): dkv = dkv + kz_ref[p - 1].astype(F32)
    cos, sin = cos_ref[...], sin_ref[...]
    qw = q_ref.shape[1]
    for i in range(qw // 128):
        dl_ref[:, 128 * i:128 * (i + 1)] = rope_back(dq_ref[:, 128 * i:128 * (i + 1)], cos, sin).astype(B16)
    mid = dkv[:, 128:256]
    dl_ref[:, qw:qw + 128] = rope_back(dkv[:, :128], cos, sin).astype(B16)
    dl_ref[:, qw + 128:qw + 256] = jnp.where(lanes(mid.shape) < 64, rope_back(mid, cos, sin), mid).astype(B16)
    dl_ref[:, qw + 256:qw + 384] = dkv[:, 256:384].astype(B16)
    npart_ref[...] = nt(dl_ref[...], A[:, :qw + 384]).astype(B16)
    nswap.start()
    stage_core(6)
    ga = tn(n1_ref[...], dl_ref[...]).astype(B16)
    for s in range(2 * nb): ga_ref[s // 2, s % 2, :, :qw + 384] = ga[s * shard:(s + 1) * shard]
    ccopy(7).start()
    stage_y(4); stage_z(3)
    stage_core(7)
    stage_y(5); stage_z(4)
    nswap.wait_recv()
    x = x_ref[...].astype(F32)
    r1 = rms(x)
    dn1 = npart_ref[...].astype(F32) + npeer_ref[...].astype(F32)
    gain1 = jnp.sum(dn1 * x * r1, axis=0, keepdims=True)
    both = jnp.where(lax.broadcasted_iota(jnp.int32, (8, x.shape[1]), 0) < 4, gain1, gain2).astype(B16)
    sel = ((lanes((8, 128)) < 64) & (lax.broadcasted_iota(jnp.int32, (8, 128), 0) == 0)) | ((lanes((8, 128)) >= 64) & (lax.broadcasted_iota(jnp.int32, (8, 128), 0) == 4))
    gcol = tn(both, sel.astype(B16)).astype(B16)
    for s in range(2 * nb): ga_ref[s // 2, s % 2, :, qw + 384:qw + 512] = gcol[s * shard:(s + 1) * shard]
    ccopy(8).start()
    dx_ref[...] = dh_ref[...] + norm_back(x, r1, gains_ref[0:1, :], dn1)
    stage_core(8)
    stage_y(6); stage_z(5); stage_y(7); stage_z(6); stage_y(8); stage_z(7); stage_z(8)
    for cp in (dswap, oswap, nswap, kvc): cp.wait_send()
    for p in range(1, nz): kvz(p).wait_send()
    for k in range(K):
        ccopy(k).wait_send()
        for p in range(1, nf): ycopy(k, p).wait_send()
        for p in range(1, nz): zcopy(k, p).wait_send()

def fast(tokens, lengths, attn_gain, w_query, w_key, w_value, w_out, ffn_gain, w_gate, w_up, w_down, cotangent):
    micros, rows, width = tokens.shape
    nf, nctx = lax.axis_size("fsdp"), lax.axis_size("ctx")
    nz = nctx // 2
    nb = nf * nz
    tp, t = lax.axis_index("tp"), lax.axis_index("ctx")
    total = rows * nctx
    nblk = total // 2 // rows + 1
    shard = w_query.shape[0]
    qw, ff = w_query.shape[1], w_gate.shape[1]
    M = micros * rows
    def kv3(w):
        w = lax.dynamic_slice_in_dim(w, tp * 2 * HD, 3 * HD, axis=1)
        return w[:, :2 * HD], w[:, 2 * HD:]
    k01, k2 = kv3(w_key); v01, v2 = kv3(w_value)
    gains = [jnp.broadcast_to(v[:, None], (shard, 64)) for v in (attn_gain, ffn_gain)]
    sa = jnp.concatenate([w_query, k01, k2, v2, v01] + gains, axis=1)
    aw = qw + 512
    ends = jnp.cumsum(lengths[0], axis=1)
    place = t * rows + jnp.arange(rows, dtype=jnp.int32)
    begin = jnp.sum(jnp.where(place[None, :, None] >= ends[:, None, :], lengths[0][:, None, :], 0), axis=2).reshape(M, 1)
    live = (jnp.tile(place, micros) < jnp.repeat(ends[:, -1], rows)).astype(F32)[:, None]
    inverse = jnp.exp(jnp.arange(HD // 2, dtype=F32) * (-2.0 * math.log(THETA) / HD))
    angle = (jnp.tile(place, micros)[:, None] - begin).astype(F32) * jnp.tile(inverse, 4)[None, :]
    cos, sin = jnp.cos(angle), jnp.sin(angle)
    begin = jnp.broadcast_to(begin, (M, 128))
    live = jnp.broadcast_to(live, (M, 128))
    x = tokens.reshape(M, width)
    pairs = qw // 128
    keys = nblk * rows
    half = ff // 2
    S = pltpu.SemaphoreType.DMA
    inv, ina = pl.BlockSpec(memory_space=VMEM), pl.BlockSpec(memory_space=pl.ANY)
    ns = nb * 2
    wide = [(m, h * half, half) for m in (2, 3, 4) for h in range(2)]
    chunks = [(0, 0, qw), (0, qw, 512), (1, 0, qw)] + wide
    outs = [((width, aw), B16), ((width, qw), B16), ((width, ff), B16), ((width, ff), B16), ((width, ff), B16), ((nctx, M, 384), B16),
        ((M, width), B16), ((M, qw), B16), ((M, qw), B16), ((micros * pairs, rows, 2 * keys), B16), ((M, width), B16), ((M, width), B16), ((8, width), F32)]
    A, O, G, U, Dn, kvall, n1, q, ao, pr, part, peer, gains = pl.pallas_call(
        functools.partial(front, nf, nz, micros, rows, nblk, chunks, shard),
        out_shape=[jax.ShapeDtypeStruct(s, d) for s, d in outs],
        in_specs=[inv] * 9, out_specs=[inv, inv, ina, ina, ina] + [inv] * 8,
        scratch_shapes=[VMEM((M, width), F32), S((9, n_slots(nf, nz))), S((9, ns)), S((5,)), S((1, n_slots(1, nz))), S((1, nctx)), S((micros,)), S((micros,))],
        compiler_params=pltpu.CompilerParams(collective_id=0, has_side_effects=True, vmem_limit_bytes=60 << 20), name="front",
    )(x, cos, sin, begin, sa, w_out.T, w_gate, w_up, w_down.T)
    outs = [((M, width), F32), ((M, width), B16), ((M, width), B16), ((M, width), B16)] + [((width, ff), B16)] * 3
    hid, part2, g, dpart, gg, gu, gd = pl.pallas_call(
        middle, out_shape=[jax.ShapeDtypeStruct(s, d) for s, d in outs],
        in_specs=[inv] * 4 + [ina] * 3 + [inv] * 2, out_specs=[inv] * 4 + [ina] * 3,
        scratch_shapes=[VMEM((width, ff), B16)] * 3 + [VMEM((M, ff), F32)] * 2 + [VMEM((M, ff), B16), VMEM((M, width), B16)] + [VMEM((width, ff), B16)] * 3 + [S((6,))],
        compiler_params=pltpu.CompilerParams(vmem_limit_bytes=60 << 20), name="middle",
    )(x, part, peer, gains, G, U, Dn, cotangent.reshape(M, width), live)
    chunks = [(m, h * half, half) for m in range(3) for h in range(2)] + [(3, 0, qw), (4, 0, qw), (4, qw, 512)]
    wd = [ff, ff, ff, qw, aw]
    K = len(chunks)
    outs = [((shard, w), F32) for w in wd] + [((M, width), F32), ((M, width), B16)]
    scratch = [VMEM((nb, shard, w), B16) for w in wd[:3]] + [VMEM((nb, shard, w), B16) for w in wd] + [VMEM((nf - 1, nz, shard, w), B16) for w in wd] + [VMEM((nz - 1, shard, w), B16) for w in wd]
    scratch += [VMEM((nb, 2, shard, qw), B16), VMEM((nb, 2, shard, aw), B16), VMEM((M, width), F32), VMEM((M, qw), B16), VMEM((M, qw), F32), VMEM((nz, 2, M, 384), B16),
        VMEM((nz, M, 384), B16), VMEM((nz - 1, M, 384), B16), VMEM((M, qw + 384), B16)] + [VMEM((M, width), B16)] * 4
    scratch += [S((K,)), S((K,)), S((K,)), S((K, nf - 1)), S((K, nf - 1)), S((K, nz - 1)), S((K, nz - 1)), S((1,)), S((1,)), S((nz - 1,)), S((nz - 1,)), S((3,)), S((3,))]
    rd, rg, ru, ro, ra, dx, output = pl.pallas_call(
        functools.partial(back, nf, nz, micros, rows, nblk, chunks, shard),
        out_shape=[jax.ShapeDtypeStruct(s, d) for s, d in outs],
        in_specs=[ina] * 3 + [inv] * 15, out_specs=[inv] * 7, scratch_shapes=scratch,
        compiler_params=pltpu.CompilerParams(collective_id=4, has_side_effects=True, vmem_limit_bytes=63 << 20), name="back",
    )(*[m.reshape(nb, 2, shard, ff) for m in (gd, gg, gu)], g, dpart, part2, hid, gains, q, kvall, O, A, ao, pr, n1, cos, sin, x)
    hs = shard // 2
    kvg = ra[:, qw:qw + 384].reshape(2, hs, 384)
    mine = lax.dynamic_index_in_dim(kvg, tp, 0, keepdims=False)
    theirs = swap(lax.dynamic_index_in_dim(kvg, 1 - tp, 0, keepdims=False), 5)
    low, high = jnp.where(tp == 0, mine, theirs), jnp.where(tp == 0, theirs, mine)
    def spread(lo, hi): return jnp.pad(lo, ((0, 0), (0, 128))) + jnp.pad(hi, ((0, 0), (128, 0)))
    def ks(v): return v[:, :192]
    def vs(v): return jnp.concatenate([v[:, 256:384], v[:, 192:256]], axis=1)
    grad_key = spread(ks(low), ks(high))
    grad_value = spread(vs(low), vs(high))
    return (output.reshape(micros, rows, width), dx.reshape(micros, rows, width), ra[:, qw + 384], ra[:, :qw], grad_key, grad_value,
            ro.T, ra[:, qw + 448], rg, ru, rd.T)


def solution(mesh):
    placed = (
        P(None, ("fsdp", "ctx"), None),
        P("fsdp", None, None),
        P(("fsdp", "ctx")),
        P(("fsdp", "ctx"), "tp"),
        P(("fsdp", "ctx"), None),
        P(("fsdp", "ctx"), None),
        P("tp", ("fsdp", "ctx")),
        P(("fsdp", "ctx")),
        P(("fsdp", "ctx"), "tp"),
        P(("fsdp", "ctx"), "tp"),
        P("tp", ("fsdp", "ctx")),
        P(None, ("fsdp", "ctx"), None),
    )
    def chosen(*args):
        fits = args[3].shape[0] % 16 == 0 and mesh.shape["tp"] == 2 and mesh.shape["fsdp"] == 2 and mesh.shape["ctx"] % 2 == 0
        return (fast if fits else shards)(*args)

    return jax.shard_map(
        chosen,
        mesh=mesh,
        in_specs=placed,
        out_specs=(
            P(None, ("fsdp", "ctx"), None),
            P(None, ("fsdp", "ctx"), None),
            P(("fsdp", "ctx")),
            P(("fsdp", "ctx"), "tp"),
            P(("fsdp", "ctx", "tp"), None),
            P(("fsdp", "ctx", "tp"), None),
            P("tp", ("fsdp", "ctx")),
            P(("fsdp", "ctx")),
            P(("fsdp", "ctx"), "tp"),
            P(("fsdp", "ctx"), "tp"),
            P("tp", ("fsdp", "ctx")),
        ),
        check_vma=False,
    )
```

```python
import functools
import math

import jax
import jax.numpy as jnp
from jax import lax
from jax.experimental import pallas as pl
from jax.experimental.pallas import tpu as pltpu
from jax.sharding import PartitionSpec as P

H = 20
KV = 5
HD = 64


EPSILON = 1e-05
THETA = 10000.0
MASKED = -1e30


def layout(lengths_row, total_rows):
    ending = jnp.cumsum(lengths_row)
    opening = ending - lengths_row
    doc_count = lengths_row.shape[0]
    places = jnp.arange(total_rows, dtype=jnp.int32)
    segment = jnp.sum((places[:, None] >= ending[None, :]).astype(jnp.int32), axis=1)
    firsts = jnp.concatenate([opening, ending[-1:]])
    labels = jnp.arange(doc_count + 1, dtype=jnp.int32)
    begins = jnp.sum(jnp.where(segment[:, None] == labels[None, :], firsts[None, :], 0), axis=1)
    return (segment, places - begins, segment < doc_count)


def rotary(position, head_size):
    halves = head_size // 2
    inverse = jnp.exp(jnp.arange(halves, dtype=jnp.float32) * (-2.0 * math.log(THETA) / head_size))
    angles = position.astype(jnp.float32)[:, None] * inverse[None, :]
    cos_table = jnp.cos(angles)
    sin_table = jnp.sin(angles)
    return (
        jnp.concatenate([cos_table, cos_table], axis=1),
        jnp.concatenate([sin_table, sin_table], axis=1),
    )


def turn(tensor, cos_table, sin_table):
    halves = tensor.shape[-1] // 2
    rotated = jnp.concatenate([-tensor[..., halves:], tensor[..., :halves]], axis=-1)
    return tensor * cos_table[:, None, :] + rotated * sin_table[:, None, :]


def turn_back(tensor, cos_table, sin_table):
    halves = tensor.shape[-1] // 2
    shifted = tensor * sin_table[:, None, :]
    rotated = jnp.concatenate([shifted[..., halves:], -shifted[..., :halves]], axis=-1)
    return tensor * cos_table[:, None, :] + rotated


def norm_back(values, factor, gain_vec, grad_in):
    scaled = gain_vec * grad_in
    return factor * scaled - values * factor**3 * jnp.mean(scaled * values, axis=-1, keepdims=True)


def collect(attn_gain, w_query, w_key, w_value, w_out, ffn_gain, w_gate, w_up, w_down):
    return (
        lax.all_gather(attn_gain, ("fsdp", "ctx"), axis=0, tiled=True),
        lax.all_gather(w_query, ("fsdp", "ctx"), axis=0, tiled=True),
        lax.all_gather(w_key, ("fsdp", "ctx"), axis=0, tiled=True),
        lax.all_gather(w_value, ("fsdp", "ctx"), axis=0, tiled=True),
        lax.all_gather(w_out, ("fsdp", "ctx"), axis=1, tiled=True),
        lax.all_gather(ffn_gain, ("fsdp", "ctx"), axis=0, tiled=True),
        lax.all_gather(w_gate, ("fsdp", "ctx"), axis=0, tiled=True),
        lax.all_gather(w_up, ("fsdp", "ctx"), axis=0, tiled=True),
        lax.all_gather(w_down, ("fsdp", "ctx"), axis=1, tiled=True),
    )


def collect_again(attn_gain, w_query, w_key, w_value, w_out, ffn_gain, w_gate, w_up, w_down):
    return (
        lax.all_gather(attn_gain, ("fsdp", "ctx"), axis=0, tiled=True),
        lax.all_gather(w_query, ("fsdp", "ctx"), axis=0, tiled=True),
        lax.all_gather(w_key, ("fsdp", "ctx"), axis=0, tiled=True),
        lax.all_gather(w_value, ("fsdp", "ctx"), axis=0, tiled=True),
        lax.all_gather(w_out, ("fsdp", "ctx"), axis=1, tiled=True),
        lax.all_gather(ffn_gain, ("fsdp", "ctx"), axis=0, tiled=True),
        lax.all_gather(w_gate, ("fsdp", "ctx"), axis=0, tiled=True),
        lax.all_gather(w_up, ("fsdp", "ctx"), axis=0, tiled=True),
        lax.all_gather(w_down, ("fsdp", "ctx"), axis=1, tiled=True),
    )


def reduce_grads(main_part, pair_part):
    shares = (
        lax.psum_scatter(main_part[0], ("fsdp", "ctx"), scatter_dimension=0, tiled=True),
        lax.psum_scatter(main_part[1], ("fsdp", "ctx"), scatter_dimension=0, tiled=True),
        lax.psum_scatter(main_part[2], ("fsdp", "ctx"), scatter_dimension=1, tiled=True),
        lax.psum_scatter(main_part[3], ("fsdp", "ctx"), scatter_dimension=0, tiled=True),
        lax.psum_scatter(main_part[4], ("fsdp", "ctx"), scatter_dimension=0, tiled=True),
        lax.psum_scatter(main_part[5], ("fsdp", "ctx"), scatter_dimension=0, tiled=True),
        lax.psum_scatter(main_part[6], ("fsdp", "ctx"), scatter_dimension=1, tiled=True),
    )
    pairs = (
        lax.psum_scatter(pair_part[0], ("fsdp", "ctx", "tp"), scatter_dimension=0, tiled=True),
        lax.psum_scatter(pair_part[1], ("fsdp", "ctx", "tp"), scatter_dimension=0, tiled=True),
    )
    return (shares, pairs)


def block_allowed(segment_rows, places_rows, segment_all, block_at, key_block):
    segment_keys = lax.dynamic_slice_in_dim(segment_all, block_at * key_block, key_block)
    place_keys = block_at * key_block + jnp.arange(key_block, dtype=jnp.int32)
    return (segment_rows[:, None] == segment_keys[None, :]) & (
        place_keys[None, :] <= places_rows[:, None]
    )


def sweep(visit, initial, block_count, useful):

    def advance(block_at, state):
        return lax.cond(
            useful(block_at),
            lambda current: visit(block_at, current),
            lambda current: current,
            state,
        )

    return lax.fori_loop(0, block_count, advance, initial)


def shards(
    tokens,
    lengths,
    attn_gain,
    w_query,
    w_key,
    w_value,
    w_out,
    ffn_gain,
    w_gate,
    w_up,
    w_down,
    cotangent,
):
    f32 = jnp.float32
    b16 = jnp.bfloat16
    micro_count = tokens.shape[0]
    tok_rows = tokens.shape[1]
    model_width = tokens.shape[2]
    ctx_count = lax.axis_size("ctx")
    tp_count = lax.axis_size("tp")
    ctx_at = lax.axis_index("ctx")
    tp_at = lax.axis_index("tp")
    total_rows = tok_rows * ctx_count
    half_rows = tok_rows // tp_count
    local_heads = w_query.shape[1] // HD
    kv_width = KV * HD
    scaling = 1.0 / math.sqrt(HD)
    key_block = min(512, total_rows)
    block_count = total_rows // key_block
    heads_global = tp_at * local_heads + jnp.arange(local_heads, dtype=jnp.int32)
    select = heads_global[:, None] // (H // KV) == jnp.arange(KV, dtype=jnp.int32)[None, :]
    select_low = select.astype(b16)
    select_high = select.astype(f32)
    row_offset = tp_at * half_rows
    start_row = ctx_at * tok_rows
    places_mine = start_row + jnp.arange(tok_rows, dtype=jnp.int32)
    outputs_list = []
    input_list = []
    main_total = None
    pair_total = None
    for micro_at in range(micro_count):
        gathered = collect(
            attn_gain, w_query, w_key, w_value, w_out, ffn_gain, w_gate, w_up, w_down
        )
        (
            gain_first,
            query_full,
            key_full,
            value_full,
            out_full,
            gain_second,
            gate_full,
            up_full,
            down_full,
        ) = gathered
        inputs = tokens[micro_at].astype(f32)
        segment_all, position_all, live_all = layout(lengths[0, micro_at], total_rows)
        segment_mine = lax.dynamic_slice_in_dim(segment_all, start_row, tok_rows)
        position_mine = lax.dynamic_slice_in_dim(position_all, start_row, tok_rows)
        live_mine = lax.dynamic_slice_in_dim(live_all, start_row, tok_rows)
        cos_table, sin_table = rotary(position_mine, HD)
        rms_first = lax.rsqrt(jnp.mean(inputs * inputs, axis=-1, keepdims=True) + EPSILON)
        normed_first = (inputs * rms_first * gain_first.astype(f32)).astype(b16)
        queries = jnp.dot(normed_first, query_full, preferred_element_type=f32).reshape(
            tok_rows, local_heads, HD
        )
        queries = turn(queries, cos_table, sin_table).astype(b16)
        key_lin = jnp.dot(normed_first, key_full, preferred_element_type=f32).reshape(
            tok_rows, KV, HD
        )
        key_rot = turn(key_lin, cos_table, sin_table).astype(b16).reshape(tok_rows, kv_width)
        value_rot = jnp.dot(normed_first, value_full, preferred_element_type=f32).astype(b16)
        keys_all, values_all = (
            lax.all_gather(key_rot, "ctx", axis=0, tiled=True),
            lax.all_gather(value_rot, "ctx", axis=0, tiled=True),
        )
        keys_local = jnp.einsum(
            "tjd,hj->thd",
            keys_all.reshape(total_rows, KV, HD),
            select_low,
            preferred_element_type=f32,
        ).astype(b16)
        values_local = jnp.einsum(
            "tjd,hj->thd",
            values_all.reshape(total_rows, KV, HD),
            select_low,
            preferred_element_type=f32,
        ).astype(b16)

        def useful(block_at):
            return jnp.any(
                block_allowed(segment_mine, places_mine, segment_all, block_at, key_block)
            )

        def logits_of(block_at):
            key_rows = lax.dynamic_slice_in_dim(keys_local, block_at * key_block, key_block)
            raw_scores = (
                jnp.einsum("qhd,khd->hqk", queries, key_rows, preferred_element_type=f32) * scaling
            )
            allowed = block_allowed(segment_mine, places_mine, segment_all, block_at, key_block)
            return jnp.where(allowed[None], raw_scores, MASKED)

        def statistic(block_at, state):
            top_score, mass_sum = state
            logits = logits_of(block_at)
            new_top = jnp.maximum(top_score, jnp.max(logits, axis=-1))
            mass_sum = mass_sum * jnp.exp(top_score - new_top) + jnp.sum(
                jnp.exp(logits - new_top[..., None]), axis=-1
            )
            return (new_top, mass_sum)

        start_state = (
            jnp.full((local_heads, tok_rows), MASKED, f32),
            jnp.zeros((local_heads, tok_rows), f32),
        )
        top_score, mass_sum = sweep(statistic, start_state, block_count, useful)

        def probable(block_at):
            return jnp.exp(logits_of(block_at) - top_score[..., None]) / mass_sum[..., None]

        def accumulate(block_at, running):
            probs_low = probable(block_at).astype(b16)
            value_rows = lax.dynamic_slice_in_dim(values_local, block_at * key_block, key_block)
            return running + jnp.einsum(
                "hqk,khd->qhd", probs_low, value_rows, preferred_element_type=f32
            )

        attended = sweep(
            accumulate, jnp.zeros((tok_rows, local_heads, HD), f32), block_count, useful
        )
        attended_low = attended.reshape(tok_rows, local_heads * HD).astype(b16)
        branch = lax.psum(
            jnp.dot(attended_low, out_full, preferred_element_type=f32).astype(jnp.bfloat16), "tp"
        ).astype(jnp.float32)
        hidden = inputs + branch
        rms_second = lax.rsqrt(jnp.mean(hidden * hidden, axis=-1, keepdims=True) + EPSILON)
        normed_second = (hidden * rms_second * gain_second.astype(f32)).astype(b16)
        gate_pre = jnp.dot(normed_second, gate_full, preferred_element_type=f32)
        upward = jnp.dot(normed_second, up_full, preferred_element_type=f32)
        sigmoid_gate = jax.nn.sigmoid(gate_pre)
        silu_gate = jax.nn.silu(gate_pre)
        active = (silu_gate * upward).astype(b16)
        mixed = lax.psum(
            jnp.dot(active, down_full, preferred_element_type=f32).astype(jnp.bfloat16), "tp"
        ).astype(jnp.float32)
        outputs_list.append((hidden + mixed).astype(b16))
        gathered = collect_again(
            attn_gain, w_query, w_key, w_value, w_out, ffn_gain, w_gate, w_up, w_down
        )
        (
            gain_first,
            query_full,
            key_full,
            value_full,
            out_full,
            gain_second,
            gate_full,
            up_full,
            down_full,
        ) = gathered
        grad_rows = cotangent[micro_at].astype(f32) * live_mine[:, None].astype(f32)
        grad_low = grad_rows.astype(b16)
        grad_down = jnp.einsum("tf,td->fd", active, grad_low, preferred_element_type=f32)
        grad_active = jnp.einsum("td,fd->tf", grad_low, down_full, preferred_element_type=f32)
        grad_gate_pre = (
            grad_active * upward * sigmoid_gate * (1.0 + gate_pre * (1.0 - sigmoid_gate))
        ).astype(b16)
        grad_upward = (grad_active * silu_gate).astype(b16)
        grad_gate = jnp.einsum(
            "te,tf->ef", normed_second, grad_gate_pre, preferred_element_type=f32
        )
        grad_up = jnp.einsum("te,tf->ef", normed_second, grad_upward, preferred_element_type=f32)
        grad_normed_second = jnp.einsum(
            "tf,ef->te", grad_gate_pre, gate_full, preferred_element_type=f32
        ) + jnp.einsum("tf,ef->te", grad_upward, up_full, preferred_element_type=f32)
        grad_normed_second = lax.psum(grad_normed_second.astype(jnp.bfloat16), "tp").astype(
            jnp.float32
        )
        grad_gain_second = jnp.sum(grad_normed_second * hidden * rms_second, axis=0)
        grad_hidden = grad_rows + norm_back(
            hidden, rms_second, gain_second.astype(f32), grad_normed_second
        )
        grad_branch = grad_hidden.astype(b16)
        grad_out = jnp.einsum("te,td->ed", attended_low, grad_branch, preferred_element_type=f32)
        grad_att = (
            jnp.einsum("td,ed->te", grad_branch, out_full, preferred_element_type=f32)
            .astype(b16)
            .reshape(tok_rows, local_heads, HD)
        )
        delta_rows = jnp.sum(grad_att.astype(f32) * attended, axis=-1).T

        def backward_visit(block_at, state):
            grad_queries, grad_keys, grad_values = state
            first_row = block_at * key_block
            key_rows = lax.dynamic_slice_in_dim(keys_local, first_row, key_block)
            value_rows = lax.dynamic_slice_in_dim(values_local, first_row, key_block)
            probs = probable(block_at)
            probs_low = probs.astype(b16)
            grad_probs = jnp.einsum(
                "qhd,khd->hqk", grad_att, value_rows, preferred_element_type=f32
            )
            grad_logits = (probs * (grad_probs - delta_rows[..., None])).astype(b16)
            grad_queries = (
                grad_queries
                + jnp.einsum("hqk,khd->qhd", grad_logits, key_rows, preferred_element_type=f32)
                * scaling
            )
            key_part = (
                jnp.einsum("hqk,qhd->khd", grad_logits, queries, preferred_element_type=f32)
                * scaling
            )
            value_part = jnp.einsum("hqk,qhd->khd", probs_low, grad_att, preferred_element_type=f32)
            grad_keys = lax.dynamic_update_slice_in_dim(grad_keys, key_part, first_row, 0)
            grad_values = lax.dynamic_update_slice_in_dim(grad_values, value_part, first_row, 0)
            return (grad_queries, grad_keys, grad_values)

        back_state = (
            jnp.zeros((tok_rows, local_heads, HD), f32),
            jnp.zeros((total_rows, local_heads, HD), f32),
            jnp.zeros((total_rows, local_heads, HD), f32),
        )
        grad_queries, grad_keys, grad_values = sweep(
            backward_visit, back_state, block_count, useful
        )
        key_heads = jnp.einsum(
            "thd,hj->tjd", grad_keys, select_high, precision=lax.Precision.HIGHEST
        ).reshape(total_rows, kv_width)
        value_heads = jnp.einsum(
            "thd,hj->tjd", grad_values, select_high, precision=lax.Precision.HIGHEST
        ).reshape(total_rows, kv_width)
        key_sum, value_sum = (
            lax.psum_scatter(
                key_heads.astype(jnp.bfloat16), ("ctx", "tp"), scatter_dimension=0, tiled=True
            ).astype(jnp.float32),
            lax.psum_scatter(
                value_heads.astype(jnp.bfloat16), ("ctx", "tp"), scatter_dimension=0, tiled=True
            ).astype(jnp.float32),
        )
        cos_half = lax.dynamic_slice_in_dim(cos_table, row_offset, half_rows)
        sin_half = lax.dynamic_slice_in_dim(sin_table, row_offset, half_rows)
        grad_key_lin = (
            turn_back(key_sum.reshape(half_rows, KV, HD), cos_half, sin_half)
            .astype(b16)
            .reshape(half_rows, kv_width)
        )
        grad_value_lin = value_sum.astype(b16)
        normed_half = lax.dynamic_slice_in_dim(normed_first, row_offset, half_rows)
        grad_key = jnp.einsum("te,tk->ek", normed_half, grad_key_lin, preferred_element_type=f32)
        grad_value = jnp.einsum(
            "te,tk->ek", normed_half, grad_value_lin, preferred_element_type=f32
        )
        grad_normed_pair = jnp.einsum(
            "tk,ek->te", grad_key_lin, key_full, preferred_element_type=f32
        ) + jnp.einsum("tk,ek->te", grad_value_lin, value_full, preferred_element_type=f32)
        grad_query_lin = (
            turn_back(grad_queries, cos_table, sin_table)
            .astype(b16)
            .reshape(tok_rows, local_heads * HD)
        )
        grad_query = jnp.einsum(
            "te,tq->eq", normed_first, grad_query_lin, preferred_element_type=f32
        )
        grad_normed_first = jnp.einsum(
            "tq,eq->te", grad_query_lin, query_full, preferred_element_type=f32
        )
        grad_normed_first = grad_normed_first + lax.dynamic_update_slice_in_dim(
            jnp.zeros((tok_rows, model_width), f32), grad_normed_pair, row_offset, 0
        )
        grad_normed_first = lax.psum(grad_normed_first.astype(jnp.bfloat16), "tp").astype(
            jnp.float32
        )
        grad_gain_first = jnp.sum(grad_normed_first * inputs * rms_first, axis=0)
        input_list.append(
            grad_hidden + norm_back(inputs, rms_first, gain_first.astype(f32), grad_normed_first)
        )
        main_part = (
            grad_gain_first,
            grad_query,
            grad_out,
            grad_gain_second,
            grad_gate,
            grad_up,
            grad_down,
        )
        pair_part = (grad_key, grad_value)
        main_part, pair_part = reduce_grads(main_part, pair_part)
        if main_total is None:
            main_total = main_part
            pair_total = pair_part
        else:
            main_total = jax.tree.map(jnp.add, main_total, main_part)
            pair_total = jax.tree.map(jnp.add, pair_total, pair_part)
    return (
        jnp.stack(outputs_list),
        jnp.stack(input_list),
        main_total[0],
        main_total[1],
        pair_total[0],
        pair_total[1],
        main_total[2],
        main_total[3],
        main_total[4],
        main_total[5],
        main_total[6],
    )


F32 = jnp.float32
B16 = jnp.bfloat16
HD = 64
EPSILON = 1e-05
THETA = 10000.0
MASKED = -1e30
SCALE = 1.0 / math.sqrt(HD)
VMEM = pltpu.VMEM

def nn(a, b): return lax.dot_general(a, b, (((1,), (0,)), ((), ())), preferred_element_type=F32)
def nt(a, b): return lax.dot_general(a, b, (((1,), (1,)), ((), ())), preferred_element_type=F32)
def tn(a, b): return lax.dot_general(a, b, (((0,), (0,)), ((), ())), preferred_element_type=F32)

def lanes(shape): return lax.broadcasted_iota(jnp.int32, shape, len(shape) - 1)

def rope(t, cos, sin):
    low = lanes(t.shape) % 64 < 32
    rot = jnp.where(low, -pltpu.roll(t, 96, 1), pltpu.roll(t, 32, 1))
    return t * cos + rot * sin

def rope_back(u, cos, sin):
    low = lanes(u.shape) % 64 < 32
    us = u * sin
    return u * cos + jnp.where(low, pltpu.roll(us, 96, 1), -pltpu.roll(us, 32, 1))

def rms(v): return lax.rsqrt(jnp.mean(v * v, axis=-1, keepdims=True) + EPSILON)

def norm_back(v, r, gain, d):
    s = gain * d
    return r * s - v * (r * r * r) * jnp.mean(s * v, axis=-1, keepdims=True)

def doubled(tile, which):
    t = tile.astype(F32)
    r = pltpu.roll(t, 64, 1)
    low = lanes(t.shape) < 64
    return (jnp.where(low, t, r) if which == 0 else jnp.where(low, r, t)).astype(B16)

def window_start(t, nblk): return jnp.maximum(t - nblk + 1, 0)

def window(kvall_ref, w0, nblk, m, rows, tile):
    return jnp.concatenate([kvall_ref[w0 + b, m * rows:(m + 1) * rows, 128 * tile:128 * (tile + 1)] for b in range(nblk)], axis=0)

def heads_kv(kvall_ref, w0, nblk, m, rows):
    k01 = window(kvall_ref, w0, nblk, m, rows, 0)
    k2v2 = window(kvall_ref, w0, nblk, m, rows, 1)
    v01 = window(kvall_ref, w0, nblk, m, rows, 2)
    ks = [doubled(k01, 0), doubled(k01, 1), doubled(k2v2, 0)]
    vs = [doubled(v01, 0), doubled(v01, 1), doubled(k2v2, 1)]
    return ks, vs

def pick(group, p, tp):
    a, b = p // 2, (p + 1) // 2
    return group[a] if a == b else jnp.where(tp == 0, group[a], group[b])

def stacked(head):
    low = lanes(head.shape) < 64
    zero = jnp.zeros_like(head)
    return jnp.concatenate([jnp.where(low, head, zero), jnp.where(low, zero, head)], axis=0)

def allowed_of(begin, row0, key0, rows, keys):
    i = row0 + lax.broadcasted_iota(jnp.int32, (rows, keys), 0)
    j = key0 + lax.broadcasted_iota(jnp.int32, (rows, keys), 1)
    return (j <= i) & (j >= begin)

MESHT = pl.DeviceIdType.MESH

def n_slots(nf, nz):
    return 3 + (nf - 1) + 2 * (nz - 1) * (2 + nf - 1) + (nf - 1) * nz

def swap_body(src_ref, dst_ref, ssem, rsem):
    other = dict(tp=1 - lax.axis_index("tp"))
    barrier = pltpu.get_barrier_semaphore()
    pl.semaphore_signal(barrier, inc=1, device_id=other, device_id_type=MESHT)
    pl.semaphore_wait(barrier, 1)
    cp = pltpu.make_async_remote_copy(src_ref=src_ref, dst_ref=dst_ref, send_sem=ssem, recv_sem=rsem, device_id=other, device_id_type=MESHT)
    cp.start()
    cp.wait()

def swap(v, cid):
    return pl.pallas_call(
        swap_body, out_shape=jax.ShapeDtypeStruct(v.shape, v.dtype),
        in_specs=[pl.BlockSpec(memory_space=VMEM)], out_specs=pl.BlockSpec(memory_space=VMEM),
        scratch_shapes=[pltpu.SemaphoreType.DMA, pltpu.SemaphoreType.DMA],
        compiler_params=pltpu.CompilerParams(collective_id=cid, has_side_effects=True),
        name="tp_swap_%d" % v.shape[0],
    )(v)

def greet(t, z, c, nz, y, nf, all_z):
    barrier = pltpu.get_barrier_semaphore()
    def sig(**dev):
        pl.semaphore_signal(barrier, inc=1, device_id=dev, device_id_type=MESHT)
    sig(ctx=t + 1 - 2 * c)
    sig(tp=1 - lax.axis_index("tp"))
    for p in range(1, nf): sig(fsdp=lax.rem(y + p, nf))
    if all_z:
        for p in range(1, nz): sig(ctx=lax.rem(z + p, nz) * 2 + c)
        pl.semaphore_wait(barrier, nf + nz)
        return
    @pl.when(z > 0)
    def _(): sig(ctx=t - 2)
    @pl.when(z < nz - 1)
    def _(): sig(ctx=t + 2)
    @pl.when((z > 0) & (z < nz - 1))
    def _(): pl.semaphore_wait(barrier, 3 + nf)
    @pl.when((z == 0) | (z == nz - 1))
    def _(): pl.semaphore_wait(barrier, 2 + nf)

class Gather:
    y_first = ()
    def __init__(self, nf, nz, at, own_src, send_sem, recv_sem):
        self.nf, self.nz, self.at, self.own_src, self.ss, self.rs = nf, nz, at, own_src, send_sem, recv_sem
        self.y = lax.axis_index("fsdp") if nf > 1 else 0
        self.t = lax.axis_index("ctx")
        self.z, self.c = self.t // 2, lax.rem(self.t, 2)
        self.sib = dict(ctx=self.t + 1 - 2 * self.c)
        self.me = self.shard(self.y, self.z, self.c)
        count = [0]
        def new(n=1):
            count[0] += n
            return count[0] - n
        self.ownL, self.ownR, self.ownC, self.ownY = new(), new(), new(), new(nf - 1)
        self.zs = {(side, d): (new(), new(), new(nf - 1)) for d in range(1, nz) for side in (0, 1)}
        self.yc = {(p, zz): new() for p in range(1, nf) for zz in range(nz)}

    def shard(self, yy, zz, cc): return yy * self.nz * 2 + zz * 2 + cc
    def ydev(self, p): return dict(fsdp=lax.rem(self.y + p, self.nf))
    def copy(self, k, s, slot, dev, src=None):
        return pltpu.make_async_remote_copy(src_ref=self.at(k, s) if src is None else src, dst_ref=self.at(k, s),
            send_sem=self.ss.at[k, slot], recv_sem=self.rs.at[k, s], device_id=dev, device_id_type=MESHT)
    def send(self, *a): self.copy(*a).start()
    def got(self, k, s): self.copy(k, s, 0, self.sib).wait_recv()
    def sent(self, k, slot): self.copy(k, self.me, slot, self.sib).wait_send()
    def when_z(self, side, d):
        z, nz = self.z, self.nz
        return ((z >= d), (z < nz - 1), z - d, self.t + 2) if side == 0 else ((z + d <= nz - 1), (z > 0), z + d, self.t - 2)

    def own(self, k):
        src = self.own_src(k)
        if k not in self.y_first: self.own_y(k)
        @pl.when(self.z > 0)
        def _(): self.send(k, self.me, self.ownL, dict(ctx=self.t - 2), src)
        @pl.when(self.z < self.nz - 1)
        def _(): self.send(k, self.me, self.ownR, dict(ctx=self.t + 2), src)
        self.send(k, self.me, self.ownC, self.sib, src)

    def own_y(self, k):
        for p in range(1, self.nf): self.send(k, self.me, self.ownY + p - 1, self.ydev(p), self.own_src(k))

    def zstep(self, k, d, side):
        ok, more, zz, far = self.when_z(side, d)
        s = self.shard(self.y, zz, self.c)
        sf, sc, sy = self.zs[(side, d)]
        @pl.when(ok)
        def _():
            self.got(k, s)
            if d < self.nz - 1:
                @pl.when(more)
                def _(): self.send(k, s, sf, dict(ctx=far))
            for p in range(1, self.nf): self.send(k, s, sy + p - 1, self.ydev(p))
            self.send(k, s, sc, self.sib)

    def ystep(self, k, p, zz):
        s = self.shard(lax.rem(self.y + self.nf - p, self.nf), zz, self.c)
        self.got(k, s)
        self.send(k, s, self.yc[(p, zz)], self.sib)

    def to_z(self, k, s, slot):
        @pl.when(self.z > 0)
        def _(): self.send(k, s, slot, dict(ctx=self.t - 2))
        @pl.when(self.z < self.nz - 1)
        def _(): self.send(k, s, slot + 1, dict(ctx=self.t + 2))
    def peer_slot(self, p): return 2 + self.nf + 3 * (p - 1)
    def far_slot(self, p, d, side): return 2 + self.nf + 3 * (self.nf - 1) + 2 * ((p * (self.nz - 1) + d - 1) * 2 + side)
    def peer(self, p): return lax.rem(self.y + p, self.nf)
    def first_y(self, k):
        for p in range(1, self.nf):
            s = self.shard(self.peer(p), self.z, self.c)
            self.got(k, s)
            self.to_z(k, s, self.peer_slot(p))
            self.send(k, s, self.peer_slot(p) + 2, self.sib)
    def then_z(self, k, d):
        for side in (0, 1):
            ok, more, zz, far = self.when_z(side, d)
            @pl.when(ok)
            def _():
                for p in range(self.nf):
                    s = self.shard(self.peer(p), zz, self.c)
                    f = self.far_slot(p, d, side)
                    self.got(k, s)
                    if d < self.nz - 1:
                        @pl.when(more)
                        def _(): self.send(k, s, f, dict(ctx=far))
                    self.send(k, s, f + 1, self.sib)
    def YZ(self, k): return [functools.partial(self.first_y, k)] + [functools.partial(self.then_z, k, d) for d in range(1, self.nz)]
    def drain_yz(self, k):
        for p in range(1, self.nf): self.sent(k, self.ownY + p - 1)
        self.sent(k, self.ownC)
        for p in range(1, self.nf): self.sent(k, self.peer_slot(p) + 2)
        for edge, own, i in ((self.z > 0, self.ownL, 0), (self.z < self.nz - 1, self.ownR, 1)):
            @pl.when(edge)
            def _():
                self.sent(k, own)
                for p in range(1, self.nf): self.sent(k, self.peer_slot(p) + i)
        for d in range(1, self.nz):
            for side in (0, 1):
                ok, more, _zz, _far = self.when_z(side, d)
                @pl.when(ok)
                def _():
                    for p in range(self.nf):
                        if d < self.nz - 1:
                            @pl.when(more)
                            def _(): self.sent(k, self.far_slot(p, d, side))
                        self.sent(k, self.far_slot(p, d, side) + 1)

    def Z(self, k): return [functools.partial(self.zstep, k, d, side) for d in range(1, self.nz) for side in (0, 1)]
    def hop(self, k, d):
        if k in self.y_first:
            if d == 1: self.first_y(k)
            self.then_z(k, d)
        else:
            for side in (0, 1): self.zstep(k, d, side)
    def last(self, k):
        if k not in self.y_first: emit(self.Y(k))
    def Y(self, k): return [functools.partial(self.ystep, k, p, zz) for p in range(1, self.nf) for zz in range(self.nz)]

    def arrived(self, k):
        for yy in range(self.nf):
            for zz in range(self.nz):
                self.got(k, self.shard(yy, zz, 1 - self.c))

    def drain(self, k):
        for p in range(1, self.nf): self.sent(k, self.ownY + p - 1)
        @pl.when(self.z > 0)
        def _(): self.sent(k, self.ownL)
        @pl.when(self.z < self.nz - 1)
        def _(): self.sent(k, self.ownR)
        self.sent(k, self.ownC)
        for d in range(1, self.nz):
            for side in (0, 1):
                ok, more, _zz, _far = self.when_z(side, d)
                sf, sc, sy = self.zs[(side, d)]
                @pl.when(ok)
                def _():
                    if d < self.nz - 1:
                        @pl.when(more)
                        def _(): self.sent(k, sf)
                    for p in range(1, self.nf): self.sent(k, sy + p - 1)
                    self.sent(k, sc)
        for v in self.yc.values(): self.sent(k, v)

def emit(*lists):
    for steps in lists:
        for step in steps: step()

class KeysGather(Gather):
    far = 2
    def own(self):
        @pl.when(self.z < self.nz - 1)
        def _(): self.send(0, self.me, self.ownR, dict(ctx=self.t + 2))
        self.send(0, self.me, self.ownC, self.sib)
    def step(self, d):
        s = self.shard(0, self.z - d, self.c)
        sf, sc, _y = self.zs[(0, d)]
        @pl.when(self.z >= d)
        def _():
            self.got(0, s)
            if d < self.far:
                @pl.when(self.z < self.nz - 1)
                def _(): self.send(0, s, sf, dict(ctx=self.t + 2))
            self.send(0, s, sc, self.sib)
    def arrived(self):
        for d in range(self.far + 1):
            @pl.when(self.z >= d)
            def _(): self.got(0, self.shard(0, self.z - d, 1 - self.c))
    def drain(self):
        @pl.when(self.z < self.nz - 1)
        def _(): self.sent(0, self.ownR)
        self.sent(0, self.ownC)
        for d in range(1, self.far + 1):
            sf, sc, _y = self.zs[(0, d)]
            @pl.when(self.z >= d)
            def _():
                if d < self.far:
                    @pl.when(self.z < self.nz - 1)
                    def _(): self.sent(0, sf)
                self.sent(0, sc)

def kv_tile(tp, wk, wv):
    n = wk.shape[1]
    i, l = lax.broadcasted_iota(jnp.int32, (n, 384), 0), lax.broadcasted_iota(jnp.int32, (n, 384), 1)
    first = tp * 2 * HD
    ek = (i == first + l) & (l < 3 * HD)
    ev = ((i == first + l - 4 * HD) & (l >= 4 * HD)) | ((i == first + l - HD) & (l >= 3 * HD) & (l < 4 * HD))
    return nn(wk, ek.astype(F32).astype(B16)) + nn(wv, ev.astype(F32).astype(B16))

def half_rows(first, second):
    return jnp.where(lax.broadcasted_iota(jnp.int32, (8, first.shape[1]), 0) < 4, first, second)

def half_select():
    low = lanes((8, 128)) < 64
    r = lax.broadcasted_iota(jnp.int32, (8, 128), 0)
    return ((low & (r == 0)) | ((lanes((8, 128)) >= 64) & (r == 4))).astype(F32).astype(B16)

def front(nf, nz, micros, rows, nblk, chunks, shard,
          x_hbm, ct_hbm, len_ref, g1_ref, g2_ref, wq, wk, wv, so, sg, su, sd,
          A_hbm, O_hbm, kvall_hbm, n1_hbm, q_hbm, ao_hbm, pr_hbm, gains_hbm, cos_hbm, sin_hbm, g_hbm, hid_hbm, part2_hbm, dpart_hbm, gd_hbm, n2T_hbm, dgate_hbm, dup_hbm,
          A, O, kvall_ref, n1_ref, q_ref, ao_ref, pr_ref, gains_ref, cos_ref, sin_ref, g_ref, hid_ref, part2_ref, dpart_ref, gT, n2T, G, U, D, gd, dgate_ref, dup_ref, part_ref, peer_ref, gate_ref, up_ref, act_ref, n2_ref, psum_ref, dsum_ref, begin_ref, skv, x_ref, ct_ref, xsem, wss, wrs, lsem, kss, krs, pss, prs, osem):
    t = lax.axis_index("ctx"); tp = lax.axis_index("tp")
    y = lax.axis_index("fsdp") if nf > 1 else 0
    z, c = t // 2, lax.rem(t, 2)
    qw = q_ref.shape[1]
    first = [pltpu.make_async_copy(a, b, xsem.at[i]) for i, (a, b) in enumerate(((ct_hbm, ct_ref), (x_hbm, x_ref)))]
    for cp in first: cp.start()
    greet(t, z, c, nz, y, nf, False)
    shards, outs = [None, so, sg, su, sd], [A, O, G, U, D]
    def at(k, s):
        m, c0, cn = chunks[k]
        return outs[m].at[pl.ds(pl.multiple_of(s * shard, 16), shard), pl.ds(c0, cn)]
    def own_src(k):
        m, c0, cn = chunks[k]
        return (wq, skv)[k] if m == 0 else shards[m].at[:, pl.ds(c0, cn)]
    W = Gather(nf, nz, at, own_src, wss, wrs)
    W.y_first = (8,)
    V = KeysGather(1, nz, lambda k, s: kvall_ref.at[s], None, kss, krs)
    K = len(chunks)
    def local(k):
        return pltpu.make_async_copy(own_src(k), at(k, W.me), lsem.at[k])
    other = dict(tp=1 - tp)
    def swap_part(m):
        sl = pl.ds(m * rows, rows)
        return pltpu.make_async_remote_copy(src_ref=part_ref.at[sl, :], dst_ref=peer_ref.at[sl, :], send_sem=pss.at[m], recv_sem=prs.at[m], device_id=other, device_id_type=MESHT)
    saved = []
    def save(a, b):
        saved.append(pltpu.make_async_copy(a, b, osem.at[len(saved)]))
        saved[-1].start()
    W.own(0)
    skv[:, :384] = kv_tile(tp, wk[...], wv[...]).astype(B16)
    skv[:, 384:] = tn(half_rows(g1_ref[...].astype(F32), g2_ref[...].astype(F32)).astype(B16), half_select()).astype(B16)
    for b in range(2 * nz):
        @pl.when((b // 2 > z) | (b // 2 < z - V.far))
        def _(): kvall_ref[b] = jnp.zeros(kvall_ref.shape[1:], B16)
    W.own(1); W.own(2)
    for k in W.y_first: W.own_y(k)
    for k in range(K): local(k).start()
    for cp in first: cp.wait()
    place = t * rows + lax.broadcasted_iota(jnp.int32, (rows, 128), 0)
    inverse = jnp.exp((lanes((1, 128)) % (HD // 2)).astype(F32) * (-2.0 * math.log(THETA) / HD))
    for m in range(micros):
        sl = slice(m * rows, (m + 1) * rows)
        begin, end = jnp.zeros((rows, 128), jnp.int32), 0
        for i in range(len_ref.shape[1]):
            end = end + len_ref[m, i]
            begin = begin + jnp.where(place >= end, len_ref[m, i], 0)
        begin_ref[sl, :] = begin
        angle = (place - begin).astype(F32) * inverse
        cos_ref[sl, :] = jnp.cos(angle)
        sin_ref[sl, :] = jnp.sin(angle)
        live = jnp.where(place < end, 1.0, 0.0)
        g_ref[sl, :] = (ct_ref[sl, :].astype(F32) * live[:, :1]).astype(B16)
    x = x_ref[...].astype(F32)
    hid_ref[...] = x * rms(x)
    gT[...] = jnp.transpose(g_ref[...].astype(F32)).astype(B16)
    save(g_ref, g_hbm); save(cos_ref, cos_hbm); save(sin_ref, sin_hbm)
    hop, last = W.hop, W.last
    hop(0, 1); W.own(3); hop(1, 1); hop(0, 2); hop(2, 1); hop(1, 2); hop(0, 3); last(0); hop(2, 2); hop(1, 3); last(1)
    local(0).wait(); local(1).wait()
    W.arrived(0); W.arrived(1)
    save(A, A_hbm)
    sel = (lax.broadcasted_iota(jnp.int32, (8, 128), 1) == jnp.where(lax.broadcasted_iota(jnp.int32, (8, 128), 0) < 4, 0, 64)).astype(B16)
    gains = nt(sel, A[:, qw + 384:qw + 512])
    gains_ref[...] = gains
    save(gains_ref, gains_hbm)
    n1_ref[...] = (hid_ref[...] * gains[0:1, :]).astype(B16)
    cos, sin = cos_ref[...], sin_ref[...]
    lin = nn(n1_ref[...], A[:, qw:qw + 384])
    low = lanes((lin.shape[0], 128)) < 64
    mid = lin[:, 128:256]
    kvall_ref[t, :, 0:128] = rope(lin[:, :128], cos, sin).astype(B16)
    kvall_ref[t, :, 128:256] = jnp.where(low, rope(mid, cos, sin), mid).astype(B16)
    kvall_ref[t, :, 256:384] = lin[:, 256:384].astype(B16)
    hop(3, 1)
    V.own()
    save(n1_ref, n1_hbm)
    hop(2, 3)
    lin = nn(n1_ref[...], A[:, :qw])
    for i in range(qw // 128):
        q_ref[:, 128 * i:128 * (i + 1)] = rope(lin[:, 128 * i:128 * (i + 1)], cos, sin).astype(B16)
    save(q_ref, q_hbm)
    W.own(4); hop(3, 2); hop(4, 1); last(2)
    V.step(1)
    hop(3, 3); W.own(5); hop(4, 2); hop(5, 1); last(3)
    V.step(2)
    V.arrived()
    save(kvall_ref, kvall_hbm)
    local(2).wait()
    W.arrived(2)
    save(O, O_hbm)
    P_ = functools.partial
    pump = [P_(W.own, 6), P_(hop, 4, 3), P_(hop, 5, 2), P_(hop, 6, 1), P_(W.own, 7), P_(hop, 5, 3), P_(hop, 6, 2), P_(hop, 7, 1)]
    w0 = window_start(t, nblk)
    keys = nblk * rows
    pairs = qw // 128
    done = 0
    for m in range(micros):
        sl = slice(m * rows, (m + 1) * rows)
        ks, vs = heads_kv(kvall_ref, w0, nblk, m, rows)
        ok = allowed_of(begin_ref[sl, :1], t * rows, w0 * rows, rows, keys)
        for p in range(pairs):
            kb = stacked(pick(ks, p, tp)); vb = stacked(pick(vs, p, tp))
            s = nt(q_ref[sl, 128 * p:128 * (p + 1)], kb) * SCALE
            halves = []
            for h in range(2):
                sh = jnp.where(ok, s[:, h * keys:(h + 1) * keys], MASKED)
                e = jnp.exp(sh - jnp.max(sh, axis=-1, keepdims=True))
                halves.append((e / jnp.sum(e, axis=-1, keepdims=True)).astype(B16))
            pr = jnp.concatenate(halves, axis=1)
            pr_ref[m * pairs + p] = pr
            ao_ref[sl, 128 * p:128 * (p + 1)] = nn(pr, vb).astype(B16)
            upto = len(pump) * (m * pairs + p + 1) // (micros * pairs)
            emit(pump[done:upto])
            done = upto
        part_ref[sl, :] = nt(ao_ref[sl, :], O[...]).astype(B16)
        swap_part(m).start()
    save(ao_ref, ao_hbm); save(pr_ref, pr_hbm)
    W.own(8); last(4); hop(6, 3); hop(7, 2); hop(8, 1); last(5); W.own(9)
    W.arrived(3); W.arrived(4); W.arrived(5)
    for k in (3, 4, 5): local(k).wait()
    for m in range(micros): swap_part(m).wait_recv()
    hid = x_ref[...].astype(F32) + (part_ref[...].astype(F32) + peer_ref[...].astype(F32))
    hid_ref[...] = hid
    n2 = hid * rms(hid) * gains[4:5, :]
    n2_ref[...] = n2.astype(B16)
    n2T[...] = jnp.transpose(n2).astype(B16)
    save(hid_ref, hid_hbm)
    save(n2T, n2T_hbm)
    def forward(j, _):
        cols = pl.ds(pl.multiple_of(j * 256, 256), 256)
        gate = nn(n2_ref[...], G[:, cols])
        up = nn(n2_ref[...], U[:, cols])
        gate_ref[:, cols] = gate
        up_ref[:, cols] = up
        act = (gate * jax.nn.sigmoid(gate) * up).astype(B16)
        act_ref[:, cols] = act
        gd[:, cols] = nn(gT[...], act).astype(B16)
        return _
    def backward(j, _):
        cols = pl.ds(pl.multiple_of(j * 256, 256), 256)
        da = nn(g_ref[...], D[:, cols])
        gate = gate_ref[:, cols]; up = up_ref[:, cols]
        sg = jax.nn.sigmoid(gate)
        dgate = (da * up * sg * (1.0 + gate * (1.0 - sg))).astype(B16)
        dup = (da * (gate * sg)).astype(B16)
        dgate_ref[:, cols] = dgate
        dup_ref[:, cols] = dup
        dsum_ref[...] += nt(dgate, G[:, cols]) + nt(dup, U[:, cols])
        psum_ref[...] += nt(act_ref[:, cols], D[:, cols])
        return _
    def save_cols(a, b, c0, cn): save(a.at[:, pl.ds(c0, cn)], b.at[:, pl.ds(c0, cn)])
    tiles = [c // 256 for _m, _c0, c in chunks]
    ff = G.shape[1]
    dsum_ref[...] = jnp.zeros_like(dsum_ref)
    psum_ref[...] = jnp.zeros_like(psum_ref)
    lax.fori_loop(0, tiles[3], forward, 0)
    hop(7, 3); hop(8, 2); hop(9, 1); W.own(10); last(6)
    W.arrived(6); local(6).wait()
    lax.fori_loop(tiles[3], ff // 256, forward, 0)
    save(gd, gd_hbm)
    hop(8, 3); hop(9, 2); hop(10, 1)
    def back_tiles(k):
        last(k)
        W.arrived(k); local(k).wait()
        _m, c0, cn = chunks[k]
        lax.fori_loop(c0 // 256, (c0 + cn) // 256, backward, 0)
        save_cols(dgate_ref, dgate_hbm, c0, cn); save_cols(dup_ref, dup_hbm, c0, cn)
    order = (8, 7) if 8 in W.y_first else (7, 8)
    back_tiles(order[0])
    hop(9, 3); hop(10, 2)
    back_tiles(order[1])
    hop(10, 3)
    back_tiles(9); back_tiles(10)
    dpart_ref[...] = dsum_ref[...].astype(B16)
    save(dpart_ref, dpart_hbm)
    part2_ref[...] = psum_ref[...].astype(B16)
    save(part2_ref, part2_hbm)
    for m in range(micros): swap_part(m).wait_send()
    for k in range(K): (W.drain_yz if k in W.y_first else W.drain)(k)
    V.drain()
    for cp in saved: cp.wait()

def back(nf, nz, micros, rows, nblk, chunks, shard,
         gd, *refs):
    given, results, refs = refs[:18], refs[18:26], refs[26:]
    back_body(nf, nz, micros, rows, nblk, chunks, shard, gd, given, results, *refs)

def back_body(nf, nz, micros, rows, nblk, chunks, shard, gd, given,
         results,
         own_d, gg, gu, c_d, c_g, c_u, c_o, c_a, y_d, y_g, y_u, y_o, y_a, z_d, z_g, z_u, z_o, z_a,
         zx_ref, go_ref, ga_ref, do_ref, dq_ref, dkv_ref, kc_ref, kz_ref, dl_ref, dpeer_ref, peer2_ref, npeer_ref,
         g_ref, dpart_ref, part2_ref, hid_ref, gains_ref, q_ref, kvall_ref, O, A, ao_ref, pr_ref, n1_ref, cos_ref, sin_ref, x_ref, n2T, dgate_ref, dup_ref, gsem,
         rd, rg, ru, ro, ra, dx_ref, kvx_ref, osem,
         lsem, cs, cr, ys, yr, zs, zr, kcs, kcr, kzs, kzr, ss, sr):
    kz_ref[...] = jnp.zeros_like(kz_ref)
    dh_ref, npart_ref, out_ref = dx_ref, dpart_ref, part2_ref
    t = lax.axis_index("ctx"); tp = lax.axis_index("tp")
    y = lax.axis_index("fsdp") if nf > 1 else 0
    z, c = t // 2, lax.rem(t, 2)
    nb = nf * nz
    greet(t, z, c, nz, y, nf, True)
    ins, outs = [gd, gg, gu, go_ref, ga_ref], [rd, rg, ru, ro, ra]
    crecv, yrecv, zrecv = [c_d, c_g, c_u, c_o, c_a], [y_d, y_g, y_u, y_o, y_a], [z_d, z_g, z_u, z_o, z_a]
    acc = [own_d, c_g, c_u, c_o, c_a]
    sib, other = dict(ctx=t + 1 - 2 * c), dict(tp=1 - tp)
    inner = (z == 1) | (z == 2)
    zin, zed = jnp.where(z < 2, 1, 2), jnp.where(z < 2, 0, 3)
    zoi, zoe = 3 - zin, 3 - zed
    def remote(src, dst, s, r, dev):
        return pltpu.make_async_remote_copy(src_ref=src, dst_ref=dst, send_sem=s, recv_sem=r, device_id=dev, device_id_type=MESHT)
    def ccopy(k):
        m, c0, cn = chunks[k]
        return remote(ins[m].at[:, 1 - c, :, pl.ds(c0, cn)], crecv[m].at[:, :, pl.ds(c0, cn)], cs.at[k], cr.at[k], sib)
    def lcopy(k):
        m, c0, cn = chunks[k]
        return pltpu.make_async_copy(ins[m].at[:, c, :, pl.ds(c0, cn)], acc[m].at[:, :, pl.ds(c0, cn)], lsem.at[k])
    def ycopy(k, p):
        m, c0, cn = chunks[k]
        yy = lax.rem(y + p, nf)
        return remote(acc[m].at[pl.ds(yy * nz, nz), :, pl.ds(c0, cn)], yrecv[m].at[p - 1, :, :, pl.ds(c0, cn)], ys.at[k, p - 1], yr.at[k, p - 1], dict(fsdp=yy))
    def zcopy(k, block, i, slot):
        m, c0, cn = chunks[k]
        return lambda dest: remote(acc[m].at[y * nz + block, :, pl.ds(c0, cn)], zrecv[m].at[slot, :, pl.ds(c0, cn)], zs.at[k, i], zr.at[k, slot], dict(ctx=dest * 2 + c))
    def zgot(k, slot): zcopy(k, z, 0, slot)(zoi).wait_recv()
    def stage_core(k):
        m, c0, cn = chunks[k]
        cols = pl.ds(c0, cn)
        if m < 1: lcopy(k).wait()
        ccopy(k).wait_recv()
        def add(b, _):
            first = acc[m][b, :, cols] if m < 1 else ins[m][b, c, :, cols]
            acc[m][b, :, cols] = first + crecv[m][b, :, cols]
            return _
        lax.fori_loop(0, nb, add, 0)
        for p in range(1, nf): ycopy(k, p).start()
    def stage_y(k):
        m, c0, cn = chunks[k]
        cols = pl.ds(c0, cn)
        for p in range(1, nf): ycopy(k, p).wait_recv()
        def add(b, _):
            total = acc[m][y * nz + b, :, cols].astype(F32)
            for p in range(1, nf): total = total + yrecv[m][p - 1, b, :, cols].astype(F32)
            acc[m][y * nz + b, :, cols] = total.astype(B16)
            return _
        lax.fori_loop(0, nz, add, 0)
        @pl.when(inner)
        def _(): zcopy(k, zed, 0, 0)(zed).start()
        @pl.when(jnp.logical_not(inner))
        def _():
            zcopy(k, zoi, 0, 2)(zin).start()
            zcopy(k, zoe, 1, 3)(zin).start()
            zcopy(k, zin, 2, 0)(zin).start()
    def stage_m(k):
        m, c0, cn = chunks[k]
        cols = pl.ds(c0, cn)
        @pl.when(inner)
        def _():
            for block, slot in ((zoi, 2), (zoe, 3)):
                zgot(k, slot)
                acc[m][y * nz + block, :, cols] = (acc[m][y * nz + block, :, cols].astype(F32) + zrecv[m][slot, :, cols].astype(F32)).astype(B16)
                zcopy(k, block, slot - 1, 1)(block).start()
    def stage_z(k):
        m, c0, cn = chunks[k]
        cols = pl.ds(c0, cn)
        zgot(k, 0); zgot(k, 1)
        outs[m][:, cols] = acc[m][y * nz + z, :, cols].astype(F32) + zrecv[m][0, :, cols].astype(F32) + zrecv[m][1, :, cols].astype(F32)
    def xcopy(q, block, i, slot):
        m, c0, cn = chunks[0]
        dst = zx_ref.at[slot] if q else zrecv[m].at[slot, :, pl.ds(c0, cn)]
        return lambda dest: remote(acc[m].at[lax.rem(y + q, nf) * nz + block, :, pl.ds(c0, cn)], dst, zs.at[0, 3 * q + i], zr.at[0, 4 * q + slot], dict(ctx=dest * 2 + c))
    def xgot(q, slot): xcopy(q, z, 0, slot)(zoi).wait_recv()
    def xycopy():
        m, c0, cn = chunks[0]
        yy = lax.rem(y + 1, nf)
        return remote(acc[m].at[yy * nz + z, :, pl.ds(c0, cn)], yrecv[m].at[0, 0, :, pl.ds(c0, cn)], ys.at[0, 0], yr.at[0, 0], dict(fsdp=yy))
    def stage_xcore():
        m, c0, cn = chunks[0]
        cols = pl.ds(c0, cn)
        lcopy(0).wait()
        ccopy(0).wait_recv()
        def add(b, _):
            acc[m][b, :, cols] = acc[m][b, :, cols] + crecv[m][b, :, cols]
            return _
        lax.fori_loop(0, nb, add, 0)
        @pl.when(inner)
        def _():
            for q in (1, 0): xcopy(q, zed, 0, 0)(zed).start()
        @pl.when(jnp.logical_not(inner))
        def _():
            for q in (1, 0):
                xcopy(q, zoi, 0, 2)(zin).start()
                xcopy(q, zoe, 1, 3)(zin).start()
                xcopy(q, zin, 2, 0)(zin).start()
    def stage_xm():
        m, c0, cn = chunks[0]
        cols = pl.ds(c0, cn)
        @pl.when(inner)
        def _():
            for q in (1, 0):
                at = lax.rem(y + q, nf) * nz
                for block, slot in ((zoi, 2), (zoe, 3)):
                    xgot(q, slot)
                    got = zx_ref[slot] if q else zrecv[m][slot, :, cols]
                    acc[m][at + block, :, cols] = (acc[m][at + block, :, cols].astype(F32) + got.astype(F32)).astype(B16)
                    xcopy(q, block, slot - 1, 1)(block).start()
    def stage_xz():
        m, c0, cn = chunks[0]
        cols = pl.ds(c0, cn)
        xgot(1, 0); xgot(1, 1)
        at = lax.rem(y + 1, nf) * nz + z
        acc[m][at, :, cols] = (acc[m][at, :, cols].astype(F32) + zx_ref[0].astype(F32) + zx_ref[1].astype(F32)).astype(B16)
        xycopy().start()
    def stage_xy():
        m, c0, cn = chunks[0]
        cols = pl.ds(c0, cn)
        xgot(0, 0); xgot(0, 1)
        total = acc[m][y * nz + z, :, cols].astype(F32) + zrecv[m][0, :, cols].astype(F32) + zrecv[m][1, :, cols].astype(F32)
        xycopy().wait_recv()
        outs[m][:, cols] = total + yrecv[m][0, 0, :, cols].astype(F32)
    dswap = remote(given[1], dpeer_ref, ss.at[0], sr.at[0], other)
    oswap = remote(given[2], peer2_ref, ss.at[1], sr.at[1], other)
    nswap = remote(npart_ref, npeer_ref, ss.at[2], sr.at[2], other)
    K = len(chunks)
    held = (g_ref, dpart_ref, part2_ref, hid_ref, gains_ref, q_ref, kvall_ref, O, A, ao_ref, pr_ref, n1_ref, cos_ref, sin_ref, x_ref, n2T, dgate_ref, dup_ref)
    loads = [pltpu.make_async_copy(a, b, gsem.at[i]) for i, (a, b) in enumerate(zip(given, held))]
    def need(*which):
        for i in which: loads[i].wait()
    saves = [pltpu.make_async_copy(a, b, osem.at[i]) for i, (a, b) in enumerate(zip((rd, rg, ru, ro, ra, dx_ref, out_ref, kvx_ref), results))]
    dswap.start()
    for k in (1, 0, 2):
        ccopy(k).start(); lcopy(k).start()
    def weights(ref, d_ref):
        def tile(j, _):
            cols = pl.ds(pl.multiple_of(j * 256, 256), 256)
            v = nn(n2T[...], d_ref[:, cols]).astype(B16)
            for s in range(2 * nb): ref[s // 2, s % 2, :, cols] = v[s * shard:(s + 1) * shard]
            return _
        lax.fori_loop(0, d_ref.shape[1] // 256, tile, 0)
    stage_core(1)
    for i in (15, 16, 17): loads[i].start()
    stage_xcore()
    for i in (1, 3, 0, 4, 7, 9, 5, 6, 10, 2, 12, 13, 8, 11, 14): loads[i].start()
    need(15, 16)
    weights(gg, dgate_ref)
    stage_core(2)
    ccopy(3).start(); ccopy(4).start()
    dkv_ref[...] = jnp.zeros_like(dkv_ref)
    need(17)
    weights(gu, dup_ref)
    stage_core(3)
    for k in (5, 6, 7): ccopy(k).start()
    stage_y(1)
    dswap.wait_recv()
    need(0, 1, 3, 4, 7)
    oswap.start()
    dn2 = dpart_ref[...].astype(F32) + dpeer_ref[...].astype(F32)
    hid = hid_ref[...]
    r2 = rms(hid)
    gain2 = jnp.sum(dn2 * hid * r2, axis=0, keepdims=True)
    dh = g_ref[...].astype(F32) + norm_back(hid, r2, gains_ref[4:5, :], dn2)
    dh_ref[...] = dh
    db = dh.astype(B16)
    do_ref[...] = nn(db, O[...]).astype(B16)
    stage_y(2)
    need(9)
    go = tn(db, ao_ref[...]).astype(B16)
    for s in range(2 * nb): go_ref[s // 2, s % 2] = go[s * shard:(s + 1) * shard]
    ccopy(8).start()
    stage_core(4)
    stage_xm()
    need(5, 6, 10)
    w0 = window_start(t, nblk)
    keys = nblk * rows
    pairs = q_ref.shape[1] // 128
    low = lanes((keys, 128)) < 64
    for m in range(micros):
        sl = slice(m * rows, (m + 1) * rows)
        ks, vs = heads_kv(kvall_ref, w0, nblk, m, rows)
        dks = [jnp.zeros((keys, 128), F32) for _ in range(3)]
        dvs = [jnp.zeros((keys, 128), F32) for _ in range(3)]
        for p in range(pairs):
            kb = stacked(pick(ks, p, tp)); vb = stacked(pick(vs, p, tp))
            qt = q_ref[sl, 128 * p:128 * (p + 1)]
            dot_ = do_ref[sl, 128 * p:128 * (p + 1)]
            pr = pr_ref[m * pairs + p]
            dp = nt(dot_, vb)
            halves = []
            for h in range(2):
                ph = pr[:, h * keys:(h + 1) * keys].astype(F32)
                dph = dp[:, h * keys:(h + 1) * keys]
                delta = jnp.sum(ph * dph, axis=-1, keepdims=True)
                halves.append((ph * (dph - delta)).astype(B16))
            ds = jnp.concatenate(halves, axis=1)
            dq_ref[sl, 128 * p:128 * (p + 1)] = nn(ds, kb) * SCALE
            dkb = tn(ds, qt) * SCALE
            dvb = tn(pr, dot_)
            dk = jnp.where(low, dkb[:keys], dkb[keys:])
            dv = jnp.where(low, dvb[:keys], dvb[keys:])
            a, b = p // 2, (p + 1) // 2
            if a == b:
                dks[a] = dks[a] + dk; dvs[a] = dvs[a] + dv
            else:
                first = (tp == 0).astype(F32); second = 1.0 - first
                dks[a] = dks[a] + dk * first; dvs[a] = dvs[a] + dv * first
                dks[b] = dks[b] + dk * second; dvs[b] = dvs[b] + dv * second
        def full(v): return v + pltpu.roll(v, 64, 1)
        dk0, dk1, dk2 = [full(v) for v in dks]
        dv0, dv1, dv2 = [full(v) for v in dvs]
        tiles = [jnp.where(low, dk0, dk1), jnp.where(low, dk2, dv2), jnp.where(low, dv0, dv1)]
        for b in range(nblk):
            at = w0 + b
            for i in range(3):
                dkv_ref[at // 2, lax.rem(at, 2), m * rows:(m + 1) * rows, 128 * i:128 * (i + 1)] = tiles[i][b * rows:(b + 1) * rows].astype(B16)
        if m == 0: stage_m(1); stage_m(2); stage_z(1)
    kvc = remote(dkv_ref.at[:, 1 - c], kc_ref, kcs.at[0], kcr.at[0], sib)
    def kvz(p): return remote(kc_ref.at[z - p], kz_ref.at[p - 1], kzs.at[p - 1], kzr.at[p - 1], dict(ctx=t - 2 * p))
    def kv_each(act):
        for p in range(1, 3):
            @pl.when(z >= p)
            def _(): act(kvz(p))
    def kv_got():
        for p in range(1, 3):
            @pl.when(z + p < nz)
            def _(): remote(kc_ref.at[z], kz_ref.at[p - 1], kzs.at[p - 1], kzr.at[p - 1], sib).wait_recv()
    kvc.start()
    stage_y(3); stage_xz(); stage_core(5)
    kvc.wait_recv()
    def add_kv(b, _):
        kc_ref[b] = kc_ref[b] + dkv_ref[b, c]
        return _
    lax.fori_loop(0, nz, add_kv, 0)
    kv_each(lambda cp: cp.start())
    stage_z(2); stage_m(3); stage_y(4); stage_xy(); saves[0].start()
    stage_z(3); stage_core(6)
    kv_got()
    dkv = kc_ref[z].astype(F32) + kz_ref[0].astype(F32) + kz_ref[1].astype(F32)
    need(8, 11, 12, 13)
    cos, sin = cos_ref[...], sin_ref[...]
    qw = q_ref.shape[1]
    for i in range(qw // 128):
        dl_ref[:, 128 * i:128 * (i + 1)] = rope_back(dq_ref[:, 128 * i:128 * (i + 1)], cos, sin).astype(B16)
    mid = dkv[:, 128:256]
    dl_ref[:, qw:qw + 128] = rope_back(dkv[:, :128], cos, sin).astype(B16)
    dl_ref[:, qw + 128:qw + 256] = jnp.where(lanes(mid.shape) < 64, rope_back(mid, cos, sin), mid).astype(B16)
    dl_ref[:, qw + 256:qw + 384] = dkv[:, 256:384].astype(B16)
    npart_ref[...] = nt(dl_ref[...], A[:, :qw + 384]).astype(B16)
    nswap.start()
    stage_core(8)
    ga = tn(n1_ref[...], dl_ref[...]).astype(B16)
    for s in range(2 * nb): ga_ref[s // 2, s % 2, :, :qw + 384] = ga[s * shard:(s + 1) * shard]
    ccopy(9).start()
    stage_m(4); stage_y(5); stage_z(4); saves[1].start()
    oswap.wait_recv()
    need(2)
    out_ref[...] = (hid_ref[...] + (part2_ref[...].astype(F32) + peer2_ref[...].astype(F32))).astype(B16)
    saves[6].start()
    stage_core(9)
    stage_m(5); stage_y(6)
    nswap.wait_recv()
    need(14)
    x = x_ref[...].astype(F32)
    r1 = rms(x)
    dn1 = npart_ref[...].astype(F32) + npeer_ref[...].astype(F32)
    gain1 = jnp.sum(dn1 * x * r1, axis=0, keepdims=True)
    gcol = tn(half_rows(gain1, gain2).astype(B16), half_select()).astype(B16)
    for s in range(2 * nb): ga_ref[s // 2, s % 2, :, qw + 384:qw + 512] = gcol[s * shard:(s + 1) * shard]
    ccopy(10).start()
    dx_ref[...] = dh_ref[...] + norm_back(x, r1, gains_ref[0:1, :], dn1)
    saves[5].start()
    stage_core(10); stage_core(7)
    stage_z(5); stage_m(6); stage_y(8); stage_z(6)
    stage_m(8); stage_y(9); stage_z(8); saves[3].start()
    stage_m(9); stage_y(10); stage_z(9)
    stage_m(10); stage_y(7); stage_m(7); stage_z(10)
    hs = shard // 2
    kswap = remote(ra.at[pl.ds(pl.multiple_of((1 - tp) * hs, 8), hs), pl.ds(qw, 384)], kvx_ref, ss.at[3], sr.at[3], other)
    kswap.start()
    saves[4].start()
    stage_z(7)
    saves[2].start()
    kswap.wait()
    saves[7].start()
    for cp in saves: cp.wait()
    for cp in (dswap, oswap, nswap, kvc): cp.wait_send()
    kv_each(lambda cp: cp.wait_send())
    for k in range(K):
        ccopy(k).wait_send()
        if k == 0:
            xycopy().wait_send()
            for q in range(2):
                for i in range(3): xcopy(q, z, i, 0)(zoi).wait_send()
            continue
        for p in range(1, nf): ycopy(k, p).wait_send()
        for i in range(3): zcopy(k, z, i, 0)(zoi).wait_send()

def finish(qw, *refs):
    given, refs = refs[:8], refs[8:]
    o_out, dx_out, gg1, gq, gk, gv, go, gg2, gg, gu, gd, rd, rg, ru, ro, ra, dx_ref, out_ref, kvx_ref, k_ref, v_ref, gr1, gr2, isem, sem = refs
    tp = lax.axis_index("tp")
    hs = kvx_ref.shape[0]
    loads = [pltpu.make_async_copy(a, b, isem.at[i]) for i, (a, b) in enumerate(zip(given, (rd, rg, ru, ro, ra, dx_ref, out_ref, kvx_ref)))]
    order = (4, 7, 5, 0, 1, 2, 6, 3)
    for i in order: loads[i].start()
    copies = []
    def store(a, b):
        copies.append(pltpu.make_async_copy(a, b, sem.at[len(copies)]))
        copies[-1].start()
    loads[4].wait()
    store(ra.at[:, pl.ds(0, qw)], gq)
    loads[7].wait()
    mine = ra[pl.ds(pl.multiple_of(tp * hs, 8), hs), qw:qw + 384]
    theirs = kvx_ref[...]
    lo, hi = jnp.where(tp == 0, mine, theirs), jnp.where(tp == 0, theirs, mine)
    low = lanes((hs, 128)) < 64
    def tile(v, i): return v[:, 128 * i:128 * (i + 1)]
    k_ref[:, :128] = tile(lo, 0)
    k_ref[:, 128:256] = jnp.where(low, tile(lo, 1) + tile(hi, 0), tile(hi, 0))
    k_ref[:, 256:320] = tile(hi, 1)[:, :64]
    v_ref[:, :128] = tile(lo, 2)
    v_ref[:, 128:256] = jnp.where(low, pltpu.roll(tile(lo, 1), 64, 1) + tile(hi, 2), tile(hi, 2))
    v_ref[:, 256:320] = pltpu.roll(tile(hi, 1), 64, 1)[:, :64]
    rowsT = jnp.transpose(ra[:, qw + 384:qw + 512])
    gr1[...] = rowsT[0:1, :]
    gr2[...] = rowsT[64:65, :]
    for i, a, b in ((5, dx_ref, dx_out), (0, rd, gd), (1, rg, gg), (2, ru, gu), (6, out_ref, o_out), (3, ro, go)):
        loads[i].wait()
        store(a, b)
    for a, b in ((k_ref, gk), (v_ref, gv), (gr1, gg1), (gr2, gg2)): store(a, b)
    for cp in copies: cp.wait()

def fast(tokens, lengths, attn_gain, w_query, w_key, w_value, w_out, ffn_gain, w_gate, w_up, w_down, cotangent):
    micros, rows, width = tokens.shape
    nf, nctx = lax.axis_size("fsdp"), lax.axis_size("ctx")
    nz = nctx // 2
    nb = nf * nz
    tp, t = lax.axis_index("tp"), lax.axis_index("ctx")
    total = rows * nctx
    nblk = total // 2 // rows + 1
    shard = w_query.shape[0]
    qw, ff = w_query.shape[1], w_gate.shape[1]
    M = micros * rows
    aw = qw + 512
    x = tokens.reshape(M, width)
    pairs = qw // 128
    keys = nblk * rows
    S = pltpu.SemaphoreType.DMA
    inv, ina = pl.BlockSpec(memory_space=VMEM), pl.BlockSpec(memory_space=pl.ANY)
    ns = nb * 2
    big = ff // 512 * 256 + 256 * (ff // 256 % 2)
    small = ff - big
    chunks = [(0, 0, qw), (0, qw, 512), (1, 0, qw), (2, 0, big), (3, 0, big), (2, big, small), (3, big, small), (4, 0, ff - 1280), (4, ff - 1280, 512), (4, ff - 768, 512), (4, ff - 256, 256)]
    outs = [((width, aw), B16), ((width, qw), B16), ((nctx, M, 384), B16), ((M, width), B16), ((M, qw), B16), ((M, qw), B16), ((micros * pairs, rows, 2 * keys), B16),
        ((8, width), F32), ((M, 128), F32), ((M, 128), F32), ((M, width), B16), ((M, width), F32), ((M, width), B16), ((M, width), B16)] + [((width, ff), B16), ((width, M), B16), ((M, ff), B16), ((M, ff), B16)]
    smem = pl.BlockSpec(memory_space=pltpu.SMEM)
    slots = 32
    A, O, kvall, n1, q, ao, pr, gains, cos, sin, g, hid, part2, dpart, gd, n2T, dgate, dup = pl.pallas_call(
        functools.partial(front, nf, nz, micros, rows, nblk, chunks, shard),
        out_shape=[jax.ShapeDtypeStruct(s, d) for s, d in outs],
        in_specs=[ina, ina, smem, inv, inv, ina, inv, inv] + [ina] * 4, out_specs=[ina] * 18,
        scratch_shapes=[VMEM(s, d) for s, d in outs[:14]] + [VMEM((width, M), B16)] * 2 + [VMEM((width, ff), B16)] * 4 + [VMEM((M, ff), B16)] * 2 + [VMEM((M, width), B16)] * 2 + [VMEM((M, ff), F32)] * 2 + [VMEM((M, ff), B16), VMEM((M, width), B16)] + [VMEM((M, width), F32)] * 2
            + [VMEM((M, 128), jnp.int32), VMEM((shard, 512), B16)] + [VMEM((M, width), B16)] * 2 + [S((2,)), S((11, slots)), S((11, ns)), S((11,)), S((1, n_slots(1, nz))), S((1, nctx)), S((micros,)), S((micros,)), S((24,))],
        compiler_params=pltpu.CompilerParams(collective_id=0, has_side_effects=True, vmem_limit_bytes=63 << 20), name="front",
    )(x, cotangent.reshape(M, width), lengths[0], attn_gain.reshape(1, shard), ffn_gain.reshape(1, shard), w_query, w_key, w_value, w_out.T, w_gate, w_up, w_down.T)
    chunks = [(0, 0, 512), (0, 512, 256), (0, 768, ff - 768), (1, 0, big), (1, big, small), (2, 0, big), (2, big, small - 256), (2, ff - 256, 256), (3, 0, qw), (4, 0, qw), (4, qw, 512)]
    wd = [ff, ff, ff, qw, aw]
    K = len(chunks)
    hs = shard // 2
    outs = [((shard, w), F32) for w in wd] + [((M, width), F32), ((M, width), B16), ((hs, 384), F32)]
    scratch = [VMEM((nb, shard, ff), B16)] + [VMEM((nb, 2, shard, ff), B16)] * 2 + [VMEM((nb, shard, w), B16) for w in wd] + [VMEM((nf - 1, nz, shard, w), B16) for w in wd] + [VMEM((4, shard, w), B16) for w in wd]
    scratch += [VMEM((4, shard, 512), B16), VMEM((nb, 2, shard, qw), B16), VMEM((nb, 2, shard, aw), B16), VMEM((M, qw), B16), VMEM((M, qw), F32), VMEM((nz, 2, M, 384), B16),
        VMEM((nz, M, 384), B16), VMEM((2, M, 384), B16), VMEM((M, qw + 384), B16)] + [VMEM((M, width), B16)] * 3
    given = [g, dpart, part2, hid, gains, q, kvall, O, A, ao, pr, n1, cos, sin, x, n2T, dgate, dup]
    scratch += [VMEM(v.shape, v.dtype) for v in given] + [S((18,))] + [VMEM(s, d) for s, d in outs[:6] + outs[7:]] + [S((8,))]
    scratch += [S((K,)), S((K,)), S((K,)), S((K, nf - 1)), S((K, nf - 1)), S((K, 6)), S((K, 8)), S((1,)), S((1,)), S((2,)), S((2,)), S((4,)), S((4,))]
    ends = pl.pallas_call(
        functools.partial(back, nf, nz, micros, rows, nblk, chunks, shard),
        out_shape=[jax.ShapeDtypeStruct(s, d) for s, d in outs],
        in_specs=[ina] * 19, out_specs=[ina] * 8, scratch_shapes=scratch,
        compiler_params=pltpu.CompilerParams(collective_id=4, has_side_effects=True, vmem_limit_bytes=67043328), name="back",
    )(gd.reshape(nb, 2, shard, ff), *given)
    outs = [((M, width), B16), ((M, width), F32), ((1, shard), F32), ((shard, qw), F32), ((hs, 5 * HD), F32), ((hs, 5 * HD), F32), ((shard, qw), F32), ((1, shard), F32)] + [((shard, ff), F32)] * 3
    output, dx, gain1, gq, gk, gv, go, gain2, gg, gu, gd = pl.pallas_call(
        functools.partial(finish, qw), out_shape=[jax.ShapeDtypeStruct(s, d) for s, d in outs],
        in_specs=[ina] * 8, out_specs=[ina] * 11,
        scratch_shapes=[VMEM(v.shape, v.dtype) for v in ends] + [VMEM((hs, 5 * HD), F32)] * 2 + [VMEM((1, shard), F32)] * 2 + [S((8,)), S((11,))], name="finish",
    )(*ends)
    return (output.reshape(micros, rows, width), dx.reshape(micros, rows, width), gain1.reshape(shard), gq, gk, gv, go.T, gain2.reshape(shard), gg, gu, gd.T)


def solution(mesh):
    placed = (
        P(None, ("fsdp", "ctx"), None),
        P("fsdp", None, None),
        P(("fsdp", "ctx")),
        P(("fsdp", "ctx"), "tp"),
        P(("fsdp", "ctx"), None),
        P(("fsdp", "ctx"), None),
        P("tp", ("fsdp", "ctx")),
        P(("fsdp", "ctx")),
        P(("fsdp", "ctx"), "tp"),
        P(("fsdp", "ctx"), "tp"),
        P("tp", ("fsdp", "ctx")),
        P(None, ("fsdp", "ctx"), None),
    )
    def chosen(*args):
        fits = args[3].shape[0] % 16 == 0 and mesh.shape["tp"] == 2 and mesh.shape["fsdp"] == 2 and mesh.shape["ctx"] == 8
        return (fast if fits else shards)(*args)

    return jax.shard_map(
        chosen,
        mesh=mesh,
        in_specs=placed,
        out_specs=(
            P(None, ("fsdp", "ctx"), None),
            P(None, ("fsdp", "ctx"), None),
            P(("fsdp", "ctx")),
            P(("fsdp", "ctx"), "tp"),
            P(("fsdp", "ctx", "tp"), None),
            P(("fsdp", "ctx", "tp"), None),
            P("tp", ("fsdp", "ctx")),
            P(("fsdp", "ctx")),
            P(("fsdp", "ctx"), "tp"),
            P(("fsdp", "ctx"), "tp"),
            P("tp", ("fsdp", "ctx")),
        ),
        check_vma=False,
    )
```

```python
import functools
import math

import jax
import jax.numpy as jnp
from jax import lax
from jax.experimental import pallas as pl
from jax.experimental.pallas import tpu as pltpu
from jax.sharding import PartitionSpec as P

H = 20
KV = 5
HD = 64


EPSILON = 1e-05
THETA = 10000.0
MASKED = -1e30


def layout(lengths_row, total_rows):
    ending = jnp.cumsum(lengths_row)
    opening = ending - lengths_row
    doc_count = lengths_row.shape[0]
    places = jnp.arange(total_rows, dtype=jnp.int32)
    segment = jnp.sum((places[:, None] >= ending[None, :]).astype(jnp.int32), axis=1)
    firsts = jnp.concatenate([opening, ending[-1:]])
    labels = jnp.arange(doc_count + 1, dtype=jnp.int32)
    begins = jnp.sum(jnp.where(segment[:, None] == labels[None, :], firsts[None, :], 0), axis=1)
    return (segment, places - begins, segment < doc_count)


def rotary(position, head_size):
    halves = head_size // 2
    inverse = jnp.exp(jnp.arange(halves, dtype=jnp.float32) * (-2.0 * math.log(THETA) / head_size))
    angles = position.astype(jnp.float32)[:, None] * inverse[None, :]
    cos_table = jnp.cos(angles)
    sin_table = jnp.sin(angles)
    return (
        jnp.concatenate([cos_table, cos_table], axis=1),
        jnp.concatenate([sin_table, sin_table], axis=1),
    )


def turn(tensor, cos_table, sin_table):
    halves = tensor.shape[-1] // 2
    rotated = jnp.concatenate([-tensor[..., halves:], tensor[..., :halves]], axis=-1)
    return tensor * cos_table[:, None, :] + rotated * sin_table[:, None, :]


def turn_back(tensor, cos_table, sin_table):
    halves = tensor.shape[-1] // 2
    shifted = tensor * sin_table[:, None, :]
    rotated = jnp.concatenate([shifted[..., halves:], -shifted[..., :halves]], axis=-1)
    return tensor * cos_table[:, None, :] + rotated


def norm_back(values, factor, gain_vec, grad_in):
    scaled = gain_vec * grad_in
    return factor * scaled - values * factor**3 * jnp.mean(scaled * values, axis=-1, keepdims=True)


def collect(attn_gain, w_query, w_key, w_value, w_out, ffn_gain, w_gate, w_up, w_down):
    return (
        lax.all_gather(attn_gain, ("fsdp", "ctx"), axis=0, tiled=True),
        lax.all_gather(w_query, ("fsdp", "ctx"), axis=0, tiled=True),
        lax.all_gather(w_key, ("fsdp", "ctx"), axis=0, tiled=True),
        lax.all_gather(w_value, ("fsdp", "ctx"), axis=0, tiled=True),
        lax.all_gather(w_out, ("fsdp", "ctx"), axis=1, tiled=True),
        lax.all_gather(ffn_gain, ("fsdp", "ctx"), axis=0, tiled=True),
        lax.all_gather(w_gate, ("fsdp", "ctx"), axis=0, tiled=True),
        lax.all_gather(w_up, ("fsdp", "ctx"), axis=0, tiled=True),
        lax.all_gather(w_down, ("fsdp", "ctx"), axis=1, tiled=True),
    )


def collect_again(attn_gain, w_query, w_key, w_value, w_out, ffn_gain, w_gate, w_up, w_down):
    return (
        lax.all_gather(attn_gain, ("fsdp", "ctx"), axis=0, tiled=True),
        lax.all_gather(w_query, ("fsdp", "ctx"), axis=0, tiled=True),
        lax.all_gather(w_key, ("fsdp", "ctx"), axis=0, tiled=True),
        lax.all_gather(w_value, ("fsdp", "ctx"), axis=0, tiled=True),
        lax.all_gather(w_out, ("fsdp", "ctx"), axis=1, tiled=True),
        lax.all_gather(ffn_gain, ("fsdp", "ctx"), axis=0, tiled=True),
        lax.all_gather(w_gate, ("fsdp", "ctx"), axis=0, tiled=True),
        lax.all_gather(w_up, ("fsdp", "ctx"), axis=0, tiled=True),
        lax.all_gather(w_down, ("fsdp", "ctx"), axis=1, tiled=True),
    )


def reduce_grads(main_part, pair_part):
    shares = (
        lax.psum_scatter(main_part[0], ("fsdp", "ctx"), scatter_dimension=0, tiled=True),
        lax.psum_scatter(main_part[1], ("fsdp", "ctx"), scatter_dimension=0, tiled=True),
        lax.psum_scatter(main_part[2], ("fsdp", "ctx"), scatter_dimension=1, tiled=True),
        lax.psum_scatter(main_part[3], ("fsdp", "ctx"), scatter_dimension=0, tiled=True),
        lax.psum_scatter(main_part[4], ("fsdp", "ctx"), scatter_dimension=0, tiled=True),
        lax.psum_scatter(main_part[5], ("fsdp", "ctx"), scatter_dimension=0, tiled=True),
        lax.psum_scatter(main_part[6], ("fsdp", "ctx"), scatter_dimension=1, tiled=True),
    )
    pairs = (
        lax.psum_scatter(pair_part[0], ("fsdp", "ctx", "tp"), scatter_dimension=0, tiled=True),
        lax.psum_scatter(pair_part[1], ("fsdp", "ctx", "tp"), scatter_dimension=0, tiled=True),
    )
    return (shares, pairs)


def block_allowed(segment_rows, places_rows, segment_all, block_at, key_block):
    segment_keys = lax.dynamic_slice_in_dim(segment_all, block_at * key_block, key_block)
    place_keys = block_at * key_block + jnp.arange(key_block, dtype=jnp.int32)
    return (segment_rows[:, None] == segment_keys[None, :]) & (
        place_keys[None, :] <= places_rows[:, None]
    )


def sweep(visit, initial, block_count, useful):

    def advance(block_at, state):
        return lax.cond(
            useful(block_at),
            lambda current: visit(block_at, current),
            lambda current: current,
            state,
        )

    return lax.fori_loop(0, block_count, advance, initial)


def shards(
    tokens,
    lengths,
    attn_gain,
    w_query,
    w_key,
    w_value,
    w_out,
    ffn_gain,
    w_gate,
    w_up,
    w_down,
    cotangent,
):
    f32 = jnp.float32
    b16 = jnp.bfloat16
    micro_count = tokens.shape[0]
    tok_rows = tokens.shape[1]
    model_width = tokens.shape[2]
    ctx_count = lax.axis_size("ctx")
    tp_count = lax.axis_size("tp")
    ctx_at = lax.axis_index("ctx")
    tp_at = lax.axis_index("tp")
    total_rows = tok_rows * ctx_count
    half_rows = tok_rows // tp_count
    local_heads = w_query.shape[1] // HD
    kv_width = KV * HD
    scaling = 1.0 / math.sqrt(HD)
    key_block = min(512, total_rows)
    block_count = total_rows // key_block
    heads_global = tp_at * local_heads + jnp.arange(local_heads, dtype=jnp.int32)
    select = heads_global[:, None] // (H // KV) == jnp.arange(KV, dtype=jnp.int32)[None, :]
    select_low = select.astype(b16)
    select_high = select.astype(f32)
    row_offset = tp_at * half_rows
    start_row = ctx_at * tok_rows
    places_mine = start_row + jnp.arange(tok_rows, dtype=jnp.int32)
    outputs_list = []
    input_list = []
    main_total = None
    pair_total = None
    for micro_at in range(micro_count):
        gathered = collect(
            attn_gain, w_query, w_key, w_value, w_out, ffn_gain, w_gate, w_up, w_down
        )
        (
            gain_first,
            query_full,
            key_full,
            value_full,
            out_full,
            gain_second,
            gate_full,
            up_full,
            down_full,
        ) = gathered
        inputs = tokens[micro_at].astype(f32)
        segment_all, position_all, live_all = layout(lengths[0, micro_at], total_rows)
        segment_mine = lax.dynamic_slice_in_dim(segment_all, start_row, tok_rows)
        position_mine = lax.dynamic_slice_in_dim(position_all, start_row, tok_rows)
        live_mine = lax.dynamic_slice_in_dim(live_all, start_row, tok_rows)
        cos_table, sin_table = rotary(position_mine, HD)
        rms_first = lax.rsqrt(jnp.mean(inputs * inputs, axis=-1, keepdims=True) + EPSILON)
        normed_first = (inputs * rms_first * gain_first.astype(f32)).astype(b16)
        queries = jnp.dot(normed_first, query_full, preferred_element_type=f32).reshape(
            tok_rows, local_heads, HD
        )
        queries = turn(queries, cos_table, sin_table).astype(b16)
        key_lin = jnp.dot(normed_first, key_full, preferred_element_type=f32).reshape(
            tok_rows, KV, HD
        )
        key_rot = turn(key_lin, cos_table, sin_table).astype(b16).reshape(tok_rows, kv_width)
        value_rot = jnp.dot(normed_first, value_full, preferred_element_type=f32).astype(b16)
        keys_all, values_all = (
            lax.all_gather(key_rot, "ctx", axis=0, tiled=True),
            lax.all_gather(value_rot, "ctx", axis=0, tiled=True),
        )
        keys_local = jnp.einsum(
            "tjd,hj->thd",
            keys_all.reshape(total_rows, KV, HD),
            select_low,
            preferred_element_type=f32,
        ).astype(b16)
        values_local = jnp.einsum(
            "tjd,hj->thd",
            values_all.reshape(total_rows, KV, HD),
            select_low,
            preferred_element_type=f32,
        ).astype(b16)

        def useful(block_at):
            return jnp.any(
                block_allowed(segment_mine, places_mine, segment_all, block_at, key_block)
            )

        def logits_of(block_at):
            key_rows = lax.dynamic_slice_in_dim(keys_local, block_at * key_block, key_block)
            raw_scores = (
                jnp.einsum("qhd,khd->hqk", queries, key_rows, preferred_element_type=f32) * scaling
            )
            allowed = block_allowed(segment_mine, places_mine, segment_all, block_at, key_block)
            return jnp.where(allowed[None], raw_scores, MASKED)

        def statistic(block_at, state):
            top_score, mass_sum = state
            logits = logits_of(block_at)
            new_top = jnp.maximum(top_score, jnp.max(logits, axis=-1))
            mass_sum = mass_sum * jnp.exp(top_score - new_top) + jnp.sum(
                jnp.exp(logits - new_top[..., None]), axis=-1
            )
            return (new_top, mass_sum)

        start_state = (
            jnp.full((local_heads, tok_rows), MASKED, f32),
            jnp.zeros((local_heads, tok_rows), f32),
        )
        top_score, mass_sum = sweep(statistic, start_state, block_count, useful)

        def probable(block_at):
            return jnp.exp(logits_of(block_at) - top_score[..., None]) / mass_sum[..., None]

        def accumulate(block_at, running):
            probs_low = probable(block_at).astype(b16)
            value_rows = lax.dynamic_slice_in_dim(values_local, block_at * key_block, key_block)
            return running + jnp.einsum(
                "hqk,khd->qhd", probs_low, value_rows, preferred_element_type=f32
            )

        attended = sweep(
            accumulate, jnp.zeros((tok_rows, local_heads, HD), f32), block_count, useful
        )
        attended_low = attended.reshape(tok_rows, local_heads * HD).astype(b16)
        branch = lax.psum(
            jnp.dot(attended_low, out_full, preferred_element_type=f32).astype(jnp.bfloat16), "tp"
        ).astype(jnp.float32)
        hidden = inputs + branch
        rms_second = lax.rsqrt(jnp.mean(hidden * hidden, axis=-1, keepdims=True) + EPSILON)
        normed_second = (hidden * rms_second * gain_second.astype(f32)).astype(b16)
        gate_pre = jnp.dot(normed_second, gate_full, preferred_element_type=f32)
        upward = jnp.dot(normed_second, up_full, preferred_element_type=f32)
        sigmoid_gate = jax.nn.sigmoid(gate_pre)
        silu_gate = jax.nn.silu(gate_pre)
        active = (silu_gate * upward).astype(b16)
        mixed = lax.psum(
            jnp.dot(active, down_full, preferred_element_type=f32).astype(jnp.bfloat16), "tp"
        ).astype(jnp.float32)
        outputs_list.append((hidden + mixed).astype(b16))
        gathered = collect_again(
            attn_gain, w_query, w_key, w_value, w_out, ffn_gain, w_gate, w_up, w_down
        )
        (
            gain_first,
            query_full,
            key_full,
            value_full,
            out_full,
            gain_second,
            gate_full,
            up_full,
            down_full,
        ) = gathered
        grad_rows = cotangent[micro_at].astype(f32) * live_mine[:, None].astype(f32)
        grad_low = grad_rows.astype(b16)
        grad_down = jnp.einsum("tf,td->fd", active, grad_low, preferred_element_type=f32)
        grad_active = jnp.einsum("td,fd->tf", grad_low, down_full, preferred_element_type=f32)
        grad_gate_pre = (
            grad_active * upward * sigmoid_gate * (1.0 + gate_pre * (1.0 - sigmoid_gate))
        ).astype(b16)
        grad_upward = (grad_active * silu_gate).astype(b16)
        grad_gate = jnp.einsum(
            "te,tf->ef", normed_second, grad_gate_pre, preferred_element_type=f32
        )
        grad_up = jnp.einsum("te,tf->ef", normed_second, grad_upward, preferred_element_type=f32)
        grad_normed_second = jnp.einsum(
            "tf,ef->te", grad_gate_pre, gate_full, preferred_element_type=f32
        ) + jnp.einsum("tf,ef->te", grad_upward, up_full, preferred_element_type=f32)
        grad_normed_second = lax.psum(grad_normed_second.astype(jnp.bfloat16), "tp").astype(
            jnp.float32
        )
        grad_gain_second = jnp.sum(grad_normed_second * hidden * rms_second, axis=0)
        grad_hidden = grad_rows + norm_back(
            hidden, rms_second, gain_second.astype(f32), grad_normed_second
        )
        grad_branch = grad_hidden.astype(b16)
        grad_out = jnp.einsum("te,td->ed", attended_low, grad_branch, preferred_element_type=f32)
        grad_att = (
            jnp.einsum("td,ed->te", grad_branch, out_full, preferred_element_type=f32)
            .astype(b16)
            .reshape(tok_rows, local_heads, HD)
        )
        delta_rows = jnp.sum(grad_att.astype(f32) * attended, axis=-1).T

        def backward_visit(block_at, state):
            grad_queries, grad_keys, grad_values = state
            first_row = block_at * key_block
            key_rows = lax.dynamic_slice_in_dim(keys_local, first_row, key_block)
            value_rows = lax.dynamic_slice_in_dim(values_local, first_row, key_block)
            probs = probable(block_at)
            probs_low = probs.astype(b16)
            grad_probs = jnp.einsum(
                "qhd,khd->hqk", grad_att, value_rows, preferred_element_type=f32
            )
            grad_logits = (probs * (grad_probs - delta_rows[..., None])).astype(b16)
            grad_queries = (
                grad_queries
                + jnp.einsum("hqk,khd->qhd", grad_logits, key_rows, preferred_element_type=f32)
                * scaling
            )
            key_part = (
                jnp.einsum("hqk,qhd->khd", grad_logits, queries, preferred_element_type=f32)
                * scaling
            )
            value_part = jnp.einsum("hqk,qhd->khd", probs_low, grad_att, preferred_element_type=f32)
            grad_keys = lax.dynamic_update_slice_in_dim(grad_keys, key_part, first_row, 0)
            grad_values = lax.dynamic_update_slice_in_dim(grad_values, value_part, first_row, 0)
            return (grad_queries, grad_keys, grad_values)

        back_state = (
            jnp.zeros((tok_rows, local_heads, HD), f32),
            jnp.zeros((total_rows, local_heads, HD), f32),
            jnp.zeros((total_rows, local_heads, HD), f32),
        )
        grad_queries, grad_keys, grad_values = sweep(
            backward_visit, back_state, block_count, useful
        )
        key_heads = jnp.einsum(
            "thd,hj->tjd", grad_keys, select_high, precision=lax.Precision.HIGHEST
        ).reshape(total_rows, kv_width)
        value_heads = jnp.einsum(
            "thd,hj->tjd", grad_values, select_high, precision=lax.Precision.HIGHEST
        ).reshape(total_rows, kv_width)
        key_sum, value_sum = (
            lax.psum_scatter(
                key_heads.astype(jnp.bfloat16), ("ctx", "tp"), scatter_dimension=0, tiled=True
            ).astype(jnp.float32),
            lax.psum_scatter(
                value_heads.astype(jnp.bfloat16), ("ctx", "tp"), scatter_dimension=0, tiled=True
            ).astype(jnp.float32),
        )
        cos_half = lax.dynamic_slice_in_dim(cos_table, row_offset, half_rows)
        sin_half = lax.dynamic_slice_in_dim(sin_table, row_offset, half_rows)
        grad_key_lin = (
            turn_back(key_sum.reshape(half_rows, KV, HD), cos_half, sin_half)
            .astype(b16)
            .reshape(half_rows, kv_width)
        )
        grad_value_lin = value_sum.astype(b16)
        normed_half = lax.dynamic_slice_in_dim(normed_first, row_offset, half_rows)
        grad_key = jnp.einsum("te,tk->ek", normed_half, grad_key_lin, preferred_element_type=f32)
        grad_value = jnp.einsum(
            "te,tk->ek", normed_half, grad_value_lin, preferred_element_type=f32
        )
        grad_normed_pair = jnp.einsum(
            "tk,ek->te", grad_key_lin, key_full, preferred_element_type=f32
        ) + jnp.einsum("tk,ek->te", grad_value_lin, value_full, preferred_element_type=f32)
        grad_query_lin = (
            turn_back(grad_queries, cos_table, sin_table)
            .astype(b16)
            .reshape(tok_rows, local_heads * HD)
        )
        grad_query = jnp.einsum(
            "te,tq->eq", normed_first, grad_query_lin, preferred_element_type=f32
        )
        grad_normed_first = jnp.einsum(
            "tq,eq->te", grad_query_lin, query_full, preferred_element_type=f32
        )
        grad_normed_first = grad_normed_first + lax.dynamic_update_slice_in_dim(
            jnp.zeros((tok_rows, model_width), f32), grad_normed_pair, row_offset, 0
        )
        grad_normed_first = lax.psum(grad_normed_first.astype(jnp.bfloat16), "tp").astype(
            jnp.float32
        )
        grad_gain_first = jnp.sum(grad_normed_first * inputs * rms_first, axis=0)
        input_list.append(
            grad_hidden + norm_back(inputs, rms_first, gain_first.astype(f32), grad_normed_first)
        )
        main_part = (
            grad_gain_first,
            grad_query,
            grad_out,
            grad_gain_second,
            grad_gate,
            grad_up,
            grad_down,
        )
        pair_part = (grad_key, grad_value)
        main_part, pair_part = reduce_grads(main_part, pair_part)
        if main_total is None:
            main_total = main_part
            pair_total = pair_part
        else:
            main_total = jax.tree.map(jnp.add, main_total, main_part)
            pair_total = jax.tree.map(jnp.add, pair_total, pair_part)
    return (
        jnp.stack(outputs_list),
        jnp.stack(input_list),
        main_total[0],
        main_total[1],
        pair_total[0],
        pair_total[1],
        main_total[2],
        main_total[3],
        main_total[4],
        main_total[5],
        main_total[6],
    )


F32 = jnp.float32
B16 = jnp.bfloat16
HD = 64
EPSILON = 1e-05
THETA = 10000.0
MASKED = -1e30
SCALE = 1.0 / math.sqrt(HD)
VMEM = pltpu.VMEM

def nn(a, b): return lax.dot_general(a, b, (((1,), (0,)), ((), ())), preferred_element_type=F32)
def nt(a, b): return lax.dot_general(a, b, (((1,), (1,)), ((), ())), preferred_element_type=F32)
def tn(a, b): return lax.dot_general(a, b, (((0,), (0,)), ((), ())), preferred_element_type=F32)

def lanes(shape): return lax.broadcasted_iota(jnp.int32, shape, len(shape) - 1)

def rope(t, cos, sin):
    low = lanes(t.shape) % 64 < 32
    rot = jnp.where(low, -pltpu.roll(t, 96, 1), pltpu.roll(t, 32, 1))
    return t * cos + rot * sin

def rope_back(u, cos, sin):
    low = lanes(u.shape) % 64 < 32
    us = u * sin
    return u * cos + jnp.where(low, pltpu.roll(us, 96, 1), -pltpu.roll(us, 32, 1))

def rms(v): return lax.rsqrt(jnp.mean(v * v, axis=-1, keepdims=True) + EPSILON)

def norm_back(v, r, gain, d):
    s = gain * d
    return r * s - v * (r * r * r) * jnp.mean(s * v, axis=-1, keepdims=True)

def doubled(tile, which):
    t = tile.astype(F32)
    r = pltpu.roll(t, 64, 1)
    low = lanes(t.shape) < 64
    return (jnp.where(low, t, r) if which == 0 else jnp.where(low, r, t)).astype(B16)

def window_start(t, nblk): return jnp.maximum(t - nblk + 1, 0)

def window(kvall_ref, w0, nblk, m, rows, tile):
    return jnp.concatenate([kvall_ref[w0 + b, m * rows:(m + 1) * rows, 128 * tile:128 * (tile + 1)] for b in range(nblk)], axis=0)

def heads_kv(kvall_ref, w0, nblk, m, rows):
    k01 = window(kvall_ref, w0, nblk, m, rows, 0)
    k2v2 = window(kvall_ref, w0, nblk, m, rows, 1)
    v01 = window(kvall_ref, w0, nblk, m, rows, 2)
    ks = [doubled(k01, 0), doubled(k01, 1), doubled(k2v2, 0)]
    vs = [doubled(v01, 0), doubled(v01, 1), doubled(k2v2, 1)]
    return ks, vs

def pick(group, p, tp):
    a, b = p // 2, (p + 1) // 2
    return group[a] if a == b else jnp.where(tp == 0, group[a], group[b])

def stacked(head):
    low = lanes(head.shape) < 64
    zero = jnp.zeros_like(head)
    return jnp.concatenate([jnp.where(low, head, zero), jnp.where(low, zero, head)], axis=0)

def allowed_of(begin, row0, key0, rows, keys):
    i = row0 + lax.broadcasted_iota(jnp.int32, (rows, keys), 0)
    j = key0 + lax.broadcasted_iota(jnp.int32, (rows, keys), 1)
    return (j <= i) & (j >= begin)

MESHT = pl.DeviceIdType.MESH

def n_slots(nf, nz):
    return 3 + (nf - 1) + 2 * (nz - 1) * (2 + nf - 1) + (nf - 1) * nz

def swap_body(src_ref, dst_ref, ssem, rsem):
    other = dict(tp=1 - lax.axis_index("tp"))
    barrier = pltpu.get_barrier_semaphore()
    pl.semaphore_signal(barrier, inc=1, device_id=other, device_id_type=MESHT)
    pl.semaphore_wait(barrier, 1)
    cp = pltpu.make_async_remote_copy(src_ref=src_ref, dst_ref=dst_ref, send_sem=ssem, recv_sem=rsem, device_id=other, device_id_type=MESHT)
    cp.start()
    cp.wait()

def swap(v, cid):
    return pl.pallas_call(
        swap_body, out_shape=jax.ShapeDtypeStruct(v.shape, v.dtype),
        in_specs=[pl.BlockSpec(memory_space=VMEM)], out_specs=pl.BlockSpec(memory_space=VMEM),
        scratch_shapes=[pltpu.SemaphoreType.DMA, pltpu.SemaphoreType.DMA],
        compiler_params=pltpu.CompilerParams(collective_id=cid, has_side_effects=True),
        name="tp_swap_%d" % v.shape[0],
    )(v)

def greet(t, z, c, nz, y, nf, all_z):
    barrier = pltpu.get_barrier_semaphore()
    def sig(**dev):
        pl.semaphore_signal(barrier, inc=1, device_id=dev, device_id_type=MESHT)
    sig(ctx=t + 1 - 2 * c)
    sig(tp=1 - lax.axis_index("tp"))
    for p in range(1, nf): sig(fsdp=lax.rem(y + p, nf))
    if all_z:
        for p in range(1, nz): sig(ctx=lax.rem(z + p, nz) * 2 + c)
        pl.semaphore_wait(barrier, nf + nz)
        return
    @pl.when(z > 0)
    def _(): sig(ctx=t - 2)
    @pl.when(z < nz - 1)
    def _(): sig(ctx=t + 2)
    @pl.when((z > 0) & (z < nz - 1))
    def _(): pl.semaphore_wait(barrier, 3 + nf)
    @pl.when((z == 0) | (z == nz - 1))
    def _(): pl.semaphore_wait(barrier, 2 + nf)

class Gather:
    y_first = ()
    def __init__(self, nf, nz, at, own_src, send_sem, recv_sem):
        self.nf, self.nz, self.at, self.own_src, self.ss, self.rs = nf, nz, at, own_src, send_sem, recv_sem
        self.y = lax.axis_index("fsdp") if nf > 1 else 0
        self.t = lax.axis_index("ctx")
        self.z, self.c = self.t // 2, lax.rem(self.t, 2)
        self.sib = dict(ctx=self.t + 1 - 2 * self.c)
        self.me = self.shard(self.y, self.z, self.c)
        count = [0]
        def new(n=1):
            count[0] += n
            return count[0] - n
        self.ownL, self.ownR, self.ownC, self.ownY = new(), new(), new(), new(nf - 1)
        self.zs = {(side, d): (new(), new(), new(nf - 1)) for d in range(1, nz) for side in (0, 1)}
        self.yc = {(p, zz): new() for p in range(1, nf) for zz in range(nz)}

    def shard(self, yy, zz, cc): return yy * self.nz * 2 + zz * 2 + cc
    def ydev(self, p): return dict(fsdp=lax.rem(self.y + p, self.nf))
    def copy(self, k, s, slot, dev, src=None):
        return pltpu.make_async_remote_copy(src_ref=self.at(k, s) if src is None else src, dst_ref=self.at(k, s),
            send_sem=self.ss.at[k, slot], recv_sem=self.rs.at[k, s], device_id=dev, device_id_type=MESHT)
    def send(self, *a): self.copy(*a).start()
    def got(self, k, s): self.copy(k, s, 0, self.sib).wait_recv()
    def sent(self, k, slot): self.copy(k, self.me, slot, self.sib).wait_send()
    def when_z(self, side, d):
        z, nz = self.z, self.nz
        return ((z >= d), (z < nz - 1), z - d, self.t + 2) if side == 0 else ((z + d <= nz - 1), (z > 0), z + d, self.t - 2)

    def own(self, k):
        src = self.own_src(k)
        if k not in self.y_first: self.own_y(k)
        @pl.when(self.z > 0)
        def _(): self.send(k, self.me, self.ownL, dict(ctx=self.t - 2), src)
        @pl.when(self.z < self.nz - 1)
        def _(): self.send(k, self.me, self.ownR, dict(ctx=self.t + 2), src)
        self.send(k, self.me, self.ownC, self.sib, src)

    def own_y(self, k):
        for p in range(1, self.nf): self.send(k, self.me, self.ownY + p - 1, self.ydev(p), self.own_src(k))

    def zstep(self, k, d, side):
        ok, more, zz, far = self.when_z(side, d)
        s = self.shard(self.y, zz, self.c)
        sf, sc, sy = self.zs[(side, d)]
        @pl.when(ok)
        def _():
            self.got(k, s)
            if d < self.nz - 1:
                @pl.when(more)
                def _(): self.send(k, s, sf, dict(ctx=far))
            for p in range(1, self.nf): self.send(k, s, sy + p - 1, self.ydev(p))
            self.send(k, s, sc, self.sib)

    def ystep(self, k, p, zz):
        s = self.shard(lax.rem(self.y + self.nf - p, self.nf), zz, self.c)
        self.got(k, s)
        self.send(k, s, self.yc[(p, zz)], self.sib)

    def to_z(self, k, s, slot):
        @pl.when(self.z > 0)
        def _(): self.send(k, s, slot, dict(ctx=self.t - 2))
        @pl.when(self.z < self.nz - 1)
        def _(): self.send(k, s, slot + 1, dict(ctx=self.t + 2))
    def peer_slot(self, p): return 2 + self.nf + 3 * (p - 1)
    def far_slot(self, p, d, side): return 2 + self.nf + 3 * (self.nf - 1) + 2 * ((p * (self.nz - 1) + d - 1) * 2 + side)
    def peer(self, p): return lax.rem(self.y + p, self.nf)
    def first_y(self, k):
        for p in range(1, self.nf):
            s = self.shard(self.peer(p), self.z, self.c)
            self.got(k, s)
            self.to_z(k, s, self.peer_slot(p))
            self.send(k, s, self.peer_slot(p) + 2, self.sib)
    def then_z(self, k, d):
        for side in (0, 1):
            ok, more, zz, far = self.when_z(side, d)
            @pl.when(ok)
            def _():
                for p in range(self.nf):
                    s = self.shard(self.peer(p), zz, self.c)
                    f = self.far_slot(p, d, side)
                    self.got(k, s)
                    if d < self.nz - 1:
                        @pl.when(more)
                        def _(): self.send(k, s, f, dict(ctx=far))
                    self.send(k, s, f + 1, self.sib)
    def YZ(self, k): return [functools.partial(self.first_y, k)] + [functools.partial(self.then_z, k, d) for d in range(1, self.nz)]
    def drain_yz(self, k):
        for p in range(1, self.nf): self.sent(k, self.ownY + p - 1)
        self.sent(k, self.ownC)
        for p in range(1, self.nf): self.sent(k, self.peer_slot(p) + 2)
        for edge, own, i in ((self.z > 0, self.ownL, 0), (self.z < self.nz - 1, self.ownR, 1)):
            @pl.when(edge)
            def _():
                self.sent(k, own)
                for p in range(1, self.nf): self.sent(k, self.peer_slot(p) + i)
        for d in range(1, self.nz):
            for side in (0, 1):
                ok, more, _zz, _far = self.when_z(side, d)
                @pl.when(ok)
                def _():
                    for p in range(self.nf):
                        if d < self.nz - 1:
                            @pl.when(more)
                            def _(): self.sent(k, self.far_slot(p, d, side))
                        self.sent(k, self.far_slot(p, d, side) + 1)

    def Z(self, k): return [functools.partial(self.zstep, k, d, side) for d in range(1, self.nz) for side in (0, 1)]
    def hop(self, k, d):
        if k in self.y_first:
            if d == 1: self.first_y(k)
            self.then_z(k, d)
        else:
            for side in (0, 1): self.zstep(k, d, side)
    def last(self, k):
        if k not in self.y_first: emit(self.Y(k))
    def Y(self, k): return [functools.partial(self.ystep, k, p, zz) for p in range(1, self.nf) for zz in range(self.nz)]

    def arrived(self, k):
        for yy in range(self.nf):
            for zz in range(self.nz):
                self.got(k, self.shard(yy, zz, 1 - self.c))

    def drain(self, k):
        for p in range(1, self.nf): self.sent(k, self.ownY + p - 1)
        @pl.when(self.z > 0)
        def _(): self.sent(k, self.ownL)
        @pl.when(self.z < self.nz - 1)
        def _(): self.sent(k, self.ownR)
        self.sent(k, self.ownC)
        for d in range(1, self.nz):
            for side in (0, 1):
                ok, more, _zz, _far = self.when_z(side, d)
                sf, sc, sy = self.zs[(side, d)]
                @pl.when(ok)
                def _():
                    if d < self.nz - 1:
                        @pl.when(more)
                        def _(): self.sent(k, sf)
                    for p in range(1, self.nf): self.sent(k, sy + p - 1)
                    self.sent(k, sc)
        for v in self.yc.values(): self.sent(k, v)

def emit(*lists):
    for steps in lists:
        for step in steps: step()

class KeysGather(Gather):
    far = 2
    def own(self):
        @pl.when(self.z < self.nz - 1)
        def _(): self.send(0, self.me, self.ownR, dict(ctx=self.t + 2))
        self.send(0, self.me, self.ownC, self.sib)
    def step(self, d):
        s = self.shard(0, self.z - d, self.c)
        sf, sc, _y = self.zs[(0, d)]
        @pl.when(self.z >= d)
        def _():
            self.got(0, s)
            if d < self.far:
                @pl.when(self.z < self.nz - 1)
                def _(): self.send(0, s, sf, dict(ctx=self.t + 2))
            self.send(0, s, sc, self.sib)
    def arrived(self):
        for d in range(self.far + 1):
            @pl.when(self.z >= d)
            def _(): self.got(0, self.shard(0, self.z - d, 1 - self.c))
    def drain(self):
        @pl.when(self.z < self.nz - 1)
        def _(): self.sent(0, self.ownR)
        self.sent(0, self.ownC)
        for d in range(1, self.far + 1):
            sf, sc, _y = self.zs[(0, d)]
            @pl.when(self.z >= d)
            def _():
                if d < self.far:
                    @pl.when(self.z < self.nz - 1)
                    def _(): self.sent(0, sf)
                self.sent(0, sc)

def kv_tile(tp, wk, wv):
    n = wk.shape[1]
    i, l = lax.broadcasted_iota(jnp.int32, (n, 384), 0), lax.broadcasted_iota(jnp.int32, (n, 384), 1)
    first = tp * 2 * HD
    ek = (i == first + l) & (l < 3 * HD)
    ev = ((i == first + l - 4 * HD) & (l >= 4 * HD)) | ((i == first + l - HD) & (l >= 3 * HD) & (l < 4 * HD))
    return nn(wk, ek.astype(F32).astype(B16)) + nn(wv, ev.astype(F32).astype(B16))

def half_rows(first, second):
    return jnp.where(lax.broadcasted_iota(jnp.int32, (8, first.shape[1]), 0) < 4, first, second)

def half_select():
    low = lanes((8, 128)) < 64
    r = lax.broadcasted_iota(jnp.int32, (8, 128), 0)
    return ((low & (r == 0)) | ((lanes((8, 128)) >= 64) & (r == 4))).astype(F32).astype(B16)

def front(nf, nz, micros, rows, nblk, chunks, shard,
          x_hbm, ct_hbm, len_ref, g1_ref, g2_ref, wq, wk, wv, so, sg, su, sd,
          A_hbm, O_hbm, kvall_hbm, n1_hbm, q_hbm, ao_hbm, pr_hbm, gains_hbm, cos_hbm, sin_hbm, g_hbm, hid_hbm, part2_hbm, dpart_hbm, gd_hbm, n2T_hbm, dgate_hbm, dup_hbm,
          A, O, kvall_ref, n1_ref, q_ref, ao_ref, pr_ref, gains_ref, cos_ref, sin_ref, g_ref, hid_ref, part2_ref, dpart_ref, gT, n2T, G, U, D, gd, dgate_ref, dup_ref, part_ref, peer_ref, gate_ref, up_ref, act_ref, n2_ref, psum_ref, dsum_ref, begin_ref, skv, x_ref, ct_ref, xsem, wss, wrs, lsem, kss, krs, pss, prs, osem):
    t = lax.axis_index("ctx"); tp = lax.axis_index("tp")
    y = lax.axis_index("fsdp") if nf > 1 else 0
    z, c = t // 2, lax.rem(t, 2)
    qw = q_ref.shape[1]
    first = [pltpu.make_async_copy(a, b, xsem.at[i]) for i, (a, b) in enumerate(((ct_hbm, ct_ref), (x_hbm, x_ref)))]
    for cp in first: cp.start()
    greet(t, z, c, nz, y, nf, False)
    shards, outs = [None, so, sg, su, sd], [A, O, G, U, D]
    def at(k, s):
        m, c0, cn = chunks[k]
        return outs[m].at[pl.ds(pl.multiple_of(s * shard, 16), shard), pl.ds(c0, cn)]
    def own_src(k):
        m, c0, cn = chunks[k]
        return (wq, skv)[k] if m == 0 else shards[m].at[:, pl.ds(c0, cn)]
    W = Gather(nf, nz, at, own_src, wss, wrs)
    W.y_first = (8,)
    V = KeysGather(1, nz, lambda k, s: kvall_ref.at[s], None, kss, krs)
    K = len(chunks)
    def local(k):
        return pltpu.make_async_copy(own_src(k), at(k, W.me), lsem.at[k])
    other = dict(tp=1 - tp)
    def swap_part(m):
        sl = pl.ds(m * rows, rows)
        return pltpu.make_async_remote_copy(src_ref=part_ref.at[sl, :], dst_ref=peer_ref.at[sl, :], send_sem=pss.at[m], recv_sem=prs.at[m], device_id=other, device_id_type=MESHT)
    saved = []
    def save(a, b):
        saved.append(pltpu.make_async_copy(a, b, osem.at[len(saved)]))
        saved[-1].start()
    W.own(0)
    skv[:, :384] = kv_tile(tp, wk[...], wv[...]).astype(B16)
    skv[:, 384:] = tn(half_rows(g1_ref[...].astype(F32), g2_ref[...].astype(F32)).astype(B16), half_select()).astype(B16)
    for b in range(2 * nz):
        @pl.when((b // 2 > z) | (b // 2 < z - V.far))
        def _(): kvall_ref[b] = jnp.zeros(kvall_ref.shape[1:], B16)
    W.own(1); W.own(2)
    for k in W.y_first: W.own_y(k)
    for k in range(K): local(k).start()
    for cp in first: cp.wait()
    place = t * rows + lax.broadcasted_iota(jnp.int32, (rows, 128), 0)
    inverse = jnp.exp((lanes((1, 128)) % (HD // 2)).astype(F32) * (-2.0 * math.log(THETA) / HD))
    for m in range(micros):
        sl = slice(m * rows, (m + 1) * rows)
        begin, end = jnp.zeros((rows, 128), jnp.int32), 0
        for i in range(len_ref.shape[1]):
            end = end + len_ref[m, i]
            begin = begin + jnp.where(place >= end, len_ref[m, i], 0)
        begin_ref[sl, :] = begin
        angle = (place - begin).astype(F32) * inverse
        cos_ref[sl, :] = jnp.cos(angle)
        sin_ref[sl, :] = jnp.sin(angle)
        live = jnp.where(place < end, 1.0, 0.0)
        g_ref[sl, :] = (ct_ref[sl, :].astype(F32) * live[:, :1]).astype(B16)
    x = x_ref[...].astype(F32)
    hid_ref[...] = x * rms(x)
    gT[...] = jnp.transpose(g_ref[...].astype(F32)).astype(B16)
    save(g_ref, g_hbm); save(cos_ref, cos_hbm); save(sin_ref, sin_hbm)
    hop, last = W.hop, W.last
    hop(0, 1); W.own(3); hop(1, 1); hop(0, 2); hop(2, 1); hop(1, 2); hop(0, 3); last(0); hop(2, 2); hop(1, 3); last(1)
    local(0).wait(); local(1).wait()
    W.arrived(0); W.arrived(1)
    save(A, A_hbm)
    sel = (lax.broadcasted_iota(jnp.int32, (8, 128), 1) == jnp.where(lax.broadcasted_iota(jnp.int32, (8, 128), 0) < 4, 0, 64)).astype(B16)
    gains = nt(sel, A[:, qw + 384:qw + 512])
    gains_ref[...] = gains
    save(gains_ref, gains_hbm)
    n1_ref[...] = (hid_ref[...] * gains[0:1, :]).astype(B16)
    cos, sin = cos_ref[...], sin_ref[...]
    lin = nn(n1_ref[...], A[:, qw:qw + 384])
    low = lanes((lin.shape[0], 128)) < 64
    mid = lin[:, 128:256]
    kvall_ref[t, :, 0:128] = rope(lin[:, :128], cos, sin).astype(B16)
    kvall_ref[t, :, 128:256] = jnp.where(low, rope(mid, cos, sin), mid).astype(B16)
    kvall_ref[t, :, 256:384] = lin[:, 256:384].astype(B16)
    hop(3, 1)
    V.own()
    save(n1_ref, n1_hbm)
    hop(2, 3)
    lin = nn(n1_ref[...], A[:, :qw])
    for i in range(qw // 128):
        q_ref[:, 128 * i:128 * (i + 1)] = rope(lin[:, 128 * i:128 * (i + 1)], cos, sin).astype(B16)
    save(q_ref, q_hbm)
    W.own(4); hop(3, 2); hop(4, 1); last(2)
    V.step(1)
    hop(3, 3); W.own(5); hop(4, 2); hop(5, 1); last(3)
    V.step(2)
    V.arrived()
    save(kvall_ref, kvall_hbm)
    local(2).wait()
    W.arrived(2)
    save(O, O_hbm)
    P_ = functools.partial
    pump = [P_(W.own, 6), P_(hop, 4, 3), P_(hop, 5, 2), P_(hop, 6, 1), P_(W.own, 7), P_(hop, 5, 3), P_(hop, 6, 2), P_(hop, 7, 1)]
    w0 = window_start(t, nblk)
    keys = nblk * rows
    pairs = qw // 128
    done = 0
    for m in range(micros):
        sl = slice(m * rows, (m + 1) * rows)
        ks, vs = heads_kv(kvall_ref, w0, nblk, m, rows)
        ok = allowed_of(begin_ref[sl, :1], t * rows, w0 * rows, rows, keys)
        for p in range(pairs):
            kb = stacked(pick(ks, p, tp)); vb = stacked(pick(vs, p, tp))
            s = nt(q_ref[sl, 128 * p:128 * (p + 1)], kb) * SCALE
            halves = []
            for h in range(2):
                sh = jnp.where(ok, s[:, h * keys:(h + 1) * keys], MASKED)
                e = jnp.exp(sh - jnp.max(sh, axis=-1, keepdims=True))
                halves.append((e / jnp.sum(e, axis=-1, keepdims=True)).astype(B16))
            pr = jnp.concatenate(halves, axis=1)
            pr_ref[m * pairs + p] = pr
            ao_ref[sl, 128 * p:128 * (p + 1)] = nn(pr, vb).astype(B16)
            upto = len(pump) * (m * pairs + p + 1) // (micros * pairs)
            emit(pump[done:upto])
            done = upto
        part_ref[sl, :] = nt(ao_ref[sl, :], O[...]).astype(B16)
        swap_part(m).start()
    save(ao_ref, ao_hbm); save(pr_ref, pr_hbm)
    W.own(8); last(4); hop(6, 3); hop(7, 2); hop(8, 1); W.own(9)
    W.arrived(3); W.arrived(4)
    for k in (3, 4): local(k).wait()
    for m in range(micros): swap_part(m).wait_recv()
    hid = x_ref[...].astype(F32) + (part_ref[...].astype(F32) + peer_ref[...].astype(F32))
    hid_ref[...] = hid
    n2 = hid * rms(hid) * gains[4:5, :]
    n2_ref[...] = n2.astype(B16)
    n2T[...] = jnp.transpose(n2).astype(B16)
    save(hid_ref, hid_hbm)
    save(n2T, n2T_hbm)
    def forward(j, _):
        cols = pl.ds(pl.multiple_of(j * 256, 256), 256)
        gate = nn(n2_ref[...], G[:, cols])
        up = nn(n2_ref[...], U[:, cols])
        gate_ref[:, cols] = gate
        up_ref[:, cols] = up
        act = (gate * jax.nn.sigmoid(gate) * up).astype(B16)
        act_ref[:, cols] = act
        gd[:, cols] = nn(gT[...], act).astype(B16)
        return _
    def backward(j, _):
        cols = pl.ds(pl.multiple_of(j * 256, 256), 256)
        da = nn(g_ref[...], D[:, cols])
        gate = gate_ref[:, cols]; up = up_ref[:, cols]
        sg = jax.nn.sigmoid(gate)
        dgate = (da * up * sg * (1.0 + gate * (1.0 - sg))).astype(B16)
        dup = (da * (gate * sg)).astype(B16)
        dgate_ref[:, cols] = dgate
        dup_ref[:, cols] = dup
        dsum_ref[...] += nt(dgate, G[:, cols]) + nt(dup, U[:, cols])
        psum_ref[...] += nt(act_ref[:, cols], D[:, cols])
        return _
    def save_cols(a, b, c0, cn): save(a.at[:, pl.ds(c0, cn)], b.at[:, pl.ds(c0, cn)])
    tiles = [c // 256 for _m, _c0, c in chunks]
    ff = G.shape[1]
    dsum_ref[...] = jnp.zeros_like(dsum_ref)
    psum_ref[...] = jnp.zeros_like(psum_ref)
    lax.fori_loop(0, tiles[3], forward, 0)
    last(5)
    W.arrived(5); local(5).wait()
    hop(7, 3); hop(8, 2); hop(9, 1); W.own(10); last(6)
    W.arrived(6); local(6).wait()
    lax.fori_loop(tiles[3], ff // 256, forward, 0)
    save(gd, gd_hbm)
    hop(8, 3); hop(9, 2); hop(10, 1)
    def back_tiles(k):
        last(k)
        W.arrived(k); local(k).wait()
        _m, c0, cn = chunks[k]
        lax.fori_loop(c0 // 256, (c0 + cn) // 256, backward, 0)
        save_cols(dgate_ref, dgate_hbm, c0, cn); save_cols(dup_ref, dup_hbm, c0, cn)
    order = (8, 7) if 8 in W.y_first else (7, 8)
    back_tiles(order[0])
    hop(9, 3); hop(10, 2)
    back_tiles(order[1])
    hop(10, 3)
    back_tiles(9); back_tiles(10)
    dpart_ref[...] = dsum_ref[...].astype(B16)
    save(dpart_ref, dpart_hbm)
    part2_ref[...] = psum_ref[...].astype(B16)
    save(part2_ref, part2_hbm)
    for m in range(micros): swap_part(m).wait_send()
    for k in range(K): (W.drain_yz if k in W.y_first else W.drain)(k)
    V.drain()
    for cp in saved: cp.wait()

def back(nf, nz, micros, rows, nblk, chunks, shard,
         gd, *refs):
    given, results, refs = refs[:18], refs[18:26], refs[26:]
    back_body(nf, nz, micros, rows, nblk, chunks, shard, gd, given, results, *refs)

def back_body(nf, nz, micros, rows, nblk, chunks, shard, gd, given,
         results,
         own_d, gg, gu, c_d, c_g, c_u, c_o, c_a, y_d, y_g, y_u, y_o, y_a, z_d, z_g, z_u, z_o, z_a,
         zx_ref, go_ref, ga_ref, do_ref, dq_ref, dkv_ref, kc_ref, kz_ref, dl_ref, dpeer_ref, peer2_ref, npeer_ref,
         g_ref, dpart_ref, part2_ref, hid_ref, gains_ref, q_ref, kvall_ref, O, A, ao_ref, pr_ref, n1_ref, cos_ref, sin_ref, x_ref, n2T, dgate_ref, dup_ref, gsem,
         rd, rg, ru, ro, ra, dx_ref, kvx_ref, osem,
         lsem, cs, cr, ys, yr, zs, zr, kcs, kcr, kzs, kzr, ss, sr):
    kz_ref[...] = jnp.zeros_like(kz_ref)
    dh_ref, npart_ref, out_ref = dx_ref, dpart_ref, part2_ref
    t = lax.axis_index("ctx"); tp = lax.axis_index("tp")
    y = lax.axis_index("fsdp") if nf > 1 else 0
    z, c = t // 2, lax.rem(t, 2)
    nb = nf * nz
    greet(t, z, c, nz, y, nf, True)
    ins, outs = [gd, gg, gu, go_ref, ga_ref], [rd, rg, ru, ro, ra]
    crecv, yrecv, zrecv = [c_d, c_g, c_u, c_o, c_a], [y_d, y_g, y_u, y_o, y_a], [z_d, z_g, z_u, z_o, z_a]
    acc = [own_d, c_g, c_u, c_o, c_a]
    sib, other = dict(ctx=t + 1 - 2 * c), dict(tp=1 - tp)
    inner = (z == 1) | (z == 2)
    zin, zed = jnp.where(z < 2, 1, 2), jnp.where(z < 2, 0, 3)
    zoi, zoe = 3 - zin, 3 - zed
    def remote(src, dst, s, r, dev):
        return pltpu.make_async_remote_copy(src_ref=src, dst_ref=dst, send_sem=s, recv_sem=r, device_id=dev, device_id_type=MESHT)
    def ccopy(k):
        m, c0, cn = chunks[k]
        return remote(ins[m].at[:, 1 - c, :, pl.ds(c0, cn)], crecv[m].at[:, :, pl.ds(c0, cn)], cs.at[k], cr.at[k], sib)
    def lcopy(k):
        m, c0, cn = chunks[k]
        return pltpu.make_async_copy(ins[m].at[:, c, :, pl.ds(c0, cn)], acc[m].at[:, :, pl.ds(c0, cn)], lsem.at[k])
    def ycopy(k, p):
        m, c0, cn = chunks[k]
        yy = lax.rem(y + p, nf)
        return remote(acc[m].at[pl.ds(yy * nz, nz), :, pl.ds(c0, cn)], yrecv[m].at[p - 1, :, :, pl.ds(c0, cn)], ys.at[k, p - 1], yr.at[k, p - 1], dict(fsdp=yy))
    def zcopy(k, block, i, slot):
        m, c0, cn = chunks[k]
        return lambda dest: remote(acc[m].at[y * nz + block, :, pl.ds(c0, cn)], zrecv[m].at[slot, :, pl.ds(c0, cn)], zs.at[k, i], zr.at[k, slot], dict(ctx=dest * 2 + c))
    def zgot(k, slot): zcopy(k, z, 0, slot)(zoi).wait_recv()
    def stage_core(k):
        m, c0, cn = chunks[k]
        cols = pl.ds(c0, cn)
        if m < 1: lcopy(k).wait()
        ccopy(k).wait_recv()
        def add(b, _):
            first = acc[m][b, :, cols] if m < 1 else ins[m][b, c, :, cols]
            acc[m][b, :, cols] = first + crecv[m][b, :, cols]
            return _
        lax.fori_loop(0, nb, add, 0)
        for p in range(1, nf): ycopy(k, p).start()
    def stage_y(k):
        m, c0, cn = chunks[k]
        cols = pl.ds(c0, cn)
        for p in range(1, nf): ycopy(k, p).wait_recv()
        def add(b, _):
            total = acc[m][y * nz + b, :, cols].astype(F32)
            for p in range(1, nf): total = total + yrecv[m][p - 1, b, :, cols].astype(F32)
            acc[m][y * nz + b, :, cols] = total.astype(B16)
            return _
        lax.fori_loop(0, nz, add, 0)
        @pl.when(inner)
        def _(): zcopy(k, zed, 0, 0)(zed).start()
        @pl.when(jnp.logical_not(inner))
        def _():
            zcopy(k, zoi, 0, 2)(zin).start()
            zcopy(k, zoe, 1, 3)(zin).start()
            zcopy(k, zin, 2, 0)(zin).start()
    def stage_m(k):
        m, c0, cn = chunks[k]
        cols = pl.ds(c0, cn)
        @pl.when(inner)
        def _():
            for block, slot in ((zoi, 2), (zoe, 3)):
                zgot(k, slot)
                acc[m][y * nz + block, :, cols] = (acc[m][y * nz + block, :, cols].astype(F32) + zrecv[m][slot, :, cols].astype(F32)).astype(B16)
                zcopy(k, block, slot - 1, 1)(block).start()
    def stage_z(k):
        m, c0, cn = chunks[k]
        cols = pl.ds(c0, cn)
        zgot(k, 0); zgot(k, 1)
        outs[m][:, cols] = acc[m][y * nz + z, :, cols].astype(F32) + zrecv[m][0, :, cols].astype(F32) + zrecv[m][1, :, cols].astype(F32)
    def xcopy(q, block, i, slot):
        m, c0, cn = chunks[0]
        dst = zx_ref.at[slot] if q else zrecv[m].at[slot, :, pl.ds(c0, cn)]
        return lambda dest: remote(acc[m].at[lax.rem(y + q, nf) * nz + block, :, pl.ds(c0, cn)], dst, zs.at[0, 3 * q + i], zr.at[0, 4 * q + slot], dict(ctx=dest * 2 + c))
    def xgot(q, slot): xcopy(q, z, 0, slot)(zoi).wait_recv()
    def xycopy():
        m, c0, cn = chunks[0]
        yy = lax.rem(y + 1, nf)
        return remote(acc[m].at[yy * nz + z, :, pl.ds(c0, cn)], yrecv[m].at[0, 0, :, pl.ds(c0, cn)], ys.at[0, 0], yr.at[0, 0], dict(fsdp=yy))
    def stage_xcore():
        m, c0, cn = chunks[0]
        cols = pl.ds(c0, cn)
        lcopy(0).wait()
        ccopy(0).wait_recv()
        def add(b, _):
            acc[m][b, :, cols] = acc[m][b, :, cols] + crecv[m][b, :, cols]
            return _
        lax.fori_loop(0, nb, add, 0)
        @pl.when(inner)
        def _():
            for q in (1, 0): xcopy(q, zed, 0, 0)(zed).start()
        @pl.when(jnp.logical_not(inner))
        def _():
            for q in (1, 0):
                xcopy(q, zoi, 0, 2)(zin).start()
                xcopy(q, zoe, 1, 3)(zin).start()
                xcopy(q, zin, 2, 0)(zin).start()
    def stage_xm():
        m, c0, cn = chunks[0]
        cols = pl.ds(c0, cn)
        @pl.when(inner)
        def _():
            for q in (1, 0):
                at = lax.rem(y + q, nf) * nz
                for block, slot in ((zoi, 2), (zoe, 3)):
                    xgot(q, slot)
                    got = zx_ref[slot] if q else zrecv[m][slot, :, cols]
                    acc[m][at + block, :, cols] = (acc[m][at + block, :, cols].astype(F32) + got.astype(F32)).astype(B16)
                    xcopy(q, block, slot - 1, 1)(block).start()
    def stage_xz():
        m, c0, cn = chunks[0]
        cols = pl.ds(c0, cn)
        xgot(1, 0); xgot(1, 1)
        at = lax.rem(y + 1, nf) * nz + z
        acc[m][at, :, cols] = (acc[m][at, :, cols].astype(F32) + zx_ref[0].astype(F32) + zx_ref[1].astype(F32)).astype(B16)
        xycopy().start()
    def stage_xy():
        m, c0, cn = chunks[0]
        cols = pl.ds(c0, cn)
        xgot(0, 0); xgot(0, 1)
        total = acc[m][y * nz + z, :, cols].astype(F32) + zrecv[m][0, :, cols].astype(F32) + zrecv[m][1, :, cols].astype(F32)
        xycopy().wait_recv()
        outs[m][:, cols] = total + yrecv[m][0, 0, :, cols].astype(F32)
    dswap = remote(given[1], dpeer_ref, ss.at[0], sr.at[0], other)
    oswap = remote(given[2], peer2_ref, ss.at[1], sr.at[1], other)
    nswap = remote(npart_ref, npeer_ref, ss.at[2], sr.at[2], other)
    K = len(chunks)
    held = (g_ref, dpart_ref, part2_ref, hid_ref, gains_ref, q_ref, kvall_ref, O, A, ao_ref, pr_ref, n1_ref, cos_ref, sin_ref, x_ref, n2T, dgate_ref, dup_ref)
    loads = [pltpu.make_async_copy(a, b, gsem.at[i]) for i, (a, b) in enumerate(zip(given, held))]
    def need(*which):
        for i in which: loads[i].wait()
    saves = [pltpu.make_async_copy(a, b, osem.at[i]) for i, (a, b) in enumerate(zip((rd, rg, ru, ro, ra, dx_ref, out_ref, kvx_ref), results))]
    dswap.start()
    for k in (1, 0, 2):
        ccopy(k).start(); lcopy(k).start()
    def weights(ref, d_ref):
        def tile(j, _):
            cols = pl.ds(pl.multiple_of(j * 256, 256), 256)
            v = nn(n2T[...], d_ref[:, cols]).astype(B16)
            for s in range(2 * nb): ref[s // 2, s % 2, :, cols] = v[s * shard:(s + 1) * shard]
            return _
        lax.fori_loop(0, d_ref.shape[1] // 256, tile, 0)
    stage_core(1)
    for i in (15, 16, 17): loads[i].start()
    stage_xcore()
    for i in (1, 3, 0, 4, 7, 9, 5, 6, 10, 2, 12, 13, 8, 11, 14): loads[i].start()
    need(15, 16)
    weights(gg, dgate_ref)
    stage_core(2)
    ccopy(3).start(); ccopy(4).start()
    dkv_ref[...] = jnp.zeros_like(dkv_ref)
    need(17)
    weights(gu, dup_ref)
    stage_core(3)
    for k in (5, 6, 7): ccopy(k).start()
    stage_y(1)
    dswap.wait_recv()
    need(0, 1, 3, 4, 7)
    oswap.start()
    dn2 = dpart_ref[...].astype(F32) + dpeer_ref[...].astype(F32)
    hid = hid_ref[...]
    r2 = rms(hid)
    gain2 = jnp.sum(dn2 * hid * r2, axis=0, keepdims=True)
    dh = g_ref[...].astype(F32) + norm_back(hid, r2, gains_ref[4:5, :], dn2)
    dh_ref[...] = dh
    db = dh.astype(B16)
    do_ref[...] = nn(db, O[...]).astype(B16)
    stage_y(2)
    need(9)
    go = tn(db, ao_ref[...]).astype(B16)
    for s in range(2 * nb): go_ref[s // 2, s % 2] = go[s * shard:(s + 1) * shard]
    ccopy(8).start()
    stage_core(4)
    stage_xm()
    need(5, 6, 10)
    w0 = window_start(t, nblk)
    keys = nblk * rows
    pairs = q_ref.shape[1] // 128
    low = lanes((keys, 128)) < 64
    for m in range(micros):
        sl = slice(m * rows, (m + 1) * rows)
        ks, vs = heads_kv(kvall_ref, w0, nblk, m, rows)
        dks = [jnp.zeros((keys, 128), F32) for _ in range(3)]
        dvs = [jnp.zeros((keys, 128), F32) for _ in range(3)]
        for p in range(pairs):
            kb = stacked(pick(ks, p, tp)); vb = stacked(pick(vs, p, tp))
            qt = q_ref[sl, 128 * p:128 * (p + 1)]
            dot_ = do_ref[sl, 128 * p:128 * (p + 1)]
            pr = pr_ref[m * pairs + p]
            dp = nt(dot_, vb)
            halves = []
            for h in range(2):
                ph = pr[:, h * keys:(h + 1) * keys].astype(F32)
                dph = dp[:, h * keys:(h + 1) * keys]
                delta = jnp.sum(ph * dph, axis=-1, keepdims=True)
                halves.append((ph * (dph - delta)).astype(B16))
            ds = jnp.concatenate(halves, axis=1)
            dq_ref[sl, 128 * p:128 * (p + 1)] = nn(ds, kb) * SCALE
            dkb = tn(ds, qt) * SCALE
            dvb = tn(pr, dot_)
            dk = jnp.where(low, dkb[:keys], dkb[keys:])
            dv = jnp.where(low, dvb[:keys], dvb[keys:])
            a, b = p // 2, (p + 1) // 2
            if a == b:
                dks[a] = dks[a] + dk; dvs[a] = dvs[a] + dv
            else:
                first = (tp == 0).astype(F32); second = 1.0 - first
                dks[a] = dks[a] + dk * first; dvs[a] = dvs[a] + dv * first
                dks[b] = dks[b] + dk * second; dvs[b] = dvs[b] + dv * second
        def full(v): return v + pltpu.roll(v, 64, 1)
        dk0, dk1, dk2 = [full(v) for v in dks]
        dv0, dv1, dv2 = [full(v) for v in dvs]
        tiles = [jnp.where(low, dk0, dk1), jnp.where(low, dk2, dv2), jnp.where(low, dv0, dv1)]
        for b in range(nblk):
            at = w0 + b
            for i in range(3):
                dkv_ref[at // 2, lax.rem(at, 2), m * rows:(m + 1) * rows, 128 * i:128 * (i + 1)] = tiles[i][b * rows:(b + 1) * rows].astype(B16)
        if m == 0: stage_m(1); stage_m(2); stage_z(1)
    kvc = remote(dkv_ref.at[:, 1 - c], kc_ref, kcs.at[0], kcr.at[0], sib)
    def kvz(p): return remote(kc_ref.at[z - p], kz_ref.at[p - 1], kzs.at[p - 1], kzr.at[p - 1], dict(ctx=t - 2 * p))
    def kv_each(act):
        for p in range(1, 3):
            @pl.when(z >= p)
            def _(): act(kvz(p))
    def kv_got():
        for p in range(1, 3):
            @pl.when(z + p < nz)
            def _(): remote(kc_ref.at[z], kz_ref.at[p - 1], kzs.at[p - 1], kzr.at[p - 1], sib).wait_recv()
    kvc.start()
    stage_y(3); stage_xz(); stage_core(5)
    kvc.wait_recv()
    def add_kv(b, _):
        kc_ref[b] = kc_ref[b] + dkv_ref[b, c]
        return _
    lax.fori_loop(0, nz, add_kv, 0)
    kv_each(lambda cp: cp.start())
    stage_z(2); stage_m(3); stage_y(4); stage_xy(); saves[0].start()
    stage_z(3); stage_core(6)
    kv_got()
    dkv = kc_ref[z].astype(F32) + kz_ref[0].astype(F32) + kz_ref[1].astype(F32)
    need(8, 11, 12, 13)
    cos, sin = cos_ref[...], sin_ref[...]
    qw = q_ref.shape[1]
    for i in range(qw // 128):
        dl_ref[:, 128 * i:128 * (i + 1)] = rope_back(dq_ref[:, 128 * i:128 * (i + 1)], cos, sin).astype(B16)
    mid = dkv[:, 128:256]
    dl_ref[:, qw:qw + 128] = rope_back(dkv[:, :128], cos, sin).astype(B16)
    dl_ref[:, qw + 128:qw + 256] = jnp.where(lanes(mid.shape) < 64, rope_back(mid, cos, sin), mid).astype(B16)
    dl_ref[:, qw + 256:qw + 384] = dkv[:, 256:384].astype(B16)
    npart_ref[...] = nt(dl_ref[...], A[:, :qw + 384]).astype(B16)
    nswap.start()
    stage_core(8)
    ga = tn(n1_ref[...], dl_ref[...]).astype(B16)
    for s in range(2 * nb): ga_ref[s // 2, s % 2, :, :qw + 384] = ga[s * shard:(s + 1) * shard]
    ccopy(9).start()
    stage_m(4); stage_y(5); stage_z(4); saves[1].start()
    oswap.wait_recv()
    need(2)
    out_ref[...] = (hid_ref[...] + (part2_ref[...].astype(F32) + peer2_ref[...].astype(F32))).astype(B16)
    saves[6].start()
    stage_core(9)
    stage_m(5); stage_y(6)
    nswap.wait_recv()
    need(14)
    x = x_ref[...].astype(F32)
    r1 = rms(x)
    dn1 = npart_ref[...].astype(F32) + npeer_ref[...].astype(F32)
    gain1 = jnp.sum(dn1 * x * r1, axis=0, keepdims=True)
    gcol = tn(half_rows(gain1, gain2).astype(B16), half_select()).astype(B16)
    for s in range(2 * nb): ga_ref[s // 2, s % 2, :, qw + 384:qw + 512] = gcol[s * shard:(s + 1) * shard]
    ccopy(10).start()
    dx_ref[...] = dh_ref[...] + norm_back(x, r1, gains_ref[0:1, :], dn1)
    saves[5].start()
    stage_core(10); stage_core(7)
    stage_z(5); stage_m(6); stage_y(8); stage_z(6)
    stage_m(8); stage_y(9); stage_z(8); saves[3].start()
    stage_m(9); stage_y(10); stage_z(9)
    stage_m(10); stage_y(7); stage_m(7); stage_z(10)
    hs = shard // 2
    kswap = remote(ra.at[pl.ds(pl.multiple_of((1 - tp) * hs, 8), hs), pl.ds(qw, 384)], kvx_ref, ss.at[3], sr.at[3], other)
    kswap.start()
    saves[4].start()
    stage_z(7)
    saves[2].start()
    kswap.wait()
    saves[7].start()
    for cp in saves: cp.wait()
    for cp in (dswap, oswap, nswap, kvc): cp.wait_send()
    kv_each(lambda cp: cp.wait_send())
    for k in range(K):
        ccopy(k).wait_send()
        if k == 0:
            xycopy().wait_send()
            for q in range(2):
                for i in range(3): xcopy(q, z, i, 0)(zoi).wait_send()
            continue
        for p in range(1, nf): ycopy(k, p).wait_send()
        for i in range(3): zcopy(k, z, i, 0)(zoi).wait_send()

def finish(qw, *refs):
    given, refs = refs[:8], refs[8:]
    o_out, dx_out, gg1, gq, gk, gv, go, gg2, gg, gu, gd, rd, rg, ru, ro, ra, dx_ref, out_ref, kvx_ref, k_ref, v_ref, gr1, gr2, isem, sem = refs
    tp = lax.axis_index("tp")
    hs = kvx_ref.shape[0]
    loads = [pltpu.make_async_copy(a, b, isem.at[i]) for i, (a, b) in enumerate(zip(given, (rd, rg, ru, ro, ra, dx_ref, out_ref, kvx_ref)))]
    order = (4, 7, 5, 0, 1, 2, 6, 3)
    for i in order: loads[i].start()
    copies = []
    def store(a, b):
        copies.append(pltpu.make_async_copy(a, b, sem.at[len(copies)]))
        copies[-1].start()
    loads[4].wait()
    store(ra.at[:, pl.ds(0, qw)], gq)
    loads[7].wait()
    mine = ra[pl.ds(pl.multiple_of(tp * hs, 8), hs), qw:qw + 384]
    theirs = kvx_ref[...]
    lo, hi = jnp.where(tp == 0, mine, theirs), jnp.where(tp == 0, theirs, mine)
    low = lanes((hs, 128)) < 64
    def tile(v, i): return v[:, 128 * i:128 * (i + 1)]
    k_ref[:, :128] = tile(lo, 0)
    k_ref[:, 128:256] = jnp.where(low, tile(lo, 1) + tile(hi, 0), tile(hi, 0))
    k_ref[:, 256:320] = tile(hi, 1)[:, :64]
    v_ref[:, :128] = tile(lo, 2)
    v_ref[:, 128:256] = jnp.where(low, pltpu.roll(tile(lo, 1), 64, 1) + tile(hi, 2), tile(hi, 2))
    v_ref[:, 256:320] = pltpu.roll(tile(hi, 1), 64, 1)[:, :64]
    rowsT = jnp.transpose(ra[:, qw + 384:qw + 512])
    gr1[...] = rowsT[0:1, :]
    gr2[...] = rowsT[64:65, :]
    for i, a, b in ((5, dx_ref, dx_out), (0, rd, gd), (1, rg, gg), (2, ru, gu), (6, out_ref, o_out), (3, ro, go)):
        loads[i].wait()
        store(a, b)
    for a, b in ((k_ref, gk), (v_ref, gv), (gr1, gg1), (gr2, gg2)): store(a, b)
    for cp in copies: cp.wait()

def fast(tokens, lengths, attn_gain, w_query, w_key, w_value, w_out, ffn_gain, w_gate, w_up, w_down, cotangent):
    micros, rows, width = tokens.shape
    nf, nctx = lax.axis_size("fsdp"), lax.axis_size("ctx")
    nz = nctx // 2
    nb = nf * nz
    tp, t = lax.axis_index("tp"), lax.axis_index("ctx")
    total = rows * nctx
    nblk = total // 2 // rows + 1
    shard = w_query.shape[0]
    qw, ff = w_query.shape[1], w_gate.shape[1]
    M = micros * rows
    aw = qw + 512
    x = tokens.reshape(M, width)
    pairs = qw // 128
    keys = nblk * rows
    S = pltpu.SemaphoreType.DMA
    inv, ina = pl.BlockSpec(memory_space=VMEM), pl.BlockSpec(memory_space=pl.ANY)
    ns = nb * 2
    big = ff // 512 * 256 + 256 * (ff // 256 % 2)
    small = ff - big
    chunks = [(0, 0, qw), (0, qw, 512), (1, 0, qw), (2, 0, big), (3, 0, big), (2, big, small), (3, big, small), (4, 0, ff - 1280), (4, ff - 1280, 512), (4, ff - 768, 512), (4, ff - 256, 256)]
    outs = [((width, aw), B16), ((width, qw), B16), ((nctx, M, 384), B16), ((M, width), B16), ((M, qw), B16), ((M, qw), B16), ((micros * pairs, rows, 2 * keys), B16),
        ((8, width), F32), ((M, 128), F32), ((M, 128), F32), ((M, width), B16), ((M, width), F32), ((M, width), B16), ((M, width), B16)] + [((width, ff), B16), ((width, M), B16), ((M, ff), B16), ((M, ff), B16)]
    smem = pl.BlockSpec(memory_space=pltpu.SMEM)
    slots = 32
    A, O, kvall, n1, q, ao, pr, gains, cos, sin, g, hid, part2, dpart, gd, n2T, dgate, dup = pl.pallas_call(
        functools.partial(front, nf, nz, micros, rows, nblk, chunks, shard),
        out_shape=[jax.ShapeDtypeStruct(s, d) for s, d in outs],
        in_specs=[ina, ina, smem, inv, inv, ina, inv, inv] + [ina] * 4, out_specs=[ina] * 18,
        scratch_shapes=[VMEM(s, d) for s, d in outs[:14]] + [VMEM((width, M), B16)] * 2 + [VMEM((width, ff), B16)] * 4 + [VMEM((M, ff), B16)] * 2 + [VMEM((M, width), B16)] * 2 + [VMEM((M, ff), F32)] * 2 + [VMEM((M, ff), B16), VMEM((M, width), B16)] + [VMEM((M, width), F32)] * 2
            + [VMEM((M, 128), jnp.int32), VMEM((shard, 512), B16)] + [VMEM((M, width), B16)] * 2 + [S((2,)), S((11, slots)), S((11, ns)), S((11,)), S((1, n_slots(1, nz))), S((1, nctx)), S((micros,)), S((micros,)), S((24,))],
        compiler_params=pltpu.CompilerParams(collective_id=0, has_side_effects=True, vmem_limit_bytes=63 << 20), name="front",
    )(x, cotangent.reshape(M, width), lengths[0], attn_gain.reshape(1, shard), ffn_gain.reshape(1, shard), w_query, w_key, w_value, w_out.T, w_gate, w_up, w_down.T)
    chunks = [(0, 0, 512), (0, 512, 256), (0, 768, ff - 768), (1, 0, big), (1, big, small), (2, 0, big), (2, big, small - 256), (2, ff - 256, 256), (3, 0, qw), (4, 0, qw), (4, qw, 512)]
    wd = [ff, ff, ff, qw, aw]
    K = len(chunks)
    hs = shard // 2
    outs = [((shard, w), F32) for w in wd] + [((M, width), F32), ((M, width), B16), ((hs, 384), F32)]
    scratch = [VMEM((nb, shard, ff), B16)] + [VMEM((nb, 2, shard, ff), B16)] * 2 + [VMEM((nb, shard, w), B16) for w in wd] + [VMEM((nf - 1, nz, shard, w), B16) for w in wd] + [VMEM((4, shard, w), B16) for w in wd]
    scratch += [VMEM((4, shard, 512), B16), VMEM((nb, 2, shard, qw), B16), VMEM((nb, 2, shard, aw), B16), VMEM((M, qw), B16), VMEM((M, qw), F32), VMEM((nz, 2, M, 384), B16),
        VMEM((nz, M, 384), B16), VMEM((2, M, 384), B16), VMEM((M, qw + 384), B16)] + [VMEM((M, width), B16)] * 3
    given = [g, dpart, part2, hid, gains, q, kvall, O, A, ao, pr, n1, cos, sin, x, n2T, dgate, dup]
    scratch += [VMEM(v.shape, v.dtype) for v in given] + [S((18,))] + [VMEM(s, d) for s, d in outs[:6] + outs[7:]] + [S((8,))]
    scratch += [S((K,)), S((K,)), S((K,)), S((K, nf - 1)), S((K, nf - 1)), S((K, 6)), S((K, 8)), S((1,)), S((1,)), S((2,)), S((2,)), S((4,)), S((4,))]
    ends = pl.pallas_call(
        functools.partial(back, nf, nz, micros, rows, nblk, chunks, shard),
        out_shape=[jax.ShapeDtypeStruct(s, d) for s, d in outs],
        in_specs=[ina] * 19, out_specs=[ina] * 8, scratch_shapes=scratch,
        compiler_params=pltpu.CompilerParams(collective_id=4, has_side_effects=True, vmem_limit_bytes=67043328), name="back",
    )(gd.reshape(nb, 2, shard, ff), *given)
    outs = [((M, width), B16), ((M, width), F32), ((1, shard), F32), ((shard, qw), F32), ((hs, 5 * HD), F32), ((hs, 5 * HD), F32), ((shard, qw), F32), ((1, shard), F32)] + [((shard, ff), F32)] * 3
    output, dx, gain1, gq, gk, gv, go, gain2, gg, gu, gd = pl.pallas_call(
        functools.partial(finish, qw), out_shape=[jax.ShapeDtypeStruct(s, d) for s, d in outs],
        in_specs=[ina] * 8, out_specs=[ina] * 11,
        scratch_shapes=[VMEM(v.shape, v.dtype) for v in ends] + [VMEM((hs, 5 * HD), F32)] * 2 + [VMEM((1, shard), F32)] * 2 + [S((8,)), S((11,))], name="finish",
    )(*ends)
    return (output.reshape(micros, rows, width), dx.reshape(micros, rows, width), gain1.reshape(shard), gq, gk, gv, go.T, gain2.reshape(shard), gg, gu, gd.T)


def solution(mesh):
    placed = (
        P(None, ("fsdp", "ctx"), None),
        P("fsdp", None, None),
        P(("fsdp", "ctx")),
        P(("fsdp", "ctx"), "tp"),
        P(("fsdp", "ctx"), None),
        P(("fsdp", "ctx"), None),
        P("tp", ("fsdp", "ctx")),
        P(("fsdp", "ctx")),
        P(("fsdp", "ctx"), "tp"),
        P(("fsdp", "ctx"), "tp"),
        P("tp", ("fsdp", "ctx")),
        P(None, ("fsdp", "ctx"), None),
    )
    def chosen(*args):
        fits = args[3].shape[0] % 16 == 0 and mesh.shape["tp"] == 2 and mesh.shape["fsdp"] == 2 and mesh.shape["ctx"] == 8
        return (fast if fits else shards)(*args)

    return jax.shard_map(
        chosen,
        mesh=mesh,
        in_specs=placed,
        out_specs=(
            P(None, ("fsdp", "ctx"), None),
            P(None, ("fsdp", "ctx"), None),
            P(("fsdp", "ctx")),
            P(("fsdp", "ctx"), "tp"),
            P(("fsdp", "ctx", "tp"), None),
            P(("fsdp", "ctx", "tp"), None),
            P("tp", ("fsdp", "ctx")),
            P(("fsdp", "ctx")),
            P(("fsdp", "ctx"), "tp"),
            P(("fsdp", "ctx"), "tp"),
            P("tp", ("fsdp", "ctx")),
        ),
        check_vma=False,
    )
```
